32 devices in a mesh: seq: 4 (over z), ctx: 8 (over y, x, core).
Axes of the slice: x: 2, y: 2, z: 4, core: 2. Of those that a mesh axis runs over, the one named last changes fastest.
Arguments:
- tokens: bfloat16 [4, 1024, 768], P('seq', 'ctx'), may hold values from -6 to 6
- block_ids: int32 [4, 1024], P('seq', 'ctx'), may hold values from 0 to 3, as said below
- ln1_gain: bfloat16 [768], P('seq'), may hold values from 0.25 to 1.75
- ln1_bias: bfloat16 [768], P('seq'), may hold values from -3 to 3
- w_qkv: bfloat16 [768, 2304], P('seq'), may hold values from -0.3125 to 0.3125
- q_bias: bfloat16 [768], P('seq'), may hold values from -3 to 3
- v_bias: bfloat16 [768], P('seq'), may hold values from -3 to 3
- w_out: bfloat16 [768, 768], P('seq'), may hold values from -1 to 1
- out_bias: bfloat16 [768], P('seq'), may hold values from -3 to 3
- ln2_gain: bfloat16 [768], P('seq'), may hold values from 0.25 to 1.75
- ln2_bias: bfloat16 [768], P('seq'), may hold values from -3 to 3
- w_up: bfloat16 [768, 3072], P('seq'), may hold values from -0.21875 to 0.21875
- up_bias: bfloat16 [3072], P('seq'), may hold values from -3 to 3
- w_down: bfloat16 [3072, 768], P('seq'), may hold values from -0.109375 to 0.109375
- down_bias: bfloat16 [768], P('seq'), may hold values from -3 to 3
- cotangent: bfloat16 [4, 1024, 768], P('seq', 'ctx'), may hold values from -6 to 6
Outputs:
- output: bfloat16 [4, 1024, 768], P('seq', 'ctx')
- input_grad: float32 [4, 1024, 768], P('seq', 'ctx')
- grad_ln1_gain: float32 [768], P('seq')
- grad_ln1_bias: float32 [768], P('seq')
- grad_w_qkv: float32 [768, 2304], P('seq')
- grad_q_bias: float32 [768], P('seq')
- grad_v_bias: float32 [768], P('seq')
- grad_w_out: float32 [768, 768], P('seq')
- grad_out_bias: float32 [768], P('seq')
- grad_ln2_gain: float32 [768], P('seq')
- grad_ln2_bias: float32 [768], P('seq')
- grad_w_up: float32 [768, 3072], P('seq')
- grad_up_bias: float32 [3072], P('seq')
- grad_w_down: float32 [3072, 768], P('seq')
- grad_down_bias: float32 [768], P('seq')
The draws below stay inside these ranges and needn't reach their ends.
Inputs may be any that keep to these rules, and one draw needn't show every extreme that they name: `block_ids`: along each sequence's true order of patches the block id starts at 0 and rises by 0 or 1 from one patch to the next; each sequence has exactly 4 blocks. Index c of ctx holds, in order, the 64 patches of true block of rows c and then those of true block of rows 15 - c, where true blocks of rows have 128 / 2 patches each.
All inputs are finite; a program needn't handle non-finite values.
Results may differ from the reference program's by a relative error of at most 0.017.
The reference program's roundings to bfloat16 on the way count: a program that leaves them out, or rounds other values in their place, can miss the bound.
Values may be sent and summed in bfloat16 or wider, within the bound.
No kernel may reach another device: no remote copies, remote signals or barrier semaphores. Data moves between devices by JAX's collectives and lax.ppermute only.
A program may use at most 256 MiB of HBM per device.

```python
import math
import jax
import jax.numpy as jnp
from jax import lax

D = 768
HEADS = 12
FF = 3072
TOK_DEV = 128
BLOCK = 256
LEN = 1024
SEQS = 4
N_CTX = 8


def draw_block_ids(key, part):
    length = TOK_DEV * N_CTX
    half = TOK_DEV // 2
    count = length // BLOCK

    def one_sequence(seq_key):
        places = jax.random.permutation(seq_key, jnp.arange(1, length, dtype=jnp.int32))
        chosen = places[:count - 1]
        starts = jnp.zeros((length,), jnp.int32).at[chosen].set(1)
        true_ids = jnp.cumsum(starts).astype(jnp.int32)
        positions = jnp.arange(length, dtype=jnp.int32)
        device = positions // TOK_DEV
        inner = positions % TOK_DEV
        piece = jnp.where(inner < half, device, 2 * N_CTX - 1 - device)
        true_place = piece * half + inner % half
        return true_ids[true_place]
    seq_keys = jax.random.split(jax.random.fold_in(key, 17), SEQS)
    return jax.vmap(one_sequence)(seq_keys)


def level_of(own_key, extent, cuts, smallest, high):
    def one(axis_at, shards_of):
        draws = jax.random.uniform(jax.random.fold_in(jax.random.fold_in(own_key, 6), axis_at), (shards_of,), jnp.float32, smallest / len(cuts), high / len(cuts))
        return jnp.repeat(jnp.exp(draws), extent[axis_at] // shards_of).reshape((-1,) + (1,) * (len(extent) - axis_at - 1))

    factor_of = one(*cuts[0])
    for cut in cuts[1:]:
        factor_of = factor_of * one(*cut)
    return factor_of


def gaussian(key, shape, deviation, reach, cuts=(), kind=jnp.bfloat16):
    drawn = jax.random.normal(key, shape, jnp.float32) * deviation
    if len(cuts) > 0:
        drawn = level_of(key, shape, cuts, -0.22, 0.18) * drawn
    return jnp.clip(drawn, min=-reach, max=reach).astype(kind)


def setup_inputs(seed: int = 0) -> dict:
    streams_of = jax.random.split(jax.random.key(seed), 17)
    tokens = gaussian(streams_of[0], (SEQS, LEN, D), 1.0, 6.0, ((0, 4), (1, 8)))
    block_ids = draw_block_ids(jax.random.fold_in(streams_of[16], 71), 0)
    ln1_gain = jnp.clip(1.0 + 0.15 * jax.random.normal(streams_of[2], (D,), jnp.float32), 0.25, 1.75).astype(jnp.bfloat16)
    ln1_bias = gaussian(streams_of[3], (D,), 0.3, 3.0, ((0, 4),))
    w_qkv = gaussian(streams_of[4], (D, 3 * D), (D // 2) ** -0.5, 0.3125, ((0, 4),))
    q_bias = gaussian(streams_of[5], (D,), 0.5, 3.0, ((0, 4),))
    v_bias = gaussian(streams_of[6], (D,), 0.5, 3.0, ((0, 4),))
    w_out = gaussian(streams_of[7], (D, D), (max(D // 24, 1)) ** -0.5, 1.0, ((0, 4),))
    out_bias = gaussian(streams_of[8], (D,), 0.3, 3.0, ((0, 4),))
    ln2_gain = jnp.clip(1.0 + 0.15 * jax.random.normal(streams_of[9], (D,), jnp.float32), 0.25, 1.75).astype(jnp.bfloat16)
    ln2_bias = gaussian(streams_of[10], (D,), 0.3, 3.0, ((0, 4),))
    w_up = gaussian(streams_of[11], (D, FF), D ** -0.5, 0.21875, ((0, 4),))
    up_bias = gaussian(streams_of[12], (FF,), 0.5, 3.0, ((0, 4),))
    w_down = gaussian(streams_of[13], (FF, D), FF ** -0.5, 0.109375, ((0, 4),))
    down_bias = gaussian(streams_of[14], (D,), 0.3, 3.0, ((0, 4),))
    cotangent = gaussian(streams_of[15], (SEQS, LEN, D), 1.0, 6.0, ((0, 4), (1, 8)))
    return {"tokens": tokens, "block_ids": block_ids, "ln1_gain": ln1_gain, "ln1_bias": ln1_bias, "w_qkv": w_qkv, "q_bias": q_bias, "v_bias": v_bias, "w_out": w_out, "out_bias": out_bias, "ln2_gain": ln2_gain, "ln2_bias": ln2_bias, "w_up": w_up, "up_bias": up_bias, "w_down": w_down, "down_bias": down_bias, "cotangent": cotangent}


EPSILON = 1e-06
NEGATIVE = -1e+30
HIGHEST = lax.Precision.HIGHEST

@jax.custom_vjp
def low(v):
    return lax.optimization_barrier(v.astype(jnp.bfloat16)).astype(jnp.float32)

@jax.custom_vjp
def low_back(v):
    return v

def low_keep(v):
    return (low(v), None)

def low_pass(kept, grad):
    return (grad,)

def back_keep(v):
    return (v, None)

def back_low(kept, grad):
    return (low(grad),)
low.defvjp(low_keep, low_pass)
low_back.defvjp(back_keep, back_low)

def rounded_both(value):
    return low(low_back(value))

def layer_norm(values, gain, shift):
    center = values - lax.optimization_barrier(jnp.mean(values, -1, keepdims=True))
    spread = lax.optimization_barrier(jnp.mean(center * center, -1, keepdims=True))
    return center * lax.rsqrt(spread + EPSILON) * gain + shift

def matmul(left, right):
    return jnp.dot(left, right, precision=HIGHEST, preferred_element_type=jnp.float32)

def attend(query, key, value, ids):
    count = query.shape[0]
    head_dim = D // HEADS
    scale = 1.0 / math.sqrt(head_dim)
    step = math.gcd(count, 512)
    key_heads = key.reshape(count, HEADS, head_dim)
    value_heads = value.reshape(count, HEADS, head_dim)

    def one_block(inputs):
        query_block, id_block = inputs
        scores = jnp.einsum('qhd,khd->hqk', query_block, key_heads, precision=HIGHEST) * scale
        scores = low_back(scores)
        allowed = ids[None, None, :] <= id_block[None, :, None]
        masked = jnp.where(allowed, scores, NEGATIVE)
        top = lax.optimization_barrier(jnp.max(masked, -1, keepdims=True))
        weights = jnp.where(allowed, jnp.exp(masked - top), 0.0)
        probs = low(weights / lax.optimization_barrier(jnp.sum(weights, -1, keepdims=True)))
        return jnp.einsum('hqk,khd->qhd', probs, value_heads, precision=HIGHEST)
    blocks = lax.map(jax.checkpoint(one_block), (query.reshape(count // step, step, HEADS, head_dim), ids.reshape(count // step, step)))
    return blocks.reshape(count, D)

def one_sequence(inputs, ids, params):
    gain_one, shift_one, weight_qkv, bias_query, bias_value, weight_out, bias_out, gain_two, shift_two, weight_up, bias_up, weight_down, bias_down = params
    normed = low(layer_norm(inputs, gain_one, shift_one))
    qkv_bias = jnp.concatenate([bias_query, jnp.zeros((D,), jnp.float32), bias_value])
    projected = rounded_both(matmul(normed, weight_qkv) + qkv_bias)
    mixed = rounded_both(attend(projected[:, :D], projected[:, D:2 * D], projected[:, 2 * D:], ids))
    attended = low_back(matmul(mixed, weight_out) + bias_out)
    middle = inputs + attended
    normed_two = low(layer_norm(middle, gain_two, shift_two))
    pre_act = low_back(matmul(normed_two, weight_up) + bias_up)
    activated = low(jax.nn.gelu(pre_act, approximate=False))
    return middle + matmul(activated, weight_down) + bias_down

def reference(tokens, block_ids, ln1_gain, ln1_bias, w_qkv, q_bias, v_bias, w_out, out_bias, ln2_gain, ln2_bias, w_up, up_bias, w_down, down_bias, cotangent):
    params = tuple((p.astype(jnp.float32) for p in (ln1_gain, ln1_bias, w_qkv, q_bias, v_bias, w_out, out_bias, ln2_gain, ln2_bias, w_up, up_bias, w_down, down_bias)))
    inputs = tokens.astype(jnp.float32)

    def forward(values, weights):

        def per_sequence(pair):
            return one_sequence(pair[0], pair[1], weights)
        return lax.map(jax.checkpoint(per_sequence), (values, block_ids))
    result, pull = jax.vjp(forward, inputs, params)
    input_grad, grads = pull(cotangent.astype(jnp.float32))
    return (result.astype(jnp.bfloat16), input_grad, grads[0], grads[1], grads[2], grads[3], grads[4], grads[5], grads[6], grads[7], grads[8], grads[9], grads[10], grads[11], grads[12])
```

```python
import math

import jax
import jax.numpy as jnp
from jax import lax
from jax.sharding import PartitionSpec as P

HEADS = 12


EPSILON = 1e-06
NEGATIVE = -1e30


def layer_norm(values, gain, shift):
    center = values - jnp.mean(values, -1, keepdims=True)
    spread = jnp.mean(center * center, -1, keepdims=True)
    return center * lax.rsqrt(spread + EPSILON) * gain + shift


def block_rows(count):
    return math.gcd(count, 512)


def masked_scores(query_heads, key_heads, query_ids, key_ids, scale):
    raw = (
        jnp.einsum("qhd,khd->hqk", query_heads, key_heads, preferred_element_type=jnp.float32)
        * scale
    )
    allowed = key_ids[None, None, :] <= query_ids[None, :, None]
    return (raw, allowed)


def attend_forward(query_heads, query_ids, keys_all, values_all, ids_all, scale):
    tok_rows, heads, head_dim = query_heads.shape
    total_keys = keys_all.shape[0]
    step = block_rows(total_keys)
    blocks = total_keys // step

    def attend_visit(carry, inputs):
        running, total, accum = carry
        key_block, value_block, id_block = inputs
        raw, allowed = masked_scores(query_heads, key_block, query_ids, id_block, scale)
        masked = jnp.where(allowed, raw, NEGATIVE)
        new_top = jnp.maximum(running, jnp.max(masked, -1))
        weights = jnp.where(allowed, jnp.exp(masked - new_top[..., None]), 0.0)
        factor = jnp.exp(running - new_top)
        total = total * factor + jnp.sum(weights, -1)
        accum = accum * factor[..., None] + jnp.einsum(
            "hqk,khd->hqd",
            weights.astype(jnp.bfloat16),
            value_block,
            preferred_element_type=jnp.float32,
        )
        return ((new_top, total, accum), None)

    start_state = (
        jnp.full((heads, tok_rows), NEGATIVE, jnp.float32),
        jnp.zeros((heads, tok_rows), jnp.float32),
        jnp.zeros((heads, tok_rows, head_dim), jnp.float32),
    )
    (running, total, accum), _ = lax.scan(
        attend_visit,
        start_state,
        (
            keys_all.reshape(blocks, step, heads, head_dim),
            values_all.reshape(blocks, step, heads, head_dim),
            ids_all.reshape(blocks, step),
        ),
    )
    output_heads = jnp.transpose(accum / total[..., None], (1, 0, 2))
    return (output_heads, running + jnp.log(total))


def query_gradient(
    query_heads, grad_heads, query_ids, keys_all, values_all, ids_all, logsum, inner, scale
):
    tok_rows, heads, head_dim = query_heads.shape
    total_keys = keys_all.shape[0]
    step = block_rows(total_keys)
    blocks = total_keys // step

    def query_visit(accum, inputs):
        key_block, value_block, id_block = inputs
        raw, allowed = masked_scores(query_heads, key_block, query_ids, id_block, scale)
        probs = jnp.where(allowed, jnp.exp(raw - logsum[..., None]), 0.0)
        grad_probs = jnp.einsum(
            "qhd,khd->hqk", grad_heads, value_block, preferred_element_type=jnp.float32
        )
        grad_scores = (probs * (grad_probs - inner[..., None])).astype(jnp.bfloat16)
        accum = accum + jnp.einsum(
            "hqk,khd->qhd", grad_scores, key_block, preferred_element_type=jnp.float32
        )
        return (accum, None)

    accum, _ = lax.scan(
        query_visit,
        jnp.zeros((tok_rows, heads, head_dim), jnp.float32),
        (
            keys_all.reshape(blocks, step, heads, head_dim),
            values_all.reshape(blocks, step, heads, head_dim),
            ids_all.reshape(blocks, step),
        ),
    )
    return accum * scale


def pair_grads(
    query_heads, grad_heads, query_ids, logsum, inner, key_heads, value_heads, key_ids, scale
):
    raw, allowed = masked_scores(query_heads, key_heads, query_ids, key_ids, scale)
    probs = jnp.where(allowed, jnp.exp(raw - logsum[..., None]), 0.0)
    grad_probs = jnp.einsum(
        "qhd,khd->hqk", grad_heads, value_heads, preferred_element_type=jnp.float32
    )
    grad_scores = (probs * (grad_probs - inner[..., None])).astype(jnp.bfloat16)
    grad_keys = (
        jnp.einsum("hqk,qhd->khd", grad_scores, query_heads, preferred_element_type=jnp.float32)
        * scale
    )
    grad_values = jnp.einsum(
        "hqk,qhd->khd", probs.astype(jnp.bfloat16), grad_heads, preferred_element_type=jnp.float32
    )
    return (grad_keys, grad_values)


def shards_general(
    tokens,
    block_ids,
    ln1_gain,
    ln1_bias,
    w_qkv,
    q_bias,
    v_bias,
    w_out,
    out_bias,
    ln2_gain,
    ln2_bias,
    w_up,
    up_bias,
    w_down,
    down_bias,
    cotangent,
):
    gathered = (
        lax.all_gather(ln1_gain, "seq", axis=0, tiled=True),
        lax.all_gather(ln1_bias, "seq", axis=0, tiled=True),
        lax.all_gather(w_qkv, "seq", axis=0, tiled=True),
        lax.all_gather(q_bias, "seq", axis=0, tiled=True),
        lax.all_gather(v_bias, "seq", axis=0, tiled=True),
        lax.all_gather(w_out, "seq", axis=0, tiled=True),
        lax.all_gather(out_bias, "seq", axis=0, tiled=True),
        lax.all_gather(ln2_gain, "seq", axis=0, tiled=True),
        lax.all_gather(ln2_bias, "seq", axis=0, tiled=True),
        lax.all_gather(w_up, "seq", axis=0, tiled=True),
        lax.all_gather(up_bias, "seq", axis=0, tiled=True),
        lax.all_gather(w_down, "seq", axis=0, tiled=True),
        lax.all_gather(down_bias, "seq", axis=0, tiled=True),
    )
    attention_part = gathered[:7]
    feed_part = gathered[7:]
    gain_one, shift_one, weight_qkv, bias_query, bias_value, weight_out, bias_out = attention_part
    width = weight_out.shape[0]
    heads = HEADS
    head_dim = width // heads
    scale = 1.0 / math.sqrt(head_dim)
    inputs = tokens[0].astype(jnp.float32)
    tok_rows = inputs.shape[0]
    own_ids = block_ids[0]
    gain_one_f = gain_one.astype(jnp.float32)
    shift_one_f = shift_one.astype(jnp.float32)
    normed_one, norm_one_pull = jax.vjp(layer_norm, inputs, gain_one_f, shift_one_f)
    normed_low = normed_one.astype(jnp.bfloat16)
    qkv_bias = jnp.concatenate(
        [
            bias_query.astype(jnp.float32),
            jnp.zeros((width,), jnp.float32),
            bias_value.astype(jnp.float32),
        ]
    )
    projected = (
        jnp.dot(normed_low, weight_qkv, preferred_element_type=jnp.float32) + qkv_bias
    ).astype(jnp.bfloat16)
    query_low = projected[:, :width]
    key_low = projected[:, width : 2 * width]
    value_low = projected[:, 2 * width :]
    ids_all = lax.all_gather(block_ids, "ctx", axis=1, tiled=True)[0]
    keys_all, values_all = (
        lax.all_gather(key_low, "ctx", axis=0, tiled=True),
        lax.all_gather(value_low, "ctx", axis=0, tiled=True),
    )
    query_heads = query_low.reshape(tok_rows, heads, head_dim)
    output_heads, logsum = attend_forward(
        query_heads, own_ids, keys_all, values_all, ids_all, scale
    )
    mixed_low = output_heads.reshape(tok_rows, width).astype(jnp.bfloat16)
    attended = jnp.dot(mixed_low, weight_out, preferred_element_type=jnp.float32) + bias_out.astype(
        jnp.float32
    )
    middle = inputs + attended
    gain_two, shift_two, weight_up, bias_up, weight_down, bias_down = feed_part
    gain_two_f = gain_two.astype(jnp.float32)
    shift_two_f = shift_two.astype(jnp.float32)
    normed_two, norm_two_pull = jax.vjp(layer_norm, middle, gain_two_f, shift_two_f)
    normed_two_low = normed_two.astype(jnp.bfloat16)
    pre_act = jnp.dot(
        normed_two_low, weight_up, preferred_element_type=jnp.float32
    ) + bias_up.astype(jnp.float32)
    activated, gelu_pull = jax.vjp(lambda values: jax.nn.gelu(values, approximate=False), pre_act)
    activated_low = activated.astype(jnp.bfloat16)
    result = (
        middle
        + jnp.dot(activated_low, weight_down, preferred_element_type=jnp.float32)
        + bias_down.astype(jnp.float32)
    )
    grad_out = cotangent[0]
    grad_out_f = grad_out.astype(jnp.float32)
    grad_weight_down = jnp.einsum(
        "tf,td->fd", activated_low, grad_out, preferred_element_type=jnp.float32
    )
    grad_bias_down = jnp.sum(grad_out_f, 0)
    grad_hidden = jnp.einsum("td,fd->tf", grad_out, weight_down, preferred_element_type=jnp.float32)
    grad_pre_low = gelu_pull(grad_hidden)[0].astype(jnp.bfloat16)
    grad_weight_up = jnp.einsum(
        "td,tf->df", normed_two_low, grad_pre_low, preferred_element_type=jnp.float32
    )
    grad_bias_up = jnp.sum(grad_pre_low.astype(jnp.float32), 0)
    grad_normed_two = jnp.einsum(
        "tf,df->td", grad_pre_low, weight_up, preferred_element_type=jnp.float32
    )
    grad_middle_part, grad_gain_two, grad_shift_two = norm_two_pull(grad_normed_two)
    grad_middle = grad_out_f + grad_middle_part
    grad_attended = grad_middle.astype(jnp.bfloat16)
    grad_weight_out = jnp.einsum(
        "td,te->de", mixed_low, grad_attended, preferred_element_type=jnp.float32
    )
    grad_bias_out = jnp.sum(grad_attended.astype(jnp.float32), 0)
    grad_mixed = jnp.einsum(
        "te,de->td", grad_attended, weight_out, preferred_element_type=jnp.float32
    ).astype(jnp.bfloat16)
    grad_heads = grad_mixed.reshape(tok_rows, heads, head_dim)
    inner = jnp.einsum("thd,thd->ht", grad_heads.astype(jnp.float32), output_heads)
    grad_query = query_gradient(
        query_heads, grad_heads, own_ids, keys_all, values_all, ids_all, logsum, inner, scale
    )
    step = block_rows(lax.axis_size("ctx") * tok_rows)
    blocks = lax.axis_size("ctx") * tok_rows // step
    key_part = keys_all.reshape(blocks, step, heads, head_dim)
    value_part = values_all.reshape(blocks, step, heads, head_dim)
    id_part = ids_all.reshape(blocks, step)

    def key_visit(carry, inputs):
        grad_keys, grad_values = pair_grads(
            query_heads, grad_heads, own_ids, logsum, inner, inputs[0], inputs[1], inputs[2], scale
        )
        joined = jnp.concatenate(
            [grad_keys.reshape(step, width), grad_values.reshape(step, width)], 1
        )
        return (carry, joined)

    _, terms = lax.scan(key_visit, jnp.zeros((), jnp.float32), (key_part, value_part, id_part))
    key_value_grads = lax.psum_scatter(
        terms.reshape(lax.axis_size("ctx") * tok_rows, 2 * width),
        "ctx",
        scatter_dimension=0,
        tiled=True,
    )
    grad_keys_all = key_value_grads[:, :width]
    grad_values_all = key_value_grads[:, width:]
    grad_query_low = grad_query.reshape(tok_rows, width).astype(jnp.bfloat16)
    grad_value_low = grad_values_all.astype(jnp.bfloat16)
    grad_projected = jnp.concatenate(
        [grad_query_low, grad_keys_all.astype(jnp.bfloat16), grad_value_low], 1
    )
    grad_weight_qkv = jnp.einsum(
        "td,te->de", normed_low, grad_projected, preferred_element_type=jnp.float32
    )
    grad_bias_query = jnp.sum(grad_query_low.astype(jnp.float32), 0)
    grad_bias_value = jnp.sum(grad_value_low.astype(jnp.float32), 0)
    grad_normed_one = jnp.einsum(
        "te,de->td", grad_projected, weight_qkv, preferred_element_type=jnp.float32
    )
    grad_input_part, grad_gain_one, grad_shift_one = norm_one_pull(grad_normed_one)
    input_grad = grad_middle + grad_input_part
    local_grads = (
        grad_gain_one,
        grad_shift_one,
        grad_weight_qkv,
        grad_bias_query,
        grad_bias_value,
        grad_weight_out,
        grad_bias_out,
        grad_gain_two,
        grad_shift_two,
        grad_weight_up,
        grad_bias_up,
        grad_weight_down,
        grad_bias_down,
    )
    shares = (
        lax.psum_scatter(
            local_grads[0].astype(jnp.bfloat16), "seq", scatter_dimension=0, tiled=True
        ).astype(jnp.float32),
        lax.psum_scatter(
            local_grads[1].astype(jnp.bfloat16), "seq", scatter_dimension=0, tiled=True
        ).astype(jnp.float32),
        lax.psum_scatter(
            local_grads[2].astype(jnp.bfloat16), "seq", scatter_dimension=0, tiled=True
        ).astype(jnp.float32),
        lax.psum_scatter(
            local_grads[3].astype(jnp.bfloat16), "seq", scatter_dimension=0, tiled=True
        ).astype(jnp.float32),
        lax.psum_scatter(
            local_grads[4].astype(jnp.bfloat16), "seq", scatter_dimension=0, tiled=True
        ).astype(jnp.float32),
        lax.psum_scatter(
            local_grads[5].astype(jnp.bfloat16), "seq", scatter_dimension=0, tiled=True
        ).astype(jnp.float32),
        lax.psum_scatter(
            local_grads[6].astype(jnp.bfloat16), "seq", scatter_dimension=0, tiled=True
        ).astype(jnp.float32),
        lax.psum_scatter(
            local_grads[7].astype(jnp.bfloat16), "seq", scatter_dimension=0, tiled=True
        ).astype(jnp.float32),
        lax.psum_scatter(
            local_grads[8].astype(jnp.bfloat16), "seq", scatter_dimension=0, tiled=True
        ).astype(jnp.float32),
        lax.psum_scatter(
            local_grads[9].astype(jnp.bfloat16), "seq", scatter_dimension=0, tiled=True
        ).astype(jnp.float32),
        lax.psum_scatter(
            local_grads[10].astype(jnp.bfloat16), "seq", scatter_dimension=0, tiled=True
        ).astype(jnp.float32),
        lax.psum_scatter(
            local_grads[11].astype(jnp.bfloat16), "seq", scatter_dimension=0, tiled=True
        ).astype(jnp.float32),
        lax.psum_scatter(
            local_grads[12].astype(jnp.bfloat16), "seq", scatter_dimension=0, tiled=True
        ).astype(jnp.float32),
    )
    totals = lax.psum(
        (
            shares[0],
            shares[1],
            shares[2],
            shares[3],
            shares[4],
            shares[5],
            shares[6],
            shares[7],
            shares[8],
            shares[9],
            shares[10],
            shares[11],
            shares[12],
        ),
        "ctx",
    )
    return (result.astype(jnp.bfloat16)[None], input_grad[None]) + tuple(totals)


def core_swap(values):
    return lax.ppermute(values, "ctx", [(i, i ^ 1) for i in range(8)])


def chip_swap(values, mask):
    return lax.ppermute(values, "ctx", [(i, i ^ (2 * mask)) for i in range(8)])


def seq_swap(values, mask):
    return lax.ppermute(values, "seq", [(i, i ^ mask) for i in range(4)])


def chip_gather(values):
    return [values] + [chip_swap(values, m) for m in (1, 2, 3)]


def seq_gather(values):
    return [values] + [seq_swap(values, m) for m in (1, 2, 3)]


def unxor(blocks, index):
    low, high = (index & 1) == 1, (index >> 1) == 1
    first = [jnp.where(low, blocks[z ^ 1], blocks[z]) for z in range(4)]
    return [jnp.where(high, first[z ^ 2], first[z]) for z in range(4)]


def core_order(own, other, core):
    return [jnp.where(core == 0, own, other), jnp.where(core == 0, other, own)]


def gather_rows(piece, seq, core):
    mine = jnp.stack(unxor(seq_gather(piece), seq))
    theirs = core_swap(mine)
    both = jnp.stack(core_order(mine, theirs, core), 1)
    return both.reshape(-1, piece.shape[1])


def column_slice(values, k, parts):
    width = values.shape[1] // parts
    quarter = width // 4
    return jnp.concatenate(
        [
            lax.dynamic_slice_in_dim(values, width * p + quarter * k, quarter, 1)
            for p in range(parts)
        ],
        1,
    )


def reduce_rows(partial, seq, core):
    low = partial.astype(jnp.bfloat16)
    other = lax.dynamic_index_in_dim(low, 1 - core, 1, False)
    own = lax.dynamic_index_in_dim(partial, core, 1, False)
    halves = own + core_swap(other).astype(jnp.float32)
    halves_low = halves.astype(jnp.bfloat16)
    total = lax.dynamic_index_in_dim(halves, seq, 0, False)
    for m in (1, 2, 3):
        block = lax.dynamic_index_in_dim(halves_low, seq ^ m, 0, False)
        total = total + seq_swap(block, m).astype(jnp.float32)
    return total


def gather_ctx(piece, k, core):
    mine = jnp.stack(unxor(chip_gather(piece), k))
    theirs = core_swap(mine)
    first, second = core_order(mine, theirs, core)
    return [[first[q], second[q]] for q in range(4)]


def shards(
    tokens,
    block_ids,
    ln1_gain,
    ln1_bias,
    w_qkv,
    q_bias,
    v_bias,
    w_out,
    out_bias,
    ln2_gain,
    ln2_bias,
    w_up,
    up_bias,
    w_down,
    down_bias,
    cotangent,
):
    f32, bf16 = jnp.float32, jnp.bfloat16
    seq = lax.axis_index("seq")
    ctx = lax.axis_index("ctx")
    k, core = ctx // 2, ctx % 2
    width = tokens.shape[-1]
    quarter = width // 4
    half = quarter // 2
    head_dim = width // HEADS
    scale = 1.0 / math.sqrt(head_dim)
    rows = tokens.shape[1]

    def placed(vec):
        return jnp.concatenate([jnp.where(seq == z, vec, jnp.zeros_like(vec)) for z in range(4)])

    small = [ln1_gain, ln1_bias, q_bias, v_bias, out_bias, ln2_gain, ln2_bias, down_bias]
    small = [placed(v) for v in small] + [
        jnp.where(seq == z, up_bias, jnp.zeros_like(up_bias)) for z in range(4)
    ]
    small_all = sum(v.astype(f32) for v in seq_gather(jnp.stack(small)))
    gain_one, shift_one, bias_q, bias_v, bias_out, gain_two, shift_two, bias_down = small_all[:8]
    bias_up = small_all[8:]

    def rows_of_core(values):
        return lax.dynamic_slice_in_dim(values, half * core, half, 0)

    weight_qkv = gather_rows(column_slice(rows_of_core(w_qkv), k, 3), seq, core)
    ids_row = jnp.pad(block_ids.astype(bf16), ((0, 7), (0, width - rows)))
    packed = chip_gather(jnp.concatenate([tokens[0], ids_row], 0))
    weight_out = gather_rows(rows_of_core(w_out), seq, core)
    weight_up = gather_rows(column_slice(rows_of_core(w_up), k, 4), seq, core)
    weight_down = gather_rows(
        lax.dynamic_slice_in_dim(w_down, quarter * k + half * core, half, 0), seq, core
    )
    inputs = jnp.concatenate([p[:rows] for p in packed], 0).astype(f32)
    ids_own = jnp.concatenate([p[rows, :rows] for p in packed])
    cot = jnp.concatenate(chip_gather(cotangent[0]), 0)

    def normal(values):
        center = values - jnp.mean(values, -1, keepdims=True)
        rstd = lax.rsqrt(jnp.mean(center * center, -1, keepdims=True) + EPSILON)
        return center * rstd, rstd

    hat_one, rstd_one = normal(inputs)
    normed = (hat_one * gain_one + shift_one).astype(bf16)
    bias_qkv = jnp.concatenate(
        [
            lax.dynamic_slice_in_dim(bias_q, quarter * k, quarter, 0),
            jnp.zeros((quarter,), f32),
            lax.dynamic_slice_in_dim(bias_v, quarter * k, quarter, 0),
        ]
    )
    projected = (jnp.dot(normed, weight_qkv, preferred_element_type=f32) + bias_qkv).astype(bf16)
    query = projected[:, :quarter]
    pair = projected[:, quarter:]
    ids_pad = jnp.pad(ids_own.reshape(4, rows), ((0, 4), (0, 2 * quarter - rows)))
    other_pack = core_swap(jnp.concatenate([pair, ids_pad], 0))
    own_rows = 4 * rows
    pair_all = jnp.concatenate([pair, other_pack[:own_rows]], 0)
    ids_all = jnp.concatenate([ids_own, other_pack[own_rows : own_rows + 4, :rows].reshape(-1)])
    heads = HEADS // 4
    query_heads = query.reshape(own_rows, heads, head_dim)
    key_heads = pair_all[:, :quarter].reshape(2 * own_rows, heads, head_dim)
    value_heads = pair_all[:, quarter:].reshape(2 * own_rows, heads, head_dim)
    allowed = (ids_all[None, :] <= ids_own[:, None])[None]
    scores = jnp.einsum("qhd,khd->hqk", query_heads, key_heads, preferred_element_type=f32) * scale
    masked = jnp.where(allowed, scores, NEGATIVE)
    top = jnp.max(masked, -1, keepdims=True)
    weights = jnp.where(allowed, jnp.exp(masked - top), 0.0)
    probs = weights / jnp.sum(weights, -1, keepdims=True)
    probs_low = probs.astype(bf16)
    mixed_f = jnp.einsum("hqk,khd->qhd", probs_low, value_heads, preferred_element_type=f32)
    mixed = mixed_f.reshape(own_rows, quarter).astype(bf16)

    mixed_blocks = chip_gather(mixed)
    attended = bias_out
    mixed_rel = []
    for m in range(4):
        block = mixed_blocks[m].reshape(4, rows, quarter)
        block = jnp.concatenate([block[r ^ m] for r in range(4)], 0)
        mixed_rel.append(block)
        w_block = lax.dynamic_slice_in_dim(weight_out, quarter * (k ^ m), quarter, 0)
        attended = attended + jnp.dot(block, w_block, preferred_element_type=f32)
    middle = inputs + attended
    hat_two, rstd_two = normal(middle)
    normed_two = (hat_two * gain_two + shift_two).astype(bf16)
    bias_up_k = lax.dynamic_slice_in_dim(bias_up, quarter * k, quarter, 1).reshape(-1)
    pre_act = jnp.dot(normed_two, weight_up, preferred_element_type=f32) + bias_up_k
    cdf = 0.5 * (1.0 + lax.erf(pre_act * (1.0 / math.sqrt(2.0))))
    activated = (pre_act * cdf).astype(bf16)
    down = jnp.dot(activated, weight_down, preferred_element_type=f32).astype(bf16)

    def scatter(partial):
        blocks = partial.reshape(4, rows, -1)
        total = blocks[0].astype(f32)
        for m in (1, 2, 3):
            total = total + chip_swap(blocks[m], m).astype(f32)
        return total

    grad_hidden = jnp.einsum("td,fd->tf", cot, weight_down, preferred_element_type=f32)
    slope = cdf + pre_act * jnp.exp(-0.5 * pre_act * pre_act) * (1.0 / math.sqrt(2.0 * math.pi))
    grad_pre = (grad_hidden * slope).astype(bf16)
    grad_normed_two = jnp.einsum("tf,df->td", grad_pre, weight_up, preferred_element_type=f32)
    grad_gain_two = jnp.sum(grad_normed_two * hat_two, 0)
    grad_shift_two = jnp.sum(grad_normed_two, 0)
    err_two = scatter(grad_normed_two.astype(bf16))

    def norm_back(err, gain, hat, rstd):
        scaled = err * gain
        return rstd * (
            scaled
            - jnp.mean(scaled, -1, keepdims=True)
            - hat * jnp.mean(scaled * hat, -1, keepdims=True)
        )

    cot_own = cot[:rows].astype(f32)
    grad_middle = cot_own + norm_back(err_two, gain_two, hat_two[:rows], rstd_two[:rows])
    grad_attended_own = grad_middle.astype(bf16)
    grad_attended = jnp.concatenate(chip_gather(grad_attended_own), 0)
    w_out_k = lax.dynamic_slice_in_dim(weight_out, quarter * k, quarter, 0)
    grad_mixed = jnp.einsum("te,de->td", grad_attended, w_out_k, preferred_element_type=f32).astype(
        bf16
    )
    grad_heads = grad_mixed.reshape(own_rows, heads, head_dim)
    grad_probs = jnp.einsum("qhd,khd->hqk", grad_heads, value_heads, preferred_element_type=f32)
    inner = jnp.sum(probs * grad_probs, -1, keepdims=True)
    grad_scores = (probs * (grad_probs - inner)).astype(bf16)
    grad_query = jnp.einsum("hqk,khd->qhd", grad_scores, key_heads, preferred_element_type=f32)
    grad_key = jnp.einsum("hqk,qhd->khd", grad_scores, query_heads, preferred_element_type=f32)
    grad_value = jnp.einsum("hqk,qhd->khd", probs_low, grad_heads, preferred_element_type=f32)
    grad_pair = jnp.concatenate(
        [
            (grad_key * scale).reshape(2 * own_rows, quarter),
            grad_value.reshape(2 * own_rows, quarter),
        ],
        1,
    )
    grad_pair_own = grad_pair[:own_rows] + core_swap(grad_pair[own_rows:].astype(bf16)).astype(f32)
    grad_projected = jnp.concatenate(
        [(grad_query * scale).reshape(own_rows, quarter).astype(bf16), grad_pair_own.astype(bf16)], 1
    )
    grad_normed_one = jnp.einsum(
        "te,de->td", grad_projected, weight_qkv, preferred_element_type=f32
    )
    grad_gain_one = jnp.sum(grad_normed_one * hat_one, 0)
    grad_shift_one = jnp.sum(grad_normed_one, 0)
    err_one = scatter(grad_normed_one.astype(bf16))
    input_grad = grad_middle + norm_back(err_one, gain_one, hat_one[:rows], rstd_one[:rows])
    result = (middle[:rows] + scatter(down) + bias_down).astype(bf16)

    def by_rows(partial):
        return partial.reshape(4, 2, half, -1)

    def wgrad(left, right):
        return jnp.einsum("td,te->de", left, right, preferred_element_type=f32)

    piece_down = reduce_rows(by_rows(wgrad(activated, cot)), seq, core)
    grad_w_down = jnp.concatenate(
        [p for pair_ in gather_ctx(piece_down.astype(bf16), k, core) for p in pair_], 0
    ).astype(f32)

    def columns(pieces, parts):
        out = []
        for c in range(2):
            cols = [
                pieces[q][c][:, quarter * p : quarter * (p + 1)]
                for p in range(parts)
                for q in range(4)
            ]
            out.append(jnp.concatenate(cols, 1))
        return jnp.concatenate(out, 0).astype(f32)

    piece_up = reduce_rows(by_rows(wgrad(normed_two, grad_pre)), seq, core)
    grad_w_up = columns(gather_ctx(piece_up.astype(bf16), k, core), 4)
    ga_k = lax.dynamic_slice_in_dim(grad_attended, quarter * k, quarter, 1)
    grad_out_part = jnp.stack(unxor([wgrad(b, ga_k) for b in mixed_rel], k)).reshape(width, quarter)
    piece_qkv = reduce_rows(
        by_rows(jnp.concatenate([wgrad(normed, grad_projected), grad_out_part], 1)), seq, core
    )
    pieces = gather_ctx(piece_qkv.astype(bf16), k, core)
    grad_w_qkv = columns([[p[:, : 3 * quarter] for p in pair_] for pair_ in pieces], 3)
    grad_w_out = columns([[p[:, 3 * quarter :] for p in pair_] for pair_ in pieces], 1)

    def chip_placed(vec):
        return jnp.concatenate([jnp.where(k == q, vec, jnp.zeros_like(vec)) for q in range(4)], -1)

    projected_sums = jnp.sum(grad_projected.astype(f32), 0)
    up_sums = jnp.sum(grad_pre.astype(f32), 0).reshape(4, quarter)
    vectors = [
        grad_gain_one,
        grad_shift_one,
        chip_placed(projected_sums[:quarter]),
        chip_placed(projected_sums[2 * quarter :]),
        jnp.sum(grad_attended_own.astype(f32), 0),
        grad_gain_two,
        grad_shift_two,
        jnp.sum(cot_own, 0),
    ]
    small_part = jnp.stack(vectors).reshape(8, 4, quarter).transpose(1, 0, 2).reshape(4, 8 * quarter)
    small_part = jnp.concatenate([small_part, chip_placed(up_sums)], 1)
    small_part = lax.psum(small_part, "ctx")
    total = lax.dynamic_index_in_dim(small_part, seq, 0, False)
    for m in (1, 2, 3):
        total = total + seq_swap(lax.dynamic_index_in_dim(small_part, seq ^ m, 0, False), m)
    g = [total[quarter * n : quarter * (n + 1)] for n in range(8)]
    g_up = total[8 * quarter :]
    return (
        result[None],
        input_grad[None],
        g[0],
        g[1],
        grad_w_qkv,
        g[2],
        g[3],
        grad_w_out,
        g[4],
        g[5],
        g[6],
        grad_w_up,
        g_up,
        grad_w_down,
        g[7],
    )


def solution(mesh):
    placed = (
        P("seq", "ctx", None),
        P("seq", "ctx"),
        P("seq"),
        P("seq"),
        P("seq", None),
        P("seq"),
        P("seq"),
        P("seq", None),
        P("seq"),
        P("seq"),
        P("seq"),
        P("seq", None),
        P("seq"),
        P("seq", None),
        P("seq"),
        P("seq", "ctx", None),
    )
    return jax.shard_map(
        shards if mesh.shape["ctx"] == 8 and mesh.shape["seq"] == 4 else shards_general,
        mesh=mesh,
        in_specs=placed,
        out_specs=(
            P("seq", "ctx", None),
            P("seq", "ctx", None),
            P("seq"),
            P("seq"),
            P("seq", None),
            P("seq"),
            P("seq"),
            P("seq", None),
            P("seq"),
            P("seq"),
            P("seq"),
            P("seq", None),
            P("seq"),
            P("seq", None),
            P("seq"),
        ),
        check_vma=False,
    )
```

```python
import math

import jax
import jax.numpy as jnp
from jax import lax
from jax.experimental import pallas as pl
from jax.experimental.pallas import tpu as pltpu
from jax.sharding import PartitionSpec as P

HEADS = 12


EPSILON = 1e-06
NEGATIVE = -1e30


def layer_norm(values, gain, shift):
    center = values - jnp.mean(values, -1, keepdims=True)
    spread = jnp.mean(center * center, -1, keepdims=True)
    return center * lax.rsqrt(spread + EPSILON) * gain + shift


def block_rows(count):
    return math.gcd(count, 512)


def masked_scores(query_heads, key_heads, query_ids, key_ids, scale):
    raw = (
        jnp.einsum("qhd,khd->hqk", query_heads, key_heads, preferred_element_type=jnp.float32)
        * scale
    )
    allowed = key_ids[None, None, :] <= query_ids[None, :, None]
    return (raw, allowed)


def attend_forward(query_heads, query_ids, keys_all, values_all, ids_all, scale):
    tok_rows, heads, head_dim = query_heads.shape
    total_keys = keys_all.shape[0]
    step = block_rows(total_keys)
    blocks = total_keys // step

    def attend_visit(carry, inputs):
        running, total, accum = carry
        key_block, value_block, id_block = inputs
        raw, allowed = masked_scores(query_heads, key_block, query_ids, id_block, scale)
        masked = jnp.where(allowed, raw, NEGATIVE)
        new_top = jnp.maximum(running, jnp.max(masked, -1))
        weights = jnp.where(allowed, jnp.exp(masked - new_top[..., None]), 0.0)
        factor = jnp.exp(running - new_top)
        total = total * factor + jnp.sum(weights, -1)
        accum = accum * factor[..., None] + jnp.einsum(
            "hqk,khd->hqd",
            weights.astype(jnp.bfloat16),
            value_block,
            preferred_element_type=jnp.float32,
        )
        return ((new_top, total, accum), None)

    start_state = (
        jnp.full((heads, tok_rows), NEGATIVE, jnp.float32),
        jnp.zeros((heads, tok_rows), jnp.float32),
        jnp.zeros((heads, tok_rows, head_dim), jnp.float32),
    )
    (running, total, accum), _ = lax.scan(
        attend_visit,
        start_state,
        (
            keys_all.reshape(blocks, step, heads, head_dim),
            values_all.reshape(blocks, step, heads, head_dim),
            ids_all.reshape(blocks, step),
        ),
    )
    output_heads = jnp.transpose(accum / total[..., None], (1, 0, 2))
    return (output_heads, running + jnp.log(total))


def query_gradient(
    query_heads, grad_heads, query_ids, keys_all, values_all, ids_all, logsum, inner, scale
):
    tok_rows, heads, head_dim = query_heads.shape
    total_keys = keys_all.shape[0]
    step = block_rows(total_keys)
    blocks = total_keys // step

    def query_visit(accum, inputs):
        key_block, value_block, id_block = inputs
        raw, allowed = masked_scores(query_heads, key_block, query_ids, id_block, scale)
        probs = jnp.where(allowed, jnp.exp(raw - logsum[..., None]), 0.0)
        grad_probs = jnp.einsum(
            "qhd,khd->hqk", grad_heads, value_block, preferred_element_type=jnp.float32
        )
        grad_scores = (probs * (grad_probs - inner[..., None])).astype(jnp.bfloat16)
        accum = accum + jnp.einsum(
            "hqk,khd->qhd", grad_scores, key_block, preferred_element_type=jnp.float32
        )
        return (accum, None)

    accum, _ = lax.scan(
        query_visit,
        jnp.zeros((tok_rows, heads, head_dim), jnp.float32),
        (
            keys_all.reshape(blocks, step, heads, head_dim),
            values_all.reshape(blocks, step, heads, head_dim),
            ids_all.reshape(blocks, step),
        ),
    )
    return accum * scale


def pair_grads(
    query_heads, grad_heads, query_ids, logsum, inner, key_heads, value_heads, key_ids, scale
):
    raw, allowed = masked_scores(query_heads, key_heads, query_ids, key_ids, scale)
    probs = jnp.where(allowed, jnp.exp(raw - logsum[..., None]), 0.0)
    grad_probs = jnp.einsum(
        "qhd,khd->hqk", grad_heads, value_heads, preferred_element_type=jnp.float32
    )
    grad_scores = (probs * (grad_probs - inner[..., None])).astype(jnp.bfloat16)
    grad_keys = (
        jnp.einsum("hqk,qhd->khd", grad_scores, query_heads, preferred_element_type=jnp.float32)
        * scale
    )
    grad_values = jnp.einsum(
        "hqk,qhd->khd", probs.astype(jnp.bfloat16), grad_heads, preferred_element_type=jnp.float32
    )
    return (grad_keys, grad_values)


def shards_general(
    tokens,
    block_ids,
    ln1_gain,
    ln1_bias,
    w_qkv,
    q_bias,
    v_bias,
    w_out,
    out_bias,
    ln2_gain,
    ln2_bias,
    w_up,
    up_bias,
    w_down,
    down_bias,
    cotangent,
):
    gathered = (
        lax.all_gather(ln1_gain, "seq", axis=0, tiled=True),
        lax.all_gather(ln1_bias, "seq", axis=0, tiled=True),
        lax.all_gather(w_qkv, "seq", axis=0, tiled=True),
        lax.all_gather(q_bias, "seq", axis=0, tiled=True),
        lax.all_gather(v_bias, "seq", axis=0, tiled=True),
        lax.all_gather(w_out, "seq", axis=0, tiled=True),
        lax.all_gather(out_bias, "seq", axis=0, tiled=True),
        lax.all_gather(ln2_gain, "seq", axis=0, tiled=True),
        lax.all_gather(ln2_bias, "seq", axis=0, tiled=True),
        lax.all_gather(w_up, "seq", axis=0, tiled=True),
        lax.all_gather(up_bias, "seq", axis=0, tiled=True),
        lax.all_gather(w_down, "seq", axis=0, tiled=True),
        lax.all_gather(down_bias, "seq", axis=0, tiled=True),
    )
    attention_part = gathered[:7]
    feed_part = gathered[7:]
    gain_one, shift_one, weight_qkv, bias_query, bias_value, weight_out, bias_out = attention_part
    width = weight_out.shape[0]
    heads = HEADS
    head_dim = width // heads
    scale = 1.0 / math.sqrt(head_dim)
    inputs = tokens[0].astype(jnp.float32)
    tok_rows = inputs.shape[0]
    own_ids = block_ids[0]
    gain_one_f = gain_one.astype(jnp.float32)
    shift_one_f = shift_one.astype(jnp.float32)
    normed_one, norm_one_pull = jax.vjp(layer_norm, inputs, gain_one_f, shift_one_f)
    normed_low = normed_one.astype(jnp.bfloat16)
    qkv_bias = jnp.concatenate(
        [
            bias_query.astype(jnp.float32),
            jnp.zeros((width,), jnp.float32),
            bias_value.astype(jnp.float32),
        ]
    )
    projected = (
        jnp.dot(normed_low, weight_qkv, preferred_element_type=jnp.float32) + qkv_bias
    ).astype(jnp.bfloat16)
    query_low = projected[:, :width]
    key_low = projected[:, width : 2 * width]
    value_low = projected[:, 2 * width :]
    ids_all = lax.all_gather(block_ids, "ctx", axis=1, tiled=True)[0]
    keys_all, values_all = (
        lax.all_gather(key_low, "ctx", axis=0, tiled=True),
        lax.all_gather(value_low, "ctx", axis=0, tiled=True),
    )
    query_heads = query_low.reshape(tok_rows, heads, head_dim)
    output_heads, logsum = attend_forward(
        query_heads, own_ids, keys_all, values_all, ids_all, scale
    )
    mixed_low = output_heads.reshape(tok_rows, width).astype(jnp.bfloat16)
    attended = jnp.dot(mixed_low, weight_out, preferred_element_type=jnp.float32) + bias_out.astype(
        jnp.float32
    )
    middle = inputs + attended
    gain_two, shift_two, weight_up, bias_up, weight_down, bias_down = feed_part
    gain_two_f = gain_two.astype(jnp.float32)
    shift_two_f = shift_two.astype(jnp.float32)
    normed_two, norm_two_pull = jax.vjp(layer_norm, middle, gain_two_f, shift_two_f)
    normed_two_low = normed_two.astype(jnp.bfloat16)
    pre_act = jnp.dot(
        normed_two_low, weight_up, preferred_element_type=jnp.float32
    ) + bias_up.astype(jnp.float32)
    activated, gelu_pull = jax.vjp(lambda values: jax.nn.gelu(values, approximate=False), pre_act)
    activated_low = activated.astype(jnp.bfloat16)
    result = (
        middle
        + jnp.dot(activated_low, weight_down, preferred_element_type=jnp.float32)
        + bias_down.astype(jnp.float32)
    )
    grad_out = cotangent[0]
    grad_out_f = grad_out.astype(jnp.float32)
    grad_weight_down = jnp.einsum(
        "tf,td->fd", activated_low, grad_out, preferred_element_type=jnp.float32
    )
    grad_bias_down = jnp.sum(grad_out_f, 0)
    grad_hidden = jnp.einsum("td,fd->tf", grad_out, weight_down, preferred_element_type=jnp.float32)
    grad_pre_low = gelu_pull(grad_hidden)[0].astype(jnp.bfloat16)
    grad_weight_up = jnp.einsum(
        "td,tf->df", normed_two_low, grad_pre_low, preferred_element_type=jnp.float32
    )
    grad_bias_up = jnp.sum(grad_pre_low.astype(jnp.float32), 0)
    grad_normed_two = jnp.einsum(
        "tf,df->td", grad_pre_low, weight_up, preferred_element_type=jnp.float32
    )
    grad_middle_part, grad_gain_two, grad_shift_two = norm_two_pull(grad_normed_two)
    grad_middle = grad_out_f + grad_middle_part
    grad_attended = grad_middle.astype(jnp.bfloat16)
    grad_weight_out = jnp.einsum(
        "td,te->de", mixed_low, grad_attended, preferred_element_type=jnp.float32
    )
    grad_bias_out = jnp.sum(grad_attended.astype(jnp.float32), 0)
    grad_mixed = jnp.einsum(
        "te,de->td", grad_attended, weight_out, preferred_element_type=jnp.float32
    ).astype(jnp.bfloat16)
    grad_heads = grad_mixed.reshape(tok_rows, heads, head_dim)
    inner = jnp.einsum("thd,thd->ht", grad_heads.astype(jnp.float32), output_heads)
    grad_query = query_gradient(
        query_heads, grad_heads, own_ids, keys_all, values_all, ids_all, logsum, inner, scale
    )
    step = block_rows(lax.axis_size("ctx") * tok_rows)
    blocks = lax.axis_size("ctx") * tok_rows // step
    key_part = keys_all.reshape(blocks, step, heads, head_dim)
    value_part = values_all.reshape(blocks, step, heads, head_dim)
    id_part = ids_all.reshape(blocks, step)

    def key_visit(carry, inputs):
        grad_keys, grad_values = pair_grads(
            query_heads, grad_heads, own_ids, logsum, inner, inputs[0], inputs[1], inputs[2], scale
        )
        joined = jnp.concatenate(
            [grad_keys.reshape(step, width), grad_values.reshape(step, width)], 1
        )
        return (carry, joined)

    _, terms = lax.scan(key_visit, jnp.zeros((), jnp.float32), (key_part, value_part, id_part))
    key_value_grads = lax.psum_scatter(
        terms.reshape(lax.axis_size("ctx") * tok_rows, 2 * width),
        "ctx",
        scatter_dimension=0,
        tiled=True,
    )
    grad_keys_all = key_value_grads[:, :width]
    grad_values_all = key_value_grads[:, width:]
    grad_query_low = grad_query.reshape(tok_rows, width).astype(jnp.bfloat16)
    grad_value_low = grad_values_all.astype(jnp.bfloat16)
    grad_projected = jnp.concatenate(
        [grad_query_low, grad_keys_all.astype(jnp.bfloat16), grad_value_low], 1
    )
    grad_weight_qkv = jnp.einsum(
        "td,te->de", normed_low, grad_projected, preferred_element_type=jnp.float32
    )
    grad_bias_query = jnp.sum(grad_query_low.astype(jnp.float32), 0)
    grad_bias_value = jnp.sum(grad_value_low.astype(jnp.float32), 0)
    grad_normed_one = jnp.einsum(
        "te,de->td", grad_projected, weight_qkv, preferred_element_type=jnp.float32
    )
    grad_input_part, grad_gain_one, grad_shift_one = norm_one_pull(grad_normed_one)
    input_grad = grad_middle + grad_input_part
    local_grads = (
        grad_gain_one,
        grad_shift_one,
        grad_weight_qkv,
        grad_bias_query,
        grad_bias_value,
        grad_weight_out,
        grad_bias_out,
        grad_gain_two,
        grad_shift_two,
        grad_weight_up,
        grad_bias_up,
        grad_weight_down,
        grad_bias_down,
    )
    shares = (
        lax.psum_scatter(
            local_grads[0].astype(jnp.bfloat16), "seq", scatter_dimension=0, tiled=True
        ).astype(jnp.float32),
        lax.psum_scatter(
            local_grads[1].astype(jnp.bfloat16), "seq", scatter_dimension=0, tiled=True
        ).astype(jnp.float32),
        lax.psum_scatter(
            local_grads[2].astype(jnp.bfloat16), "seq", scatter_dimension=0, tiled=True
        ).astype(jnp.float32),
        lax.psum_scatter(
            local_grads[3].astype(jnp.bfloat16), "seq", scatter_dimension=0, tiled=True
        ).astype(jnp.float32),
        lax.psum_scatter(
            local_grads[4].astype(jnp.bfloat16), "seq", scatter_dimension=0, tiled=True
        ).astype(jnp.float32),
        lax.psum_scatter(
            local_grads[5].astype(jnp.bfloat16), "seq", scatter_dimension=0, tiled=True
        ).astype(jnp.float32),
        lax.psum_scatter(
            local_grads[6].astype(jnp.bfloat16), "seq", scatter_dimension=0, tiled=True
        ).astype(jnp.float32),
        lax.psum_scatter(
            local_grads[7].astype(jnp.bfloat16), "seq", scatter_dimension=0, tiled=True
        ).astype(jnp.float32),
        lax.psum_scatter(
            local_grads[8].astype(jnp.bfloat16), "seq", scatter_dimension=0, tiled=True
        ).astype(jnp.float32),
        lax.psum_scatter(
            local_grads[9].astype(jnp.bfloat16), "seq", scatter_dimension=0, tiled=True
        ).astype(jnp.float32),
        lax.psum_scatter(
            local_grads[10].astype(jnp.bfloat16), "seq", scatter_dimension=0, tiled=True
        ).astype(jnp.float32),
        lax.psum_scatter(
            local_grads[11].astype(jnp.bfloat16), "seq", scatter_dimension=0, tiled=True
        ).astype(jnp.float32),
        lax.psum_scatter(
            local_grads[12].astype(jnp.bfloat16), "seq", scatter_dimension=0, tiled=True
        ).astype(jnp.float32),
    )
    totals = lax.psum(
        (
            shares[0],
            shares[1],
            shares[2],
            shares[3],
            shares[4],
            shares[5],
            shares[6],
            shares[7],
            shares[8],
            shares[9],
            shares[10],
            shares[11],
            shares[12],
        ),
        "ctx",
    )
    return (result.astype(jnp.bfloat16)[None], input_grad[None]) + tuple(totals)


QUARTER = 192
HALF = 96
ROWS = 128
WIDTH = 768
OWN = 512
f32, bf16 = jnp.float32, jnp.bfloat16


def core_swap(values):
    return lax.ppermute(values, "ctx", [(i, i ^ 1) for i in range(8)])


def chip_swap(values, mask):
    return lax.ppermute(values, "ctx", [(i, i ^ (2 * mask)) for i in range(8)])


def seq_swap(values, mask):
    return lax.ppermute(values, "seq", [(i, i ^ mask) for i in range(4)])


def chip_gather(values):
    return [values] + [chip_swap(values, m) for m in (1, 2, 3)]


def seq_gather(values):
    return [values] + [seq_swap(values, m) for m in (1, 2, 3)]


def after(values, *earlier):
    return lax.optimization_barrier((values, *earlier))[0]


def column_slice(values, k, parts):
    return jnp.concatenate(
        [
            lax.dynamic_slice_in_dim(values, WIDTH * p + QUARTER * k, QUARTER, 1)
            for p in range(parts)
        ],
        1,
    )


def run(body, pos, args, outs, scratch=(), flops=0, us=2.0, limit=40):
    vmem = pl.BlockSpec(memory_space=pltpu.VMEM)
    return pl.pallas_call(
        body,
        out_shape=[jax.ShapeDtypeStruct(shape, kind) for shape, kind in outs],
        in_specs=[pl.BlockSpec(memory_space=pltpu.SMEM)] + [vmem] * len(args),
        out_specs=[vmem] * len(outs),
        scratch_shapes=[pltpu.VMEM(shape, kind) for shape, kind in scratch],
        compiler_params=pltpu.CompilerParams(vmem_limit_bytes=limit << 20),
        cost_estimate=pl.CostEstimate(
            flops=flops, bytes_accessed=int(us * 3.0e6), transcendentals=0
        ),
    )(pos, *args)


def dot(left, right):
    return lax.dot_general(left, right, (((1,), (0,)), ((), ())), preferred_element_type=f32)


def dot_t(left, right):
    return lax.dot_general(left, right, (((1,), (1,)), ((), ())), preferred_element_type=f32)


def t_dot(left, right):
    return lax.dot_general(left, right, (((0,), (0,)), ((), ())), preferred_element_type=f32)


def normal(values):
    center = values - jnp.mean(values, -1, keepdims=True)
    rstd = lax.rsqrt(jnp.mean(center * center, -1, keepdims=True) + EPSILON)
    return center * rstd, rstd


def norm_back(err, gain, hat, rstd):
    scaled = err * gain
    return rstd * (
        scaled
        - jnp.mean(scaled, -1, keepdims=True)
        - hat * jnp.mean(scaled * hat, -1, keepdims=True)
    )


def qkv_body(pos, *refs):
    tok, small, own, oth = refs[0:4], refs[4:8], refs[8:12], refs[12:16]
    q_ref, kv_ref, normed_ref, vec_ref, w_ref, sm = refs[16:]
    s, k, c = pos[0], pos[1], pos[2]
    for m in range(4):
        z = s ^ m
        w_ref[pl.ds(pl.multiple_of(z * QUARTER + c * HALF, 32), HALF), :] = own[m][...]
        w_ref[pl.ds(pl.multiple_of(z * QUARTER + (1 - c) * HALF, 32), HALF), :] = oth[m][...]
        sm[z] = small[m][...].astype(f32)

    def vec(n):
        return jnp.concatenate([sm[z, n : n + 1, :QUARTER] for z in range(4)], 1)

    gain, shift = vec(0), vec(1)
    own_small = sm[k]
    bias = jnp.concatenate(
        [own_small[2:3, :QUARTER], jnp.zeros((1, QUARTER), f32), own_small[3:4, :QUARTER]], 1
    )
    vec_ref[...] = jnp.concatenate(
        [gain, shift, vec(4), vec(5), vec(6), vec(7), vec(8), jnp.zeros((1, WIDTH), f32)], 0
    )
    for r in range(4):
        hat, _ = normal(tok[r][:ROWS, :].astype(f32))
        normed_ref[ROWS * r : ROWS * (r + 1), :] = (hat * gain + shift).astype(bf16)
    projected = dot(normed_ref[...], w_ref[...]) + bias
    q_ref[...] = (projected[:, :QUARTER].astype(bf16).astype(f32) * 0.125).astype(bf16)
    kv_ref[:OWN, :] = projected[:, QUARTER:].astype(bf16)
    ids = [tok[r][ROWS : ROWS + 8, :ROWS].astype(f32)[:1] for r in range(4)]
    ids = jnp.concatenate(ids + [jnp.zeros((4, ROWS), f32)], 0).astype(bf16)
    kv_ref[OWN:, :] = jnp.concatenate([ids, jnp.zeros((8, 2 * QUARTER - ROWS), bf16)], 1)


def split_ids(kva, kvb):
    ids_a = kva[OWN:, :ROWS].astype(f32)
    ids_b = kvb[OWN:, :ROWS].astype(f32)
    keys = jnp.concatenate(
        [ids_a[r : r + 1] for r in range(4)] + [ids_b[r : r + 1] for r in range(4)], 1
    )
    return ids_a.T, keys


def attend_body(pos, q_ref, kva, kvb, mixed_ref, state_ref):
    cols, keys = split_ids(kva, kvb)
    lane = lax.broadcasted_iota(jnp.int32, (ROWS, 64), 1)
    for r in range(4):
        rows = slice(ROWS * r, ROWS * (r + 1))
        hidden = keys > cols[:, r : r + 1]
        heads, lse = [], jnp.zeros((ROWS, 64), f32)
        for h in range(3):
            at = slice(64 * h, 64 * h + 64)
            at_v = slice(QUARTER + 64 * h, QUARTER + 64 * h + 64)
            query = q_ref[rows, at]
            scores = jnp.concatenate(
                [dot_t(query, kva[:OWN, at]), dot_t(query, kvb[:OWN, at])], 1
            )
            scores = jnp.where(hidden, NEGATIVE, scores)
            top = jnp.max(scores, -1, keepdims=True)
            weights = jnp.exp(scores - top)
            total = jnp.sum(weights, -1, keepdims=True)
            low = weights.astype(bf16)
            out = dot(low[:, :OWN], kva[:OWN, at_v]) + dot(low[:, OWN:], kvb[:OWN, at_v])
            heads.append(out * (1.0 / total))
            lse = jnp.where(lane == h, top + jnp.log(total), lse)
        mixed = jnp.concatenate(heads, 1)
        mixed_ref[rows, :] = mixed.astype(bf16)
        state_ref[rows, :] = jnp.concatenate([mixed, lse], 1)


def feed_body(pos, *refs):
    tok, mixed, own, oth, cot = refs[0:4], refs[4:8], refs[8:12], refs[12:16], refs[16:20]
    vec_ref = refs[20]
    mid_ref, n2_ref, act_ref, pre_ref, d0, d1, d2, d3, g0, g1, g2, g3, sums_ref, wok_ref = refs[21:35]
    wo, wu, wd, hat_ref = refs[35:]
    s, k, c = pos[0], pos[1], pos[2]
    for m in range(4):
        z = s ^ m
        for half, src in ((c, own[m]), (1 - c, oth[m])):
            at = pl.ds(pl.multiple_of(z * QUARTER + half * HALF, 32), HALF)
            wo[at, :] = src[:HALF, :]
            wu[at, :] = src[HALF : 2 * HALF, :]
            wd[at, :] = src[2 * HALF :, :]
    wok_ref[...] = wo[pl.ds(pl.multiple_of(k * QUARTER, 64), QUARTER), :]
    bias_out, gain, shift = vec_ref[2:3, :], vec_ref[3:4, :], vec_ref[4:5, :]
    bias_up = vec_ref[6:7, :]
    attended = bias_out
    for m in range(4):
        block = jnp.concatenate(
            [mixed[m][ROWS * (r ^ m) : ROWS * (r ^ m) + ROWS, :] for r in range(4)], 0
        )
        at = pl.ds(pl.multiple_of((k ^ m) * QUARTER, 64), QUARTER)
        attended = attended + dot(block, wo[at, :])
    for r in range(4):
        rows = slice(ROWS * r, ROWS * (r + 1))
        middle = tok[r][:ROWS, :].astype(f32) + attended[rows]
        if r == 0:
            mid_ref[...] = middle
        hat, _ = normal(middle)
        hat_ref[rows, :] = hat
        n2_ref[rows, :] = (hat * gain + shift).astype(bf16)
    pre_act = dot(n2_ref[...], wu[...]) + bias_up
    cdf = 0.5 * (1.0 + lax.erf(pre_act * (1.0 / math.sqrt(2.0))))
    act_ref[...] = (pre_act * cdf).astype(bf16)
    slope = cdf + pre_act * jnp.exp(-0.5 * pre_act * pre_act) * (1.0 / math.sqrt(2.0 * math.pi))
    grads = jnp.concatenate([ref[...] for ref in cot], 0)
    pre = (dot_t(grads, wd[...]) * slope).astype(bf16)
    pre_ref[...] = pre
    back = dot_t(pre, wu[...])
    sums = [
        jnp.sum(back * hat_ref[...], 0, keepdims=True),
        jnp.sum(back, 0, keepdims=True),
        jnp.sum(pre.astype(f32), 0, keepdims=True),
    ]
    sums_ref[...] = jnp.concatenate(sums + [jnp.zeros((5, WIDTH), f32)], 0)
    g0[...] = back[:ROWS]
    for r, ref in ((1, g1), (2, g2), (3, g3)):
        ref[...] = back[ROWS * r : ROWS * (r + 1)].astype(bf16)
    down = dot(act_ref[...], wd[...])
    d0[...] = down[:ROWS]
    for r, ref in ((1, d1), (2, d2), (3, d3)):
        ref[...] = down[ROWS * r : ROWS * (r + 1)].astype(bf16)


def feed_grad_body(pos, act_ref, n2_ref, pre_ref, c0, c1, c2, c3, send_ref, own_ref, wg):
    s, c = pos[0], pos[2]
    grads = jnp.concatenate([ref[...] for ref in (c0, c1, c2, c3)], 0)
    for part in range(2):
        if part == 0:
            wg[...] = t_dot(act_ref[...], grads)
        else:
            wg[...] = t_dot(n2_ref[...], pre_ref[...])
        rows = slice(HALF * part, HALF * part + HALF)
        for m in range(4):
            z = s ^ m
            at = pl.ds(pl.multiple_of(z * QUARTER + c * HALF, 32), HALF)
            own_ref[m, rows, :] = wg[at, :]
            at = pl.ds(pl.multiple_of(z * QUARTER + (1 - c) * HALF, 32), HALF)
            send_ref[m, rows, :] = wg[at, :].astype(bf16)


def halves_body(pos, own_ref, got_ref, o0, o1, o2, o3):
    rows = got_ref.shape[1]
    for m, out in enumerate((o0, o1, o2, o3)):
        out[:rows, :] = (own_ref[m, :rows, :] + got_ref[m].astype(f32)).astype(out.dtype)
        if own_ref.shape[1] > rows:
            out[rows:, :] = own_ref[m, rows:, :].astype(out.dtype)


def add_body(pos, o0, r1, r2, r3, out):
    total = o0[...] + r1[...].astype(f32) + r2[...].astype(f32) + r3[...].astype(f32)
    out[...] = total.astype(out.dtype)


def middle_body(pos, g0, r1, r2, r3, mid_ref, cot_ref, vec_ref, gm_ref, ga_ref):
    err = g0[...] + r1[...].astype(f32) + r2[...].astype(f32) + r3[...].astype(f32)
    hat, rstd = normal(mid_ref[...])
    grad = cot_ref[...].astype(f32) + norm_back(err, vec_ref[3:4, :], hat, rstd)
    gm_ref[...] = grad
    ga_ref[...] = grad.astype(bf16)


def attend_grad_body(pos, a0, a1, a2, a3, wok, q_ref, kva, kvb, state_ref, *outs):
    dq_ref, own_ref, send_ref, p_ref, ds_ref = outs
    cols, keys = split_ids(kva, kvb)
    grads = jnp.concatenate([ref[...] for ref in (a0, a1, a2, a3)], 0)
    grad_mixed = dot_t(grads, wok[...]).astype(bf16)
    dq = []
    for h in range(3):
        at = slice(64 * h, 64 * h + 64)
        at_v = slice(QUARTER + 64 * h, QUARTER + 64 * h + 64)
        query, grad = q_ref[:, at], grad_mixed[:, at]
        grad_q = []
        for r in range(4):
            rows = slice(ROWS * r, ROWS * (r + 1))
            hidden = keys > cols[:, r : r + 1]
            g = grad[rows]
            inner = jnp.sum(g.astype(f32) * state_ref[rows, at], -1, keepdims=True)
            lse = state_ref[rows, QUARTER + h : QUARTER + h + 1]
            scores = jnp.concatenate(
                [dot_t(query[rows], kva[:OWN, at]), dot_t(query[rows], kvb[:OWN, at])], 1
            )
            probs = jnp.exp(jnp.where(hidden, NEGATIVE, scores) - lse)
            slopes = jnp.concatenate([dot_t(g, kva[:OWN, at_v]), dot_t(g, kvb[:OWN, at_v])], 1)
            ds = (probs * (slopes - inner)).astype(bf16)
            p_ref[rows, :] = probs.astype(bf16)
            ds_ref[rows, :] = ds
            grad_q.append(dot(ds[:, :OWN], kva[:OWN, at]) + dot(ds[:, OWN:], kvb[:OWN, at]))
        dq.append(jnp.concatenate(grad_q, 0))
        dk = t_dot(ds_ref[...], query)
        dv = t_dot(p_ref[...], grad)
        own_ref[:, at] = dk[:OWN]
        own_ref[:, at_v] = dv[:OWN]
        send_ref[:, at] = dk[OWN:].astype(bf16)
        send_ref[:, at_v] = dv[OWN:].astype(bf16)
    dq_ref[...] = (jnp.concatenate(dq, 1) * 0.125).astype(bf16)


def project_grad_body(pos, *refs):
    tok, mixed, ga = refs[0:4], refs[4:8], refs[8:12]
    normed, dq, kv_own, kv_got, w_ref, vec_ref, sums_ref, cot_ref = refs[12:20]
    send_ref, own_ref, g0, g1, g2, g3, wg, sm, gk, gp = refs[20:]
    s, k, c = pos[0], pos[1], pos[2]
    gp[:, :QUARTER] = dq[...]
    gp[:, QUARTER:] = (kv_own[...] + kv_got[...].astype(f32)).astype(bf16)
    wg[:, : 3 * QUARTER] = t_dot(normed[...], gp[...])
    for q in range(4):

        @pl.when(k == q)
        def _():
            for r in range(4):
                gk[ROWS * r : ROWS * (r + 1), :] = ga[r][:, QUARTER * q : QUARTER * (q + 1)]

    for m in range(4):
        block = jnp.concatenate(
            [mixed[m][ROWS * (r ^ m) : ROWS * (r ^ m) + ROWS, :] for r in range(4)], 0
        )
        at = pl.ds(pl.multiple_of((k ^ m) * QUARTER, 64), QUARTER)
        wg[at, 3 * QUARTER :] = t_dot(block, gk[...])
    back = dot_t(gp[...], w_ref[...])
    hat = jnp.concatenate([normal(tok[r][:ROWS, :].astype(f32))[0] for r in range(4)], 0)
    ln1_gain = jnp.sum(back * hat, 0, keepdims=True)
    ln1_bias = jnp.sum(back, 0, keepdims=True)
    g0[...] = back[:ROWS]
    for r, ref in ((1, g1), (2, g2), (3, g3)):
        ref[...] = back[ROWS * r : ROWS * (r + 1)].astype(bf16)
    gp_sums = jnp.sum(gp[...].astype(f32), 0, keepdims=True)
    out_bias = jnp.sum(ga[0][...].astype(f32), 0, keepdims=True)
    down_bias = jnp.sum(cot_ref[...].astype(f32), 0, keepdims=True)
    for z in range(4):
        at = slice(QUARTER * z, QUARTER * (z + 1))
        here = jnp.where(k == z, 1.0, 0.0).astype(f32)
        row0 = [ln1_gain[:, at], ln1_bias[:, at], gp_sums[:, :QUARTER] * here]
        row0 = jnp.concatenate(row0 + [gp_sums[:, 2 * QUARTER :] * here], 1)
        row1 = [out_bias[:, at], sums_ref[0:1, at], sums_ref[1:2, at], down_bias[:, at]]
        row1 = jnp.concatenate(row1, 1)
        row2 = jnp.concatenate([sums_ref[2:3, at], jnp.zeros((1, 3 * QUARTER), f32)], 1)
        sm[z] = jnp.concatenate([row0, row1, row2, jnp.zeros((5, WIDTH), f32)], 0)
    for m in range(4):
        z = s ^ m
        at = pl.ds(pl.multiple_of(z * QUARTER + c * HALF, 32), HALF)
        own_ref[m, :HALF, :] = wg[at, :]
        own_ref[m, HALF:, :] = sm[z]
        at = pl.ds(pl.multiple_of(z * QUARTER + (1 - c) * HALF, 32), HALF)
        send_ref[m] = wg[at, :].astype(bf16)


def input_body(pos, g0, r1, r2, r3, tok_ref, gm_ref, vec_ref, out_ref):
    err = g0[...] + r1[...].astype(f32) + r2[...].astype(f32) + r3[...].astype(f32)
    hat, rstd = normal(tok_ref[:ROWS, :].astype(f32))
    out_ref[0] = gm_ref[...] + norm_back(err, vec_ref[0:1, :], hat, rstd)


def output_body(pos, d0, r1, r2, r3, mid_ref, vec_ref, out_ref):
    total = d0[...] + r1[...].astype(f32) + r2[...].astype(f32) + r3[...].astype(f32)
    out_ref[0] = (mid_ref[...] + total + vec_ref[5:6, :]).astype(bf16)


def feed_join_body(pos, *refs):
    own, oth = refs[0:4], refs[4:8]
    down_ref, up_ref, sc = refs[8:]
    k, c = pos[1], pos[2]
    for m in range(4):
        sc[c, k ^ m] = own[m][...]
        sc[1 - c, k ^ m] = oth[m][...]
    for q in range(4):
        for half in range(2):
            at = QUARTER * q + HALF * half
            down_ref[at : at + HALF, :] = sc[half, q, :HALF, :].astype(f32)
            rows = slice(HALF * half, HALF * half + HALF)
            for p in range(4):
                cols = slice(WIDTH * p + QUARTER * q, WIDTH * p + QUARTER * (q + 1))
                piece = sc[half, q, HALF:, QUARTER * p : QUARTER * (p + 1)]
                up_ref[rows, cols] = piece.astype(f32)


def last_join_body(pos, *refs):
    own, oth = refs[0:4], refs[4:8]
    qkv_ref, out_ref, vec_ref, up_ref, sc = refs[8:]
    k, c = pos[1], pos[2]
    for m in range(4):
        sc[c, k ^ m] = own[m][...]
        sc[1 - c, k ^ m] = oth[m][...]
    total = jnp.zeros((8, WIDTH), f32)
    ups = []
    for q in range(4):
        small = sc[0, q, HALF:, :].astype(f32) + sc[1, q, HALF:, :].astype(f32)
        total = total + small
        ups.append(small[2:3, :QUARTER])
        for half in range(2):
            rows = slice(HALF * half, HALF * half + HALF)
            for p in range(3):
                cols = slice(WIDTH * p + QUARTER * q, WIDTH * p + QUARTER * (q + 1))
                piece = sc[half, q, :HALF, QUARTER * p : QUARTER * (p + 1)]
                qkv_ref[rows, cols] = piece.astype(f32)
            out_ref[rows, QUARTER * q : QUARTER * (q + 1)] = sc[
                half, q, :HALF, 3 * QUARTER :
            ].astype(f32)
    vecs = [total[n // 4 : n // 4 + 1, QUARTER * (n % 4) : QUARTER * (n % 4 + 1)] for n in range(8)]
    vec_ref[...] = jnp.concatenate(vecs, 0)
    up_ref[...] = jnp.concatenate(ups, 1)


def shards(
    tokens,
    block_ids,
    ln1_gain,
    ln1_bias,
    w_qkv,
    q_bias,
    v_bias,
    w_out,
    out_bias,
    ln2_gain,
    ln2_bias,
    w_up,
    up_bias,
    w_down,
    down_bias,
    cotangent,
):
    seq = lax.axis_index("seq")
    ctx = lax.axis_index("ctx")
    k, core = ctx // 2, ctx % 2
    pos = jnp.stack([seq, k, core]).astype(jnp.int32)

    def rows_of_core(values):
        return lax.dynamic_slice_in_dim(values, HALF * core, HALF, 0)

    got_qkv = seq_gather(column_slice(rows_of_core(w_qkv), k, 3))
    ids_row = jnp.pad(block_ids.astype(bf16), ((0, 7), (0, WIDTH - ROWS)))
    tok = chip_gather(jnp.concatenate([tokens[0], ids_row], 0))
    small = [ln1_gain, ln1_bias, q_bias, v_bias, out_bias, ln2_gain, ln2_bias, down_bias]
    small = small + [lax.dynamic_slice_in_dim(up_bias, QUARTER * k, QUARTER, 0)]
    small = [jnp.pad(v, (0, 256 - QUARTER)) for v in small] + [jnp.zeros((7 * 256,), bf16)]
    got_small = seq_gather(jnp.concatenate(small).reshape(16, 256))
    oth_qkv = [core_swap(block) for block in got_qkv]
    rest = jnp.concatenate(
        [
            rows_of_core(w_out),
            column_slice(rows_of_core(w_up), k, 4),
            lax.dynamic_slice_in_dim(w_down, QUARTER * k + HALF * core, HALF, 0),
        ],
        0,
    )
    got_rest = seq_gather(after(rest, *got_qkv, *got_small))
    cot = chip_gather(after(cotangent[0], *tok))

    query, pair, normed, vec, weight_qkv = run(
        qkv_body,
        pos,
        [*tok, *got_small, *got_qkv, *oth_qkv],
        [
            ((OWN, QUARTER), bf16),
            ((OWN + 8, 2 * QUARTER), bf16),
            ((OWN, WIDTH), bf16),
            ((8, WIDTH), f32),
            ((WIDTH, 3 * QUARTER), bf16),
        ],
        [((4, 16, 256), f32)],
    )
    pair_oth = core_swap(pair)
    mixed_own, state = run(
        attend_body,
        pos,
        [query, pair, pair_oth],
        [((OWN, QUARTER), bf16), ((OWN, 256), f32)],
        us=6.0,
    )
    mixed = chip_gather(mixed_own)
    got_rest = lax.optimization_barrier((*got_rest, mixed_own))[:4]
    oth_rest = [core_swap(block) for block in got_rest]
    big, block = (OWN, WIDTH), (ROWS, WIDTH)
    mid, normed_two, act, pre, d0, d1, d2, d3, g0, g1, g2, g3, sums, w_out_k = run(
        feed_body,
        pos,
        [*tok, *mixed, *got_rest, *oth_rest, *cot, vec],
        [(block, f32), (big, bf16), (big, bf16), (big, bf16)]
        + [(block, f32), (block, bf16), (block, bf16), (block, bf16)] * 2
        + [((8, WIDTH), f32), ((QUARTER, WIDTH), bf16)],
        [((WIDTH, WIDTH), bf16)] * 3 + [(big, f32)],
        us=8.0,
    )
    got_g = [chip_swap(g, m) for m, g in ((1, g1), (2, g2), (3, g3))]
    feed_send, feed_own = run(
        feed_grad_body,
        pos,
        [act, normed_two, pre, *cot],
        [((4, QUARTER, WIDTH), bf16), ((4, QUARTER, WIDTH), f32)],
        [((WIDTH, WIDTH), f32)],
        us=4.0,
    )
    feed_got = core_swap(feed_send)
    grad_mid, grad_att = run(
        middle_body, pos, [g0, *got_g, mid, cot[0], vec], [(block, f32), (block, bf16)]
    )
    piece = (QUARTER, WIDTH)
    h0, h1, h2, h3 = run(
        halves_body, pos, [feed_own, feed_got], [(piece, f32)] + [(piece, bf16)] * 3
    )
    ga = chip_gather(grad_att)
    feed_terms = [seq_swap(h, m) for m, h in ((1, h1), (2, h2), (3, h3))]
    *ga, h0 = lax.optimization_barrier((*ga, h0))
    got_d = [chip_swap(after(d, ga[1]), m) for m, d in ((1, d1), (2, d2), (3, d3))]
    dq, kv_own, kv_send = run(
        attend_grad_body,
        pos,
        [*ga, w_out_k, query, pair, pair_oth, state],
        [((OWN, QUARTER), bf16), ((OWN, 2 * QUARTER), f32), ((OWN, 2 * QUARTER), bf16)],
        [((OWN, 2 * OWN), bf16)] * 2,
        us=8.0,
    )
    kv_send, *feed_terms = lax.optimization_barrier((kv_send, *feed_terms))
    kv_got = core_swap(kv_send)
    (feed_sum,) = run(add_body, pos, [h0, *feed_terms], [(piece, bf16)])
    feed_blocks = chip_gather(feed_sum)
    last_send, last_own, e0, e1, e2, e3 = run(
        project_grad_body,
        pos,
        [*tok, *mixed, *ga, normed, dq, kv_own, kv_got, weight_qkv, vec, sums, cot[0]],
        [((4, HALF, WIDTH), bf16), ((4, HALF + 8, WIDTH), f32)]
        + [(block, f32), (block, bf16), (block, bf16), (block, bf16)],
        [((WIDTH, WIDTH), f32), ((4, 8, WIDTH), f32), ((OWN, QUARTER), bf16), ((OWN, 3 * QUARTER), bf16)],
        us=6.0,
    )
    last_got = core_swap(last_send)
    lpiece = (HALF + 8, WIDTH)
    l0, l1, l2, l3 = run(
        halves_body, pos, [last_own, last_got], [(lpiece, f32)] + [(lpiece, bf16)] * 3
    )
    last_terms = [seq_swap(h, m) for m, h in ((1, l1), (2, l2), (3, l3))]
    got_e = [chip_swap(e, m) for m, e in ((1, e1), (2, e2), (3, e3))]
    feed_oth = [core_swap(b) for b in feed_blocks]
    grad_w_down, grad_w_up = run(
        feed_join_body,
        pos,
        [*feed_blocks, *feed_oth],
        [((WIDTH, WIDTH), f32), ((QUARTER, 4 * WIDTH), f32)],
        [((2, 4, QUARTER, WIDTH), bf16)],
        us=4.0,
    )
    (result,) = run(output_body, pos, [d0, *got_d, mid, vec], [((1, *block), bf16)])
    (input_grad,) = run(
        input_body, pos, [e0, *got_e, tok[0], grad_mid, vec], [((1, *block), f32)]
    )
    (last_sum,) = run(add_body, pos, [l0, *last_terms], [(lpiece, bf16)])
    last_blocks = chip_gather(last_sum)
    last_oth = [core_swap(b) for b in last_blocks]
    grad_w_qkv, grad_w_out, g, g_up = run(
        last_join_body,
        pos,
        [*last_blocks, *last_oth],
        [
            ((QUARTER, 3 * WIDTH), f32),
            ((QUARTER, WIDTH), f32),
            ((8, QUARTER), f32),
            ((1, WIDTH), f32),
        ],
        [((2, 4, HALF + 8, WIDTH), bf16)],
        us=3.0,
    )
    return (
        result,
        input_grad,
        g[0],
        g[1],
        grad_w_qkv,
        g[2],
        g[3],
        grad_w_out,
        g[4],
        g[5],
        g[6],
        grad_w_up,
        g_up[0],
        grad_w_down,
        g[7],
    )


def solution(mesh):
    placed = (
        P("seq", "ctx", None),
        P("seq", "ctx"),
        P("seq"),
        P("seq"),
        P("seq", None),
        P("seq"),
        P("seq"),
        P("seq", None),
        P("seq"),
        P("seq"),
        P("seq"),
        P("seq", None),
        P("seq"),
        P("seq", None),
        P("seq"),
        P("seq", "ctx", None),
    )
    return jax.shard_map(
        shards if mesh.shape["ctx"] == 8 and mesh.shape["seq"] == 4 else shards_general,
        mesh=mesh,
        in_specs=placed,
        out_specs=(
            P("seq", "ctx", None),
            P("seq", "ctx", None),
            P("seq"),
            P("seq"),
            P("seq", None),
            P("seq"),
            P("seq"),
            P("seq", None),
            P("seq"),
            P("seq"),
            P("seq"),
            P("seq", None),
            P("seq"),
            P("seq", None),
            P("seq"),
        ),
        check_vma=False,
    )
```

```python
import math

import jax
import jax.numpy as jnp
from jax import lax
from jax.experimental import pallas as pl
from jax.experimental.pallas import tpu as pltpu
from jax.sharding import PartitionSpec as P

HEADS = 12


EPSILON = 1e-06
NEGATIVE = -1e30


def layer_norm(values, gain, shift):
    center = values - jnp.mean(values, -1, keepdims=True)
    spread = jnp.mean(center * center, -1, keepdims=True)
    return center * lax.rsqrt(spread + EPSILON) * gain + shift


def block_rows(count):
    return math.gcd(count, 512)


def masked_scores(query_heads, key_heads, query_ids, key_ids, scale):
    raw = (
        jnp.einsum("qhd,khd->hqk", query_heads, key_heads, preferred_element_type=jnp.float32)
        * scale
    )
    allowed = key_ids[None, None, :] <= query_ids[None, :, None]
    return (raw, allowed)


def attend_forward(query_heads, query_ids, keys_all, values_all, ids_all, scale):
    tok_rows, heads, head_dim = query_heads.shape
    total_keys = keys_all.shape[0]
    step = block_rows(total_keys)
    blocks = total_keys // step

    def attend_visit(carry, inputs):
        running, total, accum = carry
        key_block, value_block, id_block = inputs
        raw, allowed = masked_scores(query_heads, key_block, query_ids, id_block, scale)
        masked = jnp.where(allowed, raw, NEGATIVE)
        new_top = jnp.maximum(running, jnp.max(masked, -1))
        weights = jnp.where(allowed, jnp.exp(masked - new_top[..., None]), 0.0)
        factor = jnp.exp(running - new_top)
        total = total * factor + jnp.sum(weights, -1)
        accum = accum * factor[..., None] + jnp.einsum(
            "hqk,khd->hqd",
            weights.astype(jnp.bfloat16),
            value_block,
            preferred_element_type=jnp.float32,
        )
        return ((new_top, total, accum), None)

    start_state = (
        jnp.full((heads, tok_rows), NEGATIVE, jnp.float32),
        jnp.zeros((heads, tok_rows), jnp.float32),
        jnp.zeros((heads, tok_rows, head_dim), jnp.float32),
    )
    (running, total, accum), _ = lax.scan(
        attend_visit,
        start_state,
        (
            keys_all.reshape(blocks, step, heads, head_dim),
            values_all.reshape(blocks, step, heads, head_dim),
            ids_all.reshape(blocks, step),
        ),
    )
    output_heads = jnp.transpose(accum / total[..., None], (1, 0, 2))
    return (output_heads, running + jnp.log(total))


def query_gradient(
    query_heads, grad_heads, query_ids, keys_all, values_all, ids_all, logsum, inner, scale
):
    tok_rows, heads, head_dim = query_heads.shape
    total_keys = keys_all.shape[0]
    step = block_rows(total_keys)
    blocks = total_keys // step

    def query_visit(accum, inputs):
        key_block, value_block, id_block = inputs
        raw, allowed = masked_scores(query_heads, key_block, query_ids, id_block, scale)
        probs = jnp.where(allowed, jnp.exp(raw - logsum[..., None]), 0.0)
        grad_probs = jnp.einsum(
            "qhd,khd->hqk", grad_heads, value_block, preferred_element_type=jnp.float32
        )
        grad_scores = (probs * (grad_probs - inner[..., None])).astype(jnp.bfloat16)
        accum = accum + jnp.einsum(
            "hqk,khd->qhd", grad_scores, key_block, preferred_element_type=jnp.float32
        )
        return (accum, None)

    accum, _ = lax.scan(
        query_visit,
        jnp.zeros((tok_rows, heads, head_dim), jnp.float32),
        (
            keys_all.reshape(blocks, step, heads, head_dim),
            values_all.reshape(blocks, step, heads, head_dim),
            ids_all.reshape(blocks, step),
        ),
    )
    return accum * scale


def pair_grads(
    query_heads, grad_heads, query_ids, logsum, inner, key_heads, value_heads, key_ids, scale
):
    raw, allowed = masked_scores(query_heads, key_heads, query_ids, key_ids, scale)
    probs = jnp.where(allowed, jnp.exp(raw - logsum[..., None]), 0.0)
    grad_probs = jnp.einsum(
        "qhd,khd->hqk", grad_heads, value_heads, preferred_element_type=jnp.float32
    )
    grad_scores = (probs * (grad_probs - inner[..., None])).astype(jnp.bfloat16)
    grad_keys = (
        jnp.einsum("hqk,qhd->khd", grad_scores, query_heads, preferred_element_type=jnp.float32)
        * scale
    )
    grad_values = jnp.einsum(
        "hqk,qhd->khd", probs.astype(jnp.bfloat16), grad_heads, preferred_element_type=jnp.float32
    )
    return (grad_keys, grad_values)


def shards_general(
    tokens,
    block_ids,
    ln1_gain,
    ln1_bias,
    w_qkv,
    q_bias,
    v_bias,
    w_out,
    out_bias,
    ln2_gain,
    ln2_bias,
    w_up,
    up_bias,
    w_down,
    down_bias,
    cotangent,
):
    gathered = (
        lax.all_gather(ln1_gain, "seq", axis=0, tiled=True),
        lax.all_gather(ln1_bias, "seq", axis=0, tiled=True),
        lax.all_gather(w_qkv, "seq", axis=0, tiled=True),
        lax.all_gather(q_bias, "seq", axis=0, tiled=True),
        lax.all_gather(v_bias, "seq", axis=0, tiled=True),
        lax.all_gather(w_out, "seq", axis=0, tiled=True),
        lax.all_gather(out_bias, "seq", axis=0, tiled=True),
        lax.all_gather(ln2_gain, "seq", axis=0, tiled=True),
        lax.all_gather(ln2_bias, "seq", axis=0, tiled=True),
        lax.all_gather(w_up, "seq", axis=0, tiled=True),
        lax.all_gather(up_bias, "seq", axis=0, tiled=True),
        lax.all_gather(w_down, "seq", axis=0, tiled=True),
        lax.all_gather(down_bias, "seq", axis=0, tiled=True),
    )
    attention_part = gathered[:7]
    feed_part = gathered[7:]
    gain_one, shift_one, weight_qkv, bias_query, bias_value, weight_out, bias_out = attention_part
    width = weight_out.shape[0]
    heads = HEADS
    head_dim = width // heads
    scale = 1.0 / math.sqrt(head_dim)
    inputs = tokens[0].astype(jnp.float32)
    tok_rows = inputs.shape[0]
    own_ids = block_ids[0]
    gain_one_f = gain_one.astype(jnp.float32)
    shift_one_f = shift_one.astype(jnp.float32)
    normed_one, norm_one_pull = jax.vjp(layer_norm, inputs, gain_one_f, shift_one_f)
    normed_low = normed_one.astype(jnp.bfloat16)
    qkv_bias = jnp.concatenate(
        [
            bias_query.astype(jnp.float32),
            jnp.zeros((width,), jnp.float32),
            bias_value.astype(jnp.float32),
        ]
    )
    projected = (
        jnp.dot(normed_low, weight_qkv, preferred_element_type=jnp.float32) + qkv_bias
    ).astype(jnp.bfloat16)
    query_low = projected[:, :width]
    key_low = projected[:, width : 2 * width]
    value_low = projected[:, 2 * width :]
    ids_all = lax.all_gather(block_ids, "ctx", axis=1, tiled=True)[0]
    keys_all, values_all = (
        lax.all_gather(key_low, "ctx", axis=0, tiled=True),
        lax.all_gather(value_low, "ctx", axis=0, tiled=True),
    )
    query_heads = query_low.reshape(tok_rows, heads, head_dim)
    output_heads, logsum = attend_forward(
        query_heads, own_ids, keys_all, values_all, ids_all, scale
    )
    mixed_low = output_heads.reshape(tok_rows, width).astype(jnp.bfloat16)
    attended = jnp.dot(mixed_low, weight_out, preferred_element_type=jnp.float32) + bias_out.astype(
        jnp.float32
    )
    middle = inputs + attended
    gain_two, shift_two, weight_up, bias_up, weight_down, bias_down = feed_part
    gain_two_f = gain_two.astype(jnp.float32)
    shift_two_f = shift_two.astype(jnp.float32)
    normed_two, norm_two_pull = jax.vjp(layer_norm, middle, gain_two_f, shift_two_f)
    normed_two_low = normed_two.astype(jnp.bfloat16)
    pre_act = jnp.dot(
        normed_two_low, weight_up, preferred_element_type=jnp.float32
    ) + bias_up.astype(jnp.float32)
    activated, gelu_pull = jax.vjp(lambda values: jax.nn.gelu(values, approximate=False), pre_act)
    activated_low = activated.astype(jnp.bfloat16)
    result = (
        middle
        + jnp.dot(activated_low, weight_down, preferred_element_type=jnp.float32)
        + bias_down.astype(jnp.float32)
    )
    grad_out = cotangent[0]
    grad_out_f = grad_out.astype(jnp.float32)
    grad_weight_down = jnp.einsum(
        "tf,td->fd", activated_low, grad_out, preferred_element_type=jnp.float32
    )
    grad_bias_down = jnp.sum(grad_out_f, 0)
    grad_hidden = jnp.einsum("td,fd->tf", grad_out, weight_down, preferred_element_type=jnp.float32)
    grad_pre_low = gelu_pull(grad_hidden)[0].astype(jnp.bfloat16)
    grad_weight_up = jnp.einsum(
        "td,tf->df", normed_two_low, grad_pre_low, preferred_element_type=jnp.float32
    )
    grad_bias_up = jnp.sum(grad_pre_low.astype(jnp.float32), 0)
    grad_normed_two = jnp.einsum(
        "tf,df->td", grad_pre_low, weight_up, preferred_element_type=jnp.float32
    )
    grad_middle_part, grad_gain_two, grad_shift_two = norm_two_pull(grad_normed_two)
    grad_middle = grad_out_f + grad_middle_part
    grad_attended = grad_middle.astype(jnp.bfloat16)
    grad_weight_out = jnp.einsum(
        "td,te->de", mixed_low, grad_attended, preferred_element_type=jnp.float32
    )
    grad_bias_out = jnp.sum(grad_attended.astype(jnp.float32), 0)
    grad_mixed = jnp.einsum(
        "te,de->td", grad_attended, weight_out, preferred_element_type=jnp.float32
    ).astype(jnp.bfloat16)
    grad_heads = grad_mixed.reshape(tok_rows, heads, head_dim)
    inner = jnp.einsum("thd,thd->ht", grad_heads.astype(jnp.float32), output_heads)
    grad_query = query_gradient(
        query_heads, grad_heads, own_ids, keys_all, values_all, ids_all, logsum, inner, scale
    )
    step = block_rows(lax.axis_size("ctx") * tok_rows)
    blocks = lax.axis_size("ctx") * tok_rows // step
    key_part = keys_all.reshape(blocks, step, heads, head_dim)
    value_part = values_all.reshape(blocks, step, heads, head_dim)
    id_part = ids_all.reshape(blocks, step)

    def key_visit(carry, inputs):
        grad_keys, grad_values = pair_grads(
            query_heads, grad_heads, own_ids, logsum, inner, inputs[0], inputs[1], inputs[2], scale
        )
        joined = jnp.concatenate(
            [grad_keys.reshape(step, width), grad_values.reshape(step, width)], 1
        )
        return (carry, joined)

    _, terms = lax.scan(key_visit, jnp.zeros((), jnp.float32), (key_part, value_part, id_part))
    key_value_grads = lax.psum_scatter(
        terms.reshape(lax.axis_size("ctx") * tok_rows, 2 * width),
        "ctx",
        scatter_dimension=0,
        tiled=True,
    )
    grad_keys_all = key_value_grads[:, :width]
    grad_values_all = key_value_grads[:, width:]
    grad_query_low = grad_query.reshape(tok_rows, width).astype(jnp.bfloat16)
    grad_value_low = grad_values_all.astype(jnp.bfloat16)
    grad_projected = jnp.concatenate(
        [grad_query_low, grad_keys_all.astype(jnp.bfloat16), grad_value_low], 1
    )
    grad_weight_qkv = jnp.einsum(
        "td,te->de", normed_low, grad_projected, preferred_element_type=jnp.float32
    )
    grad_bias_query = jnp.sum(grad_query_low.astype(jnp.float32), 0)
    grad_bias_value = jnp.sum(grad_value_low.astype(jnp.float32), 0)
    grad_normed_one = jnp.einsum(
        "te,de->td", grad_projected, weight_qkv, preferred_element_type=jnp.float32
    )
    grad_input_part, grad_gain_one, grad_shift_one = norm_one_pull(grad_normed_one)
    input_grad = grad_middle + grad_input_part
    local_grads = (
        grad_gain_one,
        grad_shift_one,
        grad_weight_qkv,
        grad_bias_query,
        grad_bias_value,
        grad_weight_out,
        grad_bias_out,
        grad_gain_two,
        grad_shift_two,
        grad_weight_up,
        grad_bias_up,
        grad_weight_down,
        grad_bias_down,
    )
    shares = (
        lax.psum_scatter(
            local_grads[0].astype(jnp.bfloat16), "seq", scatter_dimension=0, tiled=True
        ).astype(jnp.float32),
        lax.psum_scatter(
            local_grads[1].astype(jnp.bfloat16), "seq", scatter_dimension=0, tiled=True
        ).astype(jnp.float32),
        lax.psum_scatter(
            local_grads[2].astype(jnp.bfloat16), "seq", scatter_dimension=0, tiled=True
        ).astype(jnp.float32),
        lax.psum_scatter(
            local_grads[3].astype(jnp.bfloat16), "seq", scatter_dimension=0, tiled=True
        ).astype(jnp.float32),
        lax.psum_scatter(
            local_grads[4].astype(jnp.bfloat16), "seq", scatter_dimension=0, tiled=True
        ).astype(jnp.float32),
        lax.psum_scatter(
            local_grads[5].astype(jnp.bfloat16), "seq", scatter_dimension=0, tiled=True
        ).astype(jnp.float32),
        lax.psum_scatter(
            local_grads[6].astype(jnp.bfloat16), "seq", scatter_dimension=0, tiled=True
        ).astype(jnp.float32),
        lax.psum_scatter(
            local_grads[7].astype(jnp.bfloat16), "seq", scatter_dimension=0, tiled=True
        ).astype(jnp.float32),
        lax.psum_scatter(
            local_grads[8].astype(jnp.bfloat16), "seq", scatter_dimension=0, tiled=True
        ).astype(jnp.float32),
        lax.psum_scatter(
            local_grads[9].astype(jnp.bfloat16), "seq", scatter_dimension=0, tiled=True
        ).astype(jnp.float32),
        lax.psum_scatter(
            local_grads[10].astype(jnp.bfloat16), "seq", scatter_dimension=0, tiled=True
        ).astype(jnp.float32),
        lax.psum_scatter(
            local_grads[11].astype(jnp.bfloat16), "seq", scatter_dimension=0, tiled=True
        ).astype(jnp.float32),
        lax.psum_scatter(
            local_grads[12].astype(jnp.bfloat16), "seq", scatter_dimension=0, tiled=True
        ).astype(jnp.float32),
    )
    totals = lax.psum(
        (
            shares[0],
            shares[1],
            shares[2],
            shares[3],
            shares[4],
            shares[5],
            shares[6],
            shares[7],
            shares[8],
            shares[9],
            shares[10],
            shares[11],
            shares[12],
        ),
        "ctx",
    )
    return (result.astype(jnp.bfloat16)[None], input_grad[None]) + tuple(totals)


QUARTER = 192
HALF = 96
ROWS = 128
WIDTH = 768
OWN = 512
f32, bf16 = jnp.float32, jnp.bfloat16


def core_swap(values):
    return lax.ppermute(values, "ctx", [(i, i ^ 1) for i in range(8)])


def chip_swap(values, mask):
    return lax.ppermute(values, "ctx", [(i, i ^ (2 * mask)) for i in range(8)])


def seq_swap(values, mask):
    return lax.ppermute(values, "seq", [(i, i ^ mask) for i in range(4)])


def chip_gather(values):
    return [values] + [chip_swap(values, m) for m in (1, 2, 3)]


def seq_gather(values):
    return [values] + [seq_swap(values, m) for m in (1, 2, 3)]


def after(values, *earlier):
    return lax.optimization_barrier((values, *earlier))[0]


def run(body, pos, args, outs, scratch=(), hbm=(), sems=0, limit=24, cost=0.001):
    vmem = pl.BlockSpec(memory_space=pltpu.VMEM)
    whole = pl.BlockSpec(memory_space=pl.ANY)
    scratch_shapes = [pltpu.VMEM(shape, kind) for shape, kind in scratch]
    if sems:
        scratch_shapes.append(pltpu.SemaphoreType.DMA((sems,)))
    return pl.pallas_call(
        body,
        out_shape=[jax.ShapeDtypeStruct(shape, kind) for shape, kind in outs],
        in_specs=[pl.BlockSpec(memory_space=pltpu.SMEM)]
        + [whole if n in hbm else vmem for n in range(len(args))],
        out_specs=[vmem] * len(outs),
        scratch_shapes=scratch_shapes,
        compiler_params=pltpu.CompilerParams(vmem_limit_bytes=limit << 20),
        cost_estimate=pl.CostEstimate(
            flops=int(cost * 524288000), bytes_accessed=1000, transcendentals=1
        ),
    )(pos, *args)


def dot(left, right):
    return lax.dot_general(left, right, (((1,), (0,)), ((), ())), preferred_element_type=f32)


def dot_t(left, right):
    return lax.dot_general(left, right, (((1,), (1,)), ((), ())), preferred_element_type=f32)


def t_dot(left, right):
    return lax.dot_general(left, right, (((0,), (0,)), ((), ())), preferred_element_type=f32)


def normal(values):
    center = values - jnp.mean(values, -1, keepdims=True)
    rstd = lax.rsqrt(jnp.mean(center * center, -1, keepdims=True) + EPSILON)
    return center * rstd, rstd


def norm_back(err, gain, hat, rstd):
    scaled = err * gain
    return rstd * (
        scaled
        - jnp.mean(scaled, -1, keepdims=True)
        - hat * jnp.mean(scaled * hat, -1, keepdims=True)
    )


def pack_body(pos, w_ref, tok_ref, cot_ref, ids_ref, *refs):
    small, up_ref = refs[:8], refs[8]
    piece_ref, mate_ref, pack_ref, w_rows, sem = refs[9:]
    k, c = pos[1], pos[2]
    copies = []
    for n, half in enumerate((c, 1 - c)):
        rows = pl.ds(pl.multiple_of(half * HALF, 32), HALF)
        copies.append(pltpu.make_async_copy(w_ref.at[rows, :], w_rows.at[n], sem.at[n]))
    copies += [
        pltpu.make_async_copy(tok_ref.at[0], pack_ref.at[pl.ds(0, ROWS), :], sem.at[2]),
        pltpu.make_async_copy(cot_ref.at[0], pack_ref.at[pl.ds(ROWS, ROWS), :], sem.at[3]),
    ]
    for copy in copies:
        copy.start()
    up = up_ref[...].astype(f32).reshape(1, WIDTH)
    part = jnp.zeros((1, QUARTER), f32)
    for q in range(4):
        part = jnp.where(k == q, up[:, QUARTER * q : QUARTER * (q + 1)], part)
    vecs = [ref[...].astype(f32).reshape(1, QUARTER) for ref in small] + [part]
    lines = [jnp.concatenate(vecs[3 * n : 3 * n + 3], 1) for n in range(3)]
    lines = jnp.concatenate(lines + [jnp.zeros((13, 3 * QUARTER), f32)], 0)
    piece_ref[HALF:, :] = lines.astype(bf16)
    ids = jnp.concatenate([ids_ref[...].astype(f32), jnp.zeros((1, WIDTH - ROWS), f32)], 1)
    pack_ref[2 * ROWS :, :] = jnp.concatenate([ids, jnp.zeros((7, WIDTH), f32)], 0).astype(bf16)
    copies[0].wait()
    copies[1].wait()
    for q in range(4):

        @pl.when(k == q)
        def _():
            for p in range(3):
                at = WIDTH * p + QUARTER * q
                cols = slice(QUARTER * p, QUARTER * (p + 1))
                piece_ref[:HALF, cols] = w_rows[0, :, at : at + QUARTER]
                mate_ref[:HALF, cols] = w_rows[1, :, at : at + QUARTER]

    copies[2].wait()
    copies[3].wait()


def rest_body(pos, wo_ref, wu_ref, wd_ref, out_ref, mate_ref, up_rows, sem):
    k, c = pos[1], pos[2]
    copies = []
    for n, (half, dst) in enumerate(((c, out_ref), (1 - c, mate_ref))):
        rows = pl.ds(pl.multiple_of(half * HALF, 32), HALF)
        down_rows = pl.ds(pl.multiple_of(k * QUARTER + half * HALF, 32), HALF)
        copies += [
            pltpu.make_async_copy(wu_ref.at[rows, :], up_rows.at[n], sem.at[3 * n]),
            pltpu.make_async_copy(wo_ref.at[rows, :], dst.at[pl.ds(0, HALF), :], sem.at[3 * n + 1]),
            pltpu.make_async_copy(
                wd_ref.at[down_rows, :], dst.at[pl.ds(2 * HALF, HALF), :], sem.at[3 * n + 2]
            ),
        ]
    for copy in copies:
        copy.start()
    copies[0].wait()
    copies[3].wait()
    for q in range(4):

        @pl.when(k == q)
        def _():
            for p in range(4):
                at = WIDTH * p + QUARTER * q
                cols = slice(QUARTER * p, QUARTER * (p + 1))
                out_ref[HALF : 2 * HALF, cols] = up_rows[0, :, at : at + QUARTER]
                mate_ref[HALF : 2 * HALF, cols] = up_rows[1, :, at : at + QUARTER]

    for n in (1, 2, 4, 5):
        copies[n].wait()


def qkv_body(pos, *refs):
    tok, own, oth = refs[0:4], refs[4:8], refs[8:12]
    q_ref, k0, k1, v0, v1, normed_ref, vec_ref, w_ref, sm = refs[12:]
    s, k, c = pos[0], pos[1], pos[2]
    for m in range(4):
        z = s ^ m
        at = pl.ds(pl.multiple_of(z * QUARTER + c * HALF, 32), HALF)
        w_ref[at, :] = own[m][:HALF, :]
        at = pl.ds(pl.multiple_of(z * QUARTER + (1 - c) * HALF, 32), HALF)
        w_ref[at, :] = oth[m][:HALF, :]
        sm[z] = own[m][HALF:, :].astype(f32)

    def seg(z, n):
        return sm[z, n // 3 : n // 3 + 1, QUARTER * (n % 3) : QUARTER * (n % 3 + 1)]

    def vec(n):
        return jnp.concatenate([seg(z, n) for z in range(4)], 1)

    def chip_seg(n):
        return seg(k, n)

    gain, shift = vec(0), vec(1)
    bias = jnp.concatenate([chip_seg(2), jnp.zeros((1, QUARTER), f32), chip_seg(3)], 1)
    vec_ref[...] = jnp.concatenate(
        [gain, shift, vec(4), vec(5), vec(6), vec(7), vec(8), jnp.zeros((1, WIDTH), f32)], 0
    )
    for r in range(4):
        hat, _ = normal(tok[r][:ROWS, :].astype(f32))
        normed_ref[ROWS * r : ROWS * (r + 1), :] = (hat * gain + shift).astype(bf16)
    projected = dot(normed_ref[...], w_ref[...]) + bias
    q_ref[...] = (projected[:, :QUARTER].astype(bf16).astype(f32) * 0.125).astype(bf16)
    k0[: OWN // 2, :] = projected[: OWN // 2, QUARTER : 2 * QUARTER].astype(bf16)
    k1[...] = projected[OWN // 2 :, QUARTER : 2 * QUARTER].astype(bf16)
    v0[...] = projected[: OWN // 2, 2 * QUARTER :].astype(bf16)
    v1[...] = projected[OWN // 2 :, 2 * QUARTER :].astype(bf16)
    ids = [tok[r][2 * ROWS :, :ROWS].astype(f32)[:1] for r in range(4)]
    ids = jnp.concatenate(ids + [jnp.zeros((4, ROWS), f32)], 0).astype(bf16)
    k0[OWN // 2 :, :] = jnp.concatenate([ids, jnp.zeros((8, QUARTER - ROWS), bf16)], 1)


def split_ids(kva, kvb):
    ids_a = kva[OWN // 2 :, :ROWS].astype(f32)
    ids_b = kvb[OWN // 2 :, :ROWS].astype(f32)
    keys = jnp.concatenate(
        [ids_a[r : r + 1] for r in range(4)] + [ids_b[r : r + 1] for r in range(4)], 1
    )
    return ids_a.T, keys


def all_keys(pair, key_ref, value_ref):
    half = OWN // 2
    for n in range(2):
        key_ref[OWN * n : OWN * n + half, :] = pair[4 * n][:half, :]
        key_ref[OWN * n + half : OWN * (n + 1), :] = pair[4 * n + 1][...]
        value_ref[OWN * n : OWN * n + half, :] = pair[4 * n + 2][...]
        value_ref[OWN * n + half : OWN * (n + 1), :] = pair[4 * n + 3][...]


def attend_body(pos, q_ref, *refs):
    pair, (mixed_ref, state_ref, key_ref, value_ref) = refs[:8], refs[8:]
    cols, keys = split_ids(pair[0], pair[4])
    all_keys(pair, key_ref, value_ref)
    lane = lax.broadcasted_iota(jnp.int32, (ROWS, 64), 1)
    for r in range(4):
        rows = slice(ROWS * r, ROWS * (r + 1))
        hidden = keys > cols[:, r : r + 1]
        heads, lse = [], jnp.zeros((ROWS, 64), f32)
        for h in range(3):
            at = slice(64 * h, 64 * h + 64)
            query = q_ref[rows, at]
            scores = dot_t(query, key_ref[:, at])
            scores = jnp.where(hidden, NEGATIVE, scores)
            top = jnp.max(scores, -1, keepdims=True)
            weights = jnp.exp(scores - top)
            total = jnp.sum(weights, -1, keepdims=True)
            low = weights.astype(bf16)
            out = dot(low, value_ref[:, at])
            heads.append(out * (1.0 / total))
            lse = jnp.where(lane == h, top + jnp.log(total), lse)
        mixed = jnp.concatenate(heads, 1)
        mixed_ref[rows, :] = mixed.astype(bf16)
        state_ref[rows, :] = jnp.concatenate([mixed, lse], 1)


def feed_body(pos, *refs):
    tok, mixed, own, oth = refs[0:4], refs[4:8], refs[8:12], refs[12:16]
    vec_ref = refs[16]
    mid_ref, n2_ref, act_ref, pre_ref, d0, d1, d2, d3, g0, g1, g2, g3, sums_ref, wok_ref = refs[17:31]
    wo, wu, wd, hat_ref = refs[31:]
    s, k, c = pos[0], pos[1], pos[2]
    for m in range(4):
        z = s ^ m
        for half, src in ((c, own[m]), (1 - c, oth[m])):
            at = pl.ds(pl.multiple_of(z * QUARTER + half * HALF, 32), HALF)
            wo[at, :] = src[:HALF, :]
            wu[at, :] = src[HALF : 2 * HALF, :]
            wd[at, :] = src[2 * HALF :, :]
    wok_ref[...] = wo[pl.ds(pl.multiple_of(k * QUARTER, 64), QUARTER), :]
    bias_out, gain, shift = vec_ref[2:3, :], vec_ref[3:4, :], vec_ref[4:5, :]
    bias_up = vec_ref[6:7, :]
    attended = bias_out
    for m in range(4):
        block = jnp.concatenate(
            [mixed[m][ROWS * (r ^ m) : ROWS * (r ^ m) + ROWS, :] for r in range(4)], 0
        )
        at = pl.ds(pl.multiple_of((k ^ m) * QUARTER, 64), QUARTER)
        attended = attended + dot(block, wo[at, :])
    for r in range(4):
        rows = slice(ROWS * r, ROWS * (r + 1))
        middle = tok[r][:ROWS, :].astype(f32) + attended[rows]
        if r == 0:
            mid_ref[...] = middle
        hat, _ = normal(middle)
        hat_ref[rows, :] = hat
        n2_ref[rows, :] = (hat * gain + shift).astype(bf16)
    pre_act = dot(n2_ref[...], wu[...]) + bias_up
    cdf = 0.5 * (1.0 + lax.erf(pre_act * (1.0 / math.sqrt(2.0))))
    act_ref[...] = (pre_act * cdf).astype(bf16)
    slope = cdf + pre_act * jnp.exp(-0.5 * pre_act * pre_act) * (1.0 / math.sqrt(2.0 * math.pi))
    grads = jnp.concatenate([ref[ROWS : 2 * ROWS, :] for ref in tok], 0)
    pre = (dot_t(grads, wd[...]) * slope).astype(bf16)
    pre_ref[...] = pre
    back = dot_t(pre, wu[...])
    sums = [
        jnp.sum(back * hat_ref[...], 0, keepdims=True),
        jnp.sum(back, 0, keepdims=True),
        jnp.sum(pre.astype(f32), 0, keepdims=True),
    ]
    sums_ref[...] = jnp.concatenate(sums + [jnp.zeros((5, WIDTH), f32)], 0)
    g0[...] = back[:ROWS]
    for r, ref in ((1, g1), (2, g2), (3, g3)):
        ref[...] = back[ROWS * r : ROWS * (r + 1)].astype(bf16)
    down = dot(act_ref[...], wd[...])
    d0[...] = down[:ROWS]
    for r, ref in ((1, d1), (2, d2), (3, d3)):
        ref[...] = down[ROWS * r : ROWS * (r + 1)].astype(bf16)


def feed_grad_body(pos, act_ref, n2_ref, pre_ref, c0, c1, c2, c3, x0, x1, x2, x3, own_ref, wg):
    s, c = pos[0], pos[2]
    grads = jnp.concatenate([ref[ROWS : 2 * ROWS, :] for ref in (c0, c1, c2, c3)], 0)
    for part in range(2):
        if part == 0:
            wg[...] = t_dot(act_ref[...], grads)
        else:
            wg[...] = t_dot(n2_ref[...], pre_ref[...])
        rows = slice(HALF * part, HALF * part + HALF)
        for m, send in enumerate((x0, x1, x2, x3)):
            z = s ^ m
            at = pl.ds(pl.multiple_of(z * QUARTER + c * HALF, 32), HALF)
            own_ref[m, rows, :] = wg[at, :]
            at = pl.ds(pl.multiple_of(z * QUARTER + (1 - c) * HALF, 32), HALF)
            send[rows, :] = wg[at, :].astype(bf16)


def halves_body(pos, own_ref, y0, y1, y2, y3, o0, o1, o2, o3):
    rows = y0.shape[0]
    for m, (got, out) in enumerate(((y0, o0), (y1, o1), (y2, o2), (y3, o3))):
        out[:rows, :] = (own_ref[m, :rows, :] + got[...].astype(f32)).astype(out.dtype)
        if own_ref.shape[1] > rows:
            out[rows:, :] = own_ref[m, rows:, :].astype(out.dtype)


def add_body(pos, o0, r1, r2, r3, out):
    total = o0[...] + r1[...].astype(f32) + r2[...].astype(f32) + r3[...].astype(f32)
    out[...] = total.astype(out.dtype)


def middle_body(pos, g0, r1, r2, r3, mid_ref, tok_ref, vec_ref, gm_ref, ga_ref):
    err = g0[...] + r1[...].astype(f32) + r2[...].astype(f32) + r3[...].astype(f32)
    hat, rstd = normal(mid_ref[...])
    grad = tok_ref[ROWS : 2 * ROWS, :].astype(f32) + norm_back(err, vec_ref[3:4, :], hat, rstd)
    gm_ref[...] = grad
    ga_ref[...] = grad.astype(bf16)


def attend_grad_body(pos, a0, a1, a2, a3, wok, q_ref, *refs):
    pair, state_ref, outs = refs[:8], refs[8], refs[9:]
    dq_ref, own_ref, x0, x1, x2, x3, p_ref, ds_ref, key_ref, value_ref = outs
    cols, keys = split_ids(pair[0], pair[4])
    all_keys(pair, key_ref, value_ref)
    grads = jnp.concatenate([ref[...] for ref in (a0, a1, a2, a3)], 0)
    grad_mixed = dot_t(grads, wok[...]).astype(bf16)
    dq = []
    for h in range(3):
        at = slice(64 * h, 64 * h + 64)
        at_v = slice(QUARTER + 64 * h, QUARTER + 64 * h + 64)
        query, grad = q_ref[:, at], grad_mixed[:, at]
        grad_q = []
        for r in range(4):
            rows = slice(ROWS * r, ROWS * (r + 1))
            hidden = keys > cols[:, r : r + 1]
            g = grad[rows]
            inner = jnp.sum(g.astype(f32) * state_ref[rows, at], -1, keepdims=True)
            lse = state_ref[rows, QUARTER + h : QUARTER + h + 1]
            scores = dot_t(query[rows], key_ref[:, at])
            probs = jnp.exp(jnp.where(hidden, NEGATIVE, scores) - lse)
            slopes = dot_t(g, value_ref[:, at])
            ds = (probs * (slopes - inner)).astype(bf16)
            p_ref[rows, :] = probs.astype(bf16)
            ds_ref[rows, :] = ds
            grad_q.append(dot(ds, key_ref[:, at]))
        dq.append(jnp.concatenate(grad_q, 0))
        dk = t_dot(ds_ref[...], query)
        dv = t_dot(p_ref[...], grad)
        own_ref[:, at] = dk[:OWN]
        own_ref[:, at_v] = dv[:OWN]
        half = OWN // 2
        x0[:, at] = dk[OWN : OWN + half].astype(bf16)
        x1[:, at] = dk[OWN + half :].astype(bf16)
        x2[:, at] = dv[OWN : OWN + half].astype(bf16)
        x3[:, at] = dv[OWN + half :].astype(bf16)
    dq_ref[...] = (jnp.concatenate(dq, 1) * 0.125).astype(bf16)


def project_grad_body(pos, *refs):
    tok, mixed, ga = refs[0:4], refs[4:8], refs[8:12]
    normed, dq, kv_own, y0, y1, y2, y3, w_ref, vec_ref, sums_ref, d1, d2, d3 = refs[12:25]
    x0, x1, x2, x3, own_ref, g0, g1, g2, g3, wg, sm, gk, gp = refs[25:]
    s, k, c = pos[0], pos[1], pos[2]
    gp[:, :QUARTER] = dq[...]
    got_k = jnp.concatenate([y0[...], y1[...]], 0)
    got_v = jnp.concatenate([y2[...], y3[...]], 0)
    got = jnp.concatenate([got_k, got_v], 1).astype(f32)
    gp[:, QUARTER:] = (kv_own[...] + got).astype(bf16)
    wg[:, : 3 * QUARTER] = t_dot(normed[...], gp[...])
    for q in range(4):

        @pl.when(k == q)
        def _():
            for r in range(4):
                gk[ROWS * r : ROWS * (r + 1), :] = ga[r][:, QUARTER * q : QUARTER * (q + 1)]

    for m in range(4):
        block = jnp.concatenate(
            [mixed[m][ROWS * (r ^ m) : ROWS * (r ^ m) + ROWS, :] for r in range(4)], 0
        )
        at = pl.ds(pl.multiple_of((k ^ m) * QUARTER, 64), QUARTER)
        wg[at, 3 * QUARTER :] = t_dot(block, gk[...])
    back = dot_t(gp[...], w_ref[...])
    hat = jnp.concatenate([normal(tok[r][:ROWS, :].astype(f32))[0] for r in range(4)], 0)
    ln1_gain = jnp.sum(back * hat, 0, keepdims=True)
    ln1_bias = jnp.sum(back, 0, keepdims=True)
    g0[...] = back[:ROWS]
    for r, ref, down in ((1, g1, d1), (2, g2, d2), (3, g3, d3)):
        ref[:ROWS, :] = back[ROWS * r : ROWS * (r + 1)].astype(bf16)
        ref[ROWS:, :] = down[...]
    gp_sums = jnp.sum(gp[...].astype(f32), 0, keepdims=True)
    out_bias = jnp.sum(ga[0][...].astype(f32), 0, keepdims=True)
    down_bias = jnp.sum(tok[0][ROWS : 2 * ROWS, :].astype(f32), 0, keepdims=True)
    for z in range(4):
        at = slice(QUARTER * z, QUARTER * (z + 1))
        here = jnp.where(k == z, 1.0, 0.0).astype(f32)
        row0 = [ln1_gain[:, at], ln1_bias[:, at], gp_sums[:, :QUARTER] * here]
        row0 = jnp.concatenate(row0 + [gp_sums[:, 2 * QUARTER :] * here], 1)
        row1 = [out_bias[:, at], sums_ref[0:1, at], sums_ref[1:2, at], down_bias[:, at]]
        row1 = jnp.concatenate(row1, 1)
        row2 = jnp.concatenate([sums_ref[2:3, at], jnp.zeros((1, 3 * QUARTER), f32)], 1)
        sm[z] = jnp.concatenate([row0, row1, row2, jnp.zeros((5, WIDTH), f32)], 0)
    for m in range(4):
        z = s ^ m
        at = pl.ds(pl.multiple_of(z * QUARTER + c * HALF, 32), HALF)
        own_ref[m, :HALF, :] = wg[at, :]
        own_ref[m, HALF:, :] = sm[z]
        at = pl.ds(pl.multiple_of(z * QUARTER + (1 - c) * HALF, 32), HALF)
        (x0, x1, x2, x3)[m][...] = wg[at, :].astype(bf16)


def rows_body(pos, g0, r1, r2, r3, d0, tok_ref, gm_ref, mid_ref, vec_ref, grad_ref, out_ref):
    got = [ref[...].astype(f32) for ref in (r1, r2, r3)]
    err = g0[...] + got[0][:ROWS] + got[1][:ROWS] + got[2][:ROWS]
    hat, rstd = normal(tok_ref[:ROWS, :].astype(f32))
    grad_ref[0] = gm_ref[...] + norm_back(err, vec_ref[0:1, :], hat, rstd)
    total = d0[...] + got[0][ROWS:] + got[1][ROWS:] + got[2][ROWS:]
    out_ref[0] = (mid_ref[...] + total + vec_ref[5:6, :]).astype(bf16)


def feed_join_body(pos, *refs):
    own, oth = refs[0:4], refs[4:8]
    down_ref, up_ref, sc = refs[8:]
    k, c = pos[1], pos[2]
    for m in range(4):
        sc[c, k ^ m] = own[m][...]
        sc[1 - c, k ^ m] = oth[m][...]
    for q in range(4):
        for half in range(2):
            at = QUARTER * q + HALF * half
            down_ref[at : at + HALF, :] = sc[half, q, :HALF, :].astype(f32)
            rows = slice(HALF * half, HALF * half + HALF)
            for p in range(4):
                cols = slice(WIDTH * p + QUARTER * q, WIDTH * p + QUARTER * (q + 1))
                piece = sc[half, q, HALF:, QUARTER * p : QUARTER * (p + 1)]
                up_ref[rows, cols] = piece.astype(f32)


def last_join_body(pos, *refs):
    own, oth = refs[0:4], refs[4:8]
    qkv_ref, out_ref, up_ref, sc = refs[8], refs[9], refs[18], refs[19]
    vec_refs = refs[10:18]
    k, c = pos[1], pos[2]
    for m in range(4):
        sc[c, k ^ m] = own[m][...]
        sc[1 - c, k ^ m] = oth[m][...]
    total = jnp.zeros((8, WIDTH), f32)
    ups = []
    for q in range(4):
        small = sc[0, q, HALF:, :].astype(f32) + sc[1, q, HALF:, :].astype(f32)
        total = total + small
        ups.append(small[2:3, :QUARTER])
        for half in range(2):
            rows = slice(HALF * half, HALF * half + HALF)
            for p in range(3):
                cols = slice(WIDTH * p + QUARTER * q, WIDTH * p + QUARTER * (q + 1))
                piece = sc[half, q, :HALF, QUARTER * p : QUARTER * (p + 1)]
                qkv_ref[rows, cols] = piece.astype(f32)
            out_ref[rows, QUARTER * q : QUARTER * (q + 1)] = sc[
                half, q, :HALF, 3 * QUARTER :
            ].astype(f32)
    for n, ref in enumerate(vec_refs):
        row = total[n // 4 : n // 4 + 1, QUARTER * (n % 4) : QUARTER * (n % 4 + 1)]
        ref[...] = row.reshape(QUARTER)
    up_ref[...] = jnp.concatenate(ups, 1).reshape(WIDTH)


def shards(
    tokens,
    block_ids,
    ln1_gain,
    ln1_bias,
    w_qkv,
    q_bias,
    v_bias,
    w_out,
    out_bias,
    ln2_gain,
    ln2_bias,
    w_up,
    up_bias,
    w_down,
    down_bias,
    cotangent,
):
    seq = lax.axis_index("seq")
    ctx = lax.axis_index("ctx")
    k, core = ctx // 2, ctx % 2
    pos = jnp.stack([seq, k, core]).astype(jnp.int32)

    small = [ln1_gain, ln1_bias, q_bias, v_bias, out_bias, ln2_gain, ln2_bias, down_bias, up_bias]
    piece_qkv, mate_qkv, pack = run(
        pack_body,
        pos,
        [w_qkv, tokens, cotangent, block_ids, *small],
        [((HALF + 16, 3 * QUARTER), bf16)] * 2 + [((2 * ROWS + 8, WIDTH), bf16)],
        [((2, HALF, 3 * WIDTH), bf16)],
        hbm=(0, 1, 2),
        sems=4,
        limit=60,
    )
    rest, mate_rest = run(
        rest_body,
        pos,
        [w_out, w_up, w_down],
        [((3 * HALF, WIDTH), bf16)] * 2,
        [((2, HALF, 4 * WIDTH), bf16)],
        hbm=(0, 1, 2),
        sems=6,
        limit=60,
    )
    got_qkv = seq_gather(piece_qkv)
    tok = chip_gather(pack)
    got_rest = seq_gather(rest)
    oth_qkv = [mate_qkv] + [core_swap(block) for block in got_qkv[1:]]
    half = (OWN // 2, QUARTER)
    query, *pair, normed, vec, weight_qkv = run(
        qkv_body,
        pos,
        [*tok, *got_qkv, *oth_qkv],
        [((OWN, QUARTER), bf16), ((OWN // 2 + 8, QUARTER), bf16), (half, bf16), (half, bf16)]
        + [(half, bf16), ((OWN, WIDTH), bf16), ((8, WIDTH), f32), ((WIDTH, 3 * QUARTER), bf16)],
        [((4, 16, 3 * QUARTER), f32)],
    )
    pair = [*pair, *[core_swap(x) for x in pair]]
    mixed_own, state = run(
        attend_body,
        pos,
        [query, *pair],
        [((OWN, QUARTER), bf16), ((OWN, 256), f32)],
        [((2 * OWN, QUARTER), bf16)] * 2,
    )
    mixed = chip_gather(mixed_own)
    got_rest = lax.optimization_barrier((*got_rest, *mixed[1:]))[:4]
    oth_rest = [mate_rest] + [core_swap(block) for block in got_rest[1:]]
    big, block = (OWN, WIDTH), (ROWS, WIDTH)
    mid, normed_two, act, pre, d0, d1, d2, d3, g0, g1, g2, g3, sums, w_out_k = run(
        feed_body,
        pos,
        [*tok, *mixed, *got_rest, *oth_rest, vec],
        [(block, f32), (big, bf16), (big, bf16), (big, bf16)]
        + [(block, f32), (block, bf16), (block, bf16), (block, bf16)] * 2
        + [((8, WIDTH), f32), ((QUARTER, WIDTH), bf16)],
        [((WIDTH, WIDTH), bf16)] * 3 + [(big, f32)],
        limit=32,
    )
    got_g = [chip_swap(g, m) for m, g in ((1, g1), (2, g2), (3, g3))]
    piece = (QUARTER, WIDTH)
    *feed_send, feed_own = run(
        feed_grad_body,
        pos,
        [after(act, got_g[0]), normed_two, pre, *tok],
        [(piece, bf16)] * 4 + [((4, *piece), f32)],
        [((WIDTH, WIDTH), f32)],
    )
    feed_got = [core_swap(x) for x in feed_send]
    grad_mid, grad_att = run(
        middle_body, pos, [g0, *got_g, mid, tok[0], vec], [(block, f32), (block, bf16)]
    )
    ga = chip_gather(grad_att)
    h0, h1, h2, h3 = run(
        halves_body, pos, [feed_own, *feed_got], [(piece, f32)] + [(piece, bf16)] * 3
    )
    feed_terms = [seq_swap(h, m) for m, h in ((1, h1), (2, h2), (3, h3))]
    dq, kv_own, *pair_send = run(
        attend_grad_body,
        pos,
        [*ga, w_out_k, after(query, h0), *pair, state],
        [((OWN, QUARTER), bf16), ((OWN, 2 * QUARTER), f32)] + [(half, bf16)] * 4,
        [((OWN, 2 * OWN), bf16)] * 2 + [((2 * OWN, QUARTER), bf16)] * 2,
    )
    pair_got = [core_swap(x) for x in pair_send]
    dq, *feed_two = lax.optimization_barrier((dq, *feed_terms[:2]))
    feed_terms = feed_two + feed_terms[2:]
    lpiece = (HALF + 8, WIDTH)
    *last_send, last_own, e0, e1, e2, e3 = run(
        project_grad_body,
        pos,
        [*tok, *mixed, *ga, normed, dq, kv_own, *pair_got, weight_qkv, vec, sums, d1, d2, d3],
        [((HALF, WIDTH), bf16)] * 4
        + [((4, *lpiece), f32), (block, f32)]
        + [((2 * ROWS, WIDTH), bf16)] * 3,
        [
            ((WIDTH, WIDTH), f32),
            ((4, 8, WIDTH), f32),
            ((OWN, QUARTER), bf16),
            ((OWN, 3 * QUARTER), bf16),
        ],
    )
    last_got = [core_swap(x) for x in last_send]
    l0, l1, l2, l3 = run(
        halves_body, pos, [last_own, *last_got], [(lpiece, f32)] + [(lpiece, bf16)] * 3
    )
    l1, l2, l3, *feed_last = lax.optimization_barrier((l1, l2, l3, *feed_terms[2:]))
    feed_terms = feed_two + feed_last
    last_terms = [seq_swap(h, m) for m, h in ((1, l1), (2, l2), (3, l3))]
    got_e = [chip_swap(e, m) for m, e in ((1, e1), (2, e2), (3, e3))]
    (feed_sum,) = run(add_body, pos, [h0, *feed_terms], [(piece, bf16)])
    feed_blocks = chip_gather(feed_sum)
    input_grad, result = run(
        rows_body,
        pos,
        [e0, *got_e, d0, tok[0], grad_mid, mid, vec],
        [((1, *block), f32), ((1, *block), bf16)],
    )
    (last_sum,) = run(add_body, pos, [l0, *last_terms], [(lpiece, bf16)])
    last_sum, got_e[0] = lax.optimization_barrier((last_sum, got_e[0]))
    last_blocks = chip_gather(last_sum)
    feed_oth = [core_swap(b) for b in feed_blocks]
    grad_w_down, grad_w_up = run(
        feed_join_body,
        pos,
        [after(feed_blocks[0], last_sum), *feed_blocks[1:], *feed_oth],
        [((WIDTH, WIDTH), f32), ((QUARTER, 4 * WIDTH), f32)],
        [((2, 4, QUARTER, WIDTH), bf16)],
    )
    last_oth = [core_swap(b) for b in last_blocks]
    grad_w_qkv, grad_w_out, *g, g_up = run(
        last_join_body,
        pos,
        [*last_blocks, *last_oth],
        [((QUARTER, 3 * WIDTH), f32), ((QUARTER, WIDTH), f32)]
        + [((QUARTER,), f32)] * 8
        + [((WIDTH,), f32)],
        [((2, 4, HALF + 8, WIDTH), bf16)],
    )
    return (
        result,
        input_grad,
        g[0],
        g[1],
        grad_w_qkv,
        g[2],
        g[3],
        grad_w_out,
        g[4],
        g[5],
        g[6],
        grad_w_up,
        g_up,
        grad_w_down,
        g[7],
    )


def solution(mesh):
    placed = (
        P("seq", "ctx", None),
        P("seq", "ctx"),
        P("seq"),
        P("seq"),
        P("seq", None),
        P("seq"),
        P("seq"),
        P("seq", None),
        P("seq"),
        P("seq"),
        P("seq"),
        P("seq", None),
        P("seq"),
        P("seq", None),
        P("seq"),
        P("seq", "ctx", None),
    )
    return jax.shard_map(
        shards if mesh.shape["ctx"] == 8 and mesh.shape["seq"] == 4 else shards_general,
        mesh=mesh,
        in_specs=placed,
        out_specs=(
            P("seq", "ctx", None),
            P("seq", "ctx", None),
            P("seq"),
            P("seq"),
            P("seq", None),
            P("seq"),
            P("seq"),
            P("seq", None),
            P("seq"),
            P("seq"),
            P("seq"),
            P("seq", None),
            P("seq"),
            P("seq", None),
            P("seq"),
        ),
        check_vma=False,
    )
```

```python
import math

import jax
import jax.numpy as jnp
from jax import lax
from jax.experimental import pallas as pl
from jax.experimental.pallas import tpu as pltpu
from jax.sharding import PartitionSpec as P

HEADS = 12


EPSILON = 1e-06
NEGATIVE = -1e30


def layer_norm(values, gain, shift):
    center = values - jnp.mean(values, -1, keepdims=True)
    spread = jnp.mean(center * center, -1, keepdims=True)
    return center * lax.rsqrt(spread + EPSILON) * gain + shift


def block_rows(count):
    return math.gcd(count, 512)


def masked_scores(query_heads, key_heads, query_ids, key_ids, scale):
    raw = (
        jnp.einsum("qhd,khd->hqk", query_heads, key_heads, preferred_element_type=jnp.float32)
        * scale
    )
    allowed = key_ids[None, None, :] <= query_ids[None, :, None]
    return (raw, allowed)


def attend_forward(query_heads, query_ids, keys_all, values_all, ids_all, scale):
    tok_rows, heads, head_dim = query_heads.shape
    total_keys = keys_all.shape[0]
    step = block_rows(total_keys)
    blocks = total_keys // step

    def attend_visit(carry, inputs):
        running, total, accum = carry
        key_block, value_block, id_block = inputs
        raw, allowed = masked_scores(query_heads, key_block, query_ids, id_block, scale)
        masked = jnp.where(allowed, raw, NEGATIVE)
        new_top = jnp.maximum(running, jnp.max(masked, -1))
        weights = jnp.where(allowed, jnp.exp(masked - new_top[..., None]), 0.0)
        factor = jnp.exp(running - new_top)
        total = total * factor + jnp.sum(weights, -1)
        accum = accum * factor[..., None] + jnp.einsum(
            "hqk,khd->hqd",
            weights.astype(jnp.bfloat16),
            value_block,
            preferred_element_type=jnp.float32,
        )
        return ((new_top, total, accum), None)

    start_state = (
        jnp.full((heads, tok_rows), NEGATIVE, jnp.float32),
        jnp.zeros((heads, tok_rows), jnp.float32),
        jnp.zeros((heads, tok_rows, head_dim), jnp.float32),
    )
    (running, total, accum), _ = lax.scan(
        attend_visit,
        start_state,
        (
            keys_all.reshape(blocks, step, heads, head_dim),
            values_all.reshape(blocks, step, heads, head_dim),
            ids_all.reshape(blocks, step),
        ),
    )
    output_heads = jnp.transpose(accum / total[..., None], (1, 0, 2))
    return (output_heads, running + jnp.log(total))


def query_gradient(
    query_heads, grad_heads, query_ids, keys_all, values_all, ids_all, logsum, inner, scale
):
    tok_rows, heads, head_dim = query_heads.shape
    total_keys = keys_all.shape[0]
    step = block_rows(total_keys)
    blocks = total_keys // step

    def query_visit(accum, inputs):
        key_block, value_block, id_block = inputs
        raw, allowed = masked_scores(query_heads, key_block, query_ids, id_block, scale)
        probs = jnp.where(allowed, jnp.exp(raw - logsum[..., None]), 0.0)
        grad_probs = jnp.einsum(
            "qhd,khd->hqk", grad_heads, value_block, preferred_element_type=jnp.float32
        )
        grad_scores = (probs * (grad_probs - inner[..., None])).astype(jnp.bfloat16)
        accum = accum + jnp.einsum(
            "hqk,khd->qhd", grad_scores, key_block, preferred_element_type=jnp.float32
        )
        return (accum, None)

    accum, _ = lax.scan(
        query_visit,
        jnp.zeros((tok_rows, heads, head_dim), jnp.float32),
        (
            keys_all.reshape(blocks, step, heads, head_dim),
            values_all.reshape(blocks, step, heads, head_dim),
            ids_all.reshape(blocks, step),
        ),
    )
    return accum * scale


def pair_grads(
    query_heads, grad_heads, query_ids, logsum, inner, key_heads, value_heads, key_ids, scale
):
    raw, allowed = masked_scores(query_heads, key_heads, query_ids, key_ids, scale)
    probs = jnp.where(allowed, jnp.exp(raw - logsum[..., None]), 0.0)
    grad_probs = jnp.einsum(
        "qhd,khd->hqk", grad_heads, value_heads, preferred_element_type=jnp.float32
    )
    grad_scores = (probs * (grad_probs - inner[..., None])).astype(jnp.bfloat16)
    grad_keys = (
        jnp.einsum("hqk,qhd->khd", grad_scores, query_heads, preferred_element_type=jnp.float32)
        * scale
    )
    grad_values = jnp.einsum(
        "hqk,qhd->khd", probs.astype(jnp.bfloat16), grad_heads, preferred_element_type=jnp.float32
    )
    return (grad_keys, grad_values)


def shards_general(
    tokens,
    block_ids,
    ln1_gain,
    ln1_bias,
    w_qkv,
    q_bias,
    v_bias,
    w_out,
    out_bias,
    ln2_gain,
    ln2_bias,
    w_up,
    up_bias,
    w_down,
    down_bias,
    cotangent,
):
    gathered = (
        lax.all_gather(ln1_gain, "seq", axis=0, tiled=True),
        lax.all_gather(ln1_bias, "seq", axis=0, tiled=True),
        lax.all_gather(w_qkv, "seq", axis=0, tiled=True),
        lax.all_gather(q_bias, "seq", axis=0, tiled=True),
        lax.all_gather(v_bias, "seq", axis=0, tiled=True),
        lax.all_gather(w_out, "seq", axis=0, tiled=True),
        lax.all_gather(out_bias, "seq", axis=0, tiled=True),
        lax.all_gather(ln2_gain, "seq", axis=0, tiled=True),
        lax.all_gather(ln2_bias, "seq", axis=0, tiled=True),
        lax.all_gather(w_up, "seq", axis=0, tiled=True),
        lax.all_gather(up_bias, "seq", axis=0, tiled=True),
        lax.all_gather(w_down, "seq", axis=0, tiled=True),
        lax.all_gather(down_bias, "seq", axis=0, tiled=True),
    )
    attention_part = gathered[:7]
    feed_part = gathered[7:]
    gain_one, shift_one, weight_qkv, bias_query, bias_value, weight_out, bias_out = attention_part
    width = weight_out.shape[0]
    heads = HEADS
    head_dim = width // heads
    scale = 1.0 / math.sqrt(head_dim)
    inputs = tokens[0].astype(jnp.float32)
    tok_rows = inputs.shape[0]
    own_ids = block_ids[0]
    gain_one_f = gain_one.astype(jnp.float32)
    shift_one_f = shift_one.astype(jnp.float32)
    normed_one, norm_one_pull = jax.vjp(layer_norm, inputs, gain_one_f, shift_one_f)
    normed_low = normed_one.astype(jnp.bfloat16)
    qkv_bias = jnp.concatenate(
        [
            bias_query.astype(jnp.float32),
            jnp.zeros((width,), jnp.float32),
            bias_value.astype(jnp.float32),
        ]
    )
    projected = (
        jnp.dot(normed_low, weight_qkv, preferred_element_type=jnp.float32) + qkv_bias
    ).astype(jnp.bfloat16)
    query_low = projected[:, :width]
    key_low = projected[:, width : 2 * width]
    value_low = projected[:, 2 * width :]
    ids_all = lax.all_gather(block_ids, "ctx", axis=1, tiled=True)[0]
    keys_all, values_all = (
        lax.all_gather(key_low, "ctx", axis=0, tiled=True),
        lax.all_gather(value_low, "ctx", axis=0, tiled=True),
    )
    query_heads = query_low.reshape(tok_rows, heads, head_dim)
    output_heads, logsum = attend_forward(
        query_heads, own_ids, keys_all, values_all, ids_all, scale
    )
    mixed_low = output_heads.reshape(tok_rows, width).astype(jnp.bfloat16)
    attended = jnp.dot(mixed_low, weight_out, preferred_element_type=jnp.float32) + bias_out.astype(
        jnp.float32
    )
    middle = inputs + attended
    gain_two, shift_two, weight_up, bias_up, weight_down, bias_down = feed_part
    gain_two_f = gain_two.astype(jnp.float32)
    shift_two_f = shift_two.astype(jnp.float32)
    normed_two, norm_two_pull = jax.vjp(layer_norm, middle, gain_two_f, shift_two_f)
    normed_two_low = normed_two.astype(jnp.bfloat16)
    pre_act = jnp.dot(
        normed_two_low, weight_up, preferred_element_type=jnp.float32
    ) + bias_up.astype(jnp.float32)
    activated, gelu_pull = jax.vjp(lambda values: jax.nn.gelu(values, approximate=False), pre_act)
    activated_low = activated.astype(jnp.bfloat16)
    result = (
        middle
        + jnp.dot(activated_low, weight_down, preferred_element_type=jnp.float32)
        + bias_down.astype(jnp.float32)
    )
    grad_out = cotangent[0]
    grad_out_f = grad_out.astype(jnp.float32)
    grad_weight_down = jnp.einsum(
        "tf,td->fd", activated_low, grad_out, preferred_element_type=jnp.float32
    )
    grad_bias_down = jnp.sum(grad_out_f, 0)
    grad_hidden = jnp.einsum("td,fd->tf", grad_out, weight_down, preferred_element_type=jnp.float32)
    grad_pre_low = gelu_pull(grad_hidden)[0].astype(jnp.bfloat16)
    grad_weight_up = jnp.einsum(
        "td,tf->df", normed_two_low, grad_pre_low, preferred_element_type=jnp.float32
    )
    grad_bias_up = jnp.sum(grad_pre_low.astype(jnp.float32), 0)
    grad_normed_two = jnp.einsum(
        "tf,df->td", grad_pre_low, weight_up, preferred_element_type=jnp.float32
    )
    grad_middle_part, grad_gain_two, grad_shift_two = norm_two_pull(grad_normed_two)
    grad_middle = grad_out_f + grad_middle_part
    grad_attended = grad_middle.astype(jnp.bfloat16)
    grad_weight_out = jnp.einsum(
        "td,te->de", mixed_low, grad_attended, preferred_element_type=jnp.float32
    )
    grad_bias_out = jnp.sum(grad_attended.astype(jnp.float32), 0)
    grad_mixed = jnp.einsum(
        "te,de->td", grad_attended, weight_out, preferred_element_type=jnp.float32
    ).astype(jnp.bfloat16)
    grad_heads = grad_mixed.reshape(tok_rows, heads, head_dim)
    inner = jnp.einsum("thd,thd->ht", grad_heads.astype(jnp.float32), output_heads)
    grad_query = query_gradient(
        query_heads, grad_heads, own_ids, keys_all, values_all, ids_all, logsum, inner, scale
    )
    step = block_rows(lax.axis_size("ctx") * tok_rows)
    blocks = lax.axis_size("ctx") * tok_rows // step
    key_part = keys_all.reshape(blocks, step, heads, head_dim)
    value_part = values_all.reshape(blocks, step, heads, head_dim)
    id_part = ids_all.reshape(blocks, step)

    def key_visit(carry, inputs):
        grad_keys, grad_values = pair_grads(
            query_heads, grad_heads, own_ids, logsum, inner, inputs[0], inputs[1], inputs[2], scale
        )
        joined = jnp.concatenate(
            [grad_keys.reshape(step, width), grad_values.reshape(step, width)], 1
        )
        return (carry, joined)

    _, terms = lax.scan(key_visit, jnp.zeros((), jnp.float32), (key_part, value_part, id_part))
    key_value_grads = lax.psum_scatter(
        terms.reshape(lax.axis_size("ctx") * tok_rows, 2 * width),
        "ctx",
        scatter_dimension=0,
        tiled=True,
    )
    grad_keys_all = key_value_grads[:, :width]
    grad_values_all = key_value_grads[:, width:]
    grad_query_low = grad_query.reshape(tok_rows, width).astype(jnp.bfloat16)
    grad_value_low = grad_values_all.astype(jnp.bfloat16)
    grad_projected = jnp.concatenate(
        [grad_query_low, grad_keys_all.astype(jnp.bfloat16), grad_value_low], 1
    )
    grad_weight_qkv = jnp.einsum(
        "td,te->de", normed_low, grad_projected, preferred_element_type=jnp.float32
    )
    grad_bias_query = jnp.sum(grad_query_low.astype(jnp.float32), 0)
    grad_bias_value = jnp.sum(grad_value_low.astype(jnp.float32), 0)
    grad_normed_one = jnp.einsum(
        "te,de->td", grad_projected, weight_qkv, preferred_element_type=jnp.float32
    )
    grad_input_part, grad_gain_one, grad_shift_one = norm_one_pull(grad_normed_one)
    input_grad = grad_middle + grad_input_part
    local_grads = (
        grad_gain_one,
        grad_shift_one,
        grad_weight_qkv,
        grad_bias_query,
        grad_bias_value,
        grad_weight_out,
        grad_bias_out,
        grad_gain_two,
        grad_shift_two,
        grad_weight_up,
        grad_bias_up,
        grad_weight_down,
        grad_bias_down,
    )
    shares = (
        lax.psum_scatter(
            local_grads[0].astype(jnp.bfloat16), "seq", scatter_dimension=0, tiled=True
        ).astype(jnp.float32),
        lax.psum_scatter(
            local_grads[1].astype(jnp.bfloat16), "seq", scatter_dimension=0, tiled=True
        ).astype(jnp.float32),
        lax.psum_scatter(
            local_grads[2].astype(jnp.bfloat16), "seq", scatter_dimension=0, tiled=True
        ).astype(jnp.float32),
        lax.psum_scatter(
            local_grads[3].astype(jnp.bfloat16), "seq", scatter_dimension=0, tiled=True
        ).astype(jnp.float32),
        lax.psum_scatter(
            local_grads[4].astype(jnp.bfloat16), "seq", scatter_dimension=0, tiled=True
        ).astype(jnp.float32),
        lax.psum_scatter(
            local_grads[5].astype(jnp.bfloat16), "seq", scatter_dimension=0, tiled=True
        ).astype(jnp.float32),
        lax.psum_scatter(
            local_grads[6].astype(jnp.bfloat16), "seq", scatter_dimension=0, tiled=True
        ).astype(jnp.float32),
        lax.psum_scatter(
            local_grads[7].astype(jnp.bfloat16), "seq", scatter_dimension=0, tiled=True
        ).astype(jnp.float32),
        lax.psum_scatter(
            local_grads[8].astype(jnp.bfloat16), "seq", scatter_dimension=0, tiled=True
        ).astype(jnp.float32),
        lax.psum_scatter(
            local_grads[9].astype(jnp.bfloat16), "seq", scatter_dimension=0, tiled=True
        ).astype(jnp.float32),
        lax.psum_scatter(
            local_grads[10].astype(jnp.bfloat16), "seq", scatter_dimension=0, tiled=True
        ).astype(jnp.float32),
        lax.psum_scatter(
            local_grads[11].astype(jnp.bfloat16), "seq", scatter_dimension=0, tiled=True
        ).astype(jnp.float32),
        lax.psum_scatter(
            local_grads[12].astype(jnp.bfloat16), "seq", scatter_dimension=0, tiled=True
        ).astype(jnp.float32),
    )
    totals = lax.psum(
        (
            shares[0],
            shares[1],
            shares[2],
            shares[3],
            shares[4],
            shares[5],
            shares[6],
            shares[7],
            shares[8],
            shares[9],
            shares[10],
            shares[11],
            shares[12],
        ),
        "ctx",
    )
    return (result.astype(jnp.bfloat16)[None], input_grad[None]) + tuple(totals)


QUARTER = 192
HALF = 96
ROWS = 128
WIDTH = 768
OWN = 512
f32, bf16 = jnp.float32, jnp.bfloat16


def core_swap(values):
    return lax.ppermute(values, "ctx", [(i, i ^ 1) for i in range(8)])


def chip_swap(values, mask):
    return lax.ppermute(values, "ctx", [(i, i ^ (2 * mask)) for i in range(8)])


def seq_swap(values, mask):
    return lax.ppermute(values, "seq", [(i, i ^ mask) for i in range(4)])


def chip_gather(values):
    return [values] + [chip_swap(values, m) for m in (1, 2, 3)]


def seq_gather(values):
    return [values] + [seq_swap(values, m) for m in (1, 2, 3)]


def after(values, *earlier):
    return lax.optimization_barrier((values, *earlier))[0]


def run(body, pos, args, outs, scratch=(), hbm=(), sems=0, limit=24, cost=0.001):
    vmem = pl.BlockSpec(memory_space=pltpu.VMEM)
    whole = pl.BlockSpec(memory_space=pl.ANY)
    scratch_shapes = [pltpu.VMEM(shape, kind) for shape, kind in scratch]
    if sems:
        scratch_shapes.append(pltpu.SemaphoreType.DMA((sems,)))
    return pl.pallas_call(
        body,
        out_shape=[jax.ShapeDtypeStruct(shape, kind) for shape, kind in outs],
        in_specs=[pl.BlockSpec(memory_space=pltpu.SMEM)]
        + [whole if n in hbm else vmem for n in range(len(args))],
        out_specs=[vmem] * len(outs),
        scratch_shapes=scratch_shapes,
        compiler_params=pltpu.CompilerParams(vmem_limit_bytes=limit << 20),
        cost_estimate=pl.CostEstimate(
            flops=int(cost * 524288000), bytes_accessed=1000, transcendentals=1
        ),
    )(pos, *args)


def dot(left, right):
    return lax.dot_general(left, right, (((1,), (0,)), ((), ())), preferred_element_type=f32)


def dot_t(left, right):
    return lax.dot_general(left, right, (((1,), (1,)), ((), ())), preferred_element_type=f32)


def t_dot(left, right):
    return lax.dot_general(left, right, (((0,), (0,)), ((), ())), preferred_element_type=f32)


def normal(values):
    center = values - jnp.mean(values, -1, keepdims=True)
    rstd = lax.rsqrt(jnp.mean(center * center, -1, keepdims=True) + EPSILON)
    return center * rstd, rstd


def norm_back(err, gain, hat, rstd):
    scaled = err * gain
    return rstd * (
        scaled
        - jnp.mean(scaled, -1, keepdims=True)
        - hat * jnp.mean(scaled * hat, -1, keepdims=True)
    )


def pack_body(pos, w_ref, tok_ref, cot_ref, wo_ref, wu_ref, wd_ref, ids_ref, *refs):
    small, up_ref = refs[:8], refs[8]
    piece_ref, mate_ref, pack_ref, rest_ref, rest_mate, w_rows, up_rows, sem = refs[9:]
    k, c = pos[1], pos[2]
    copies = [
        pltpu.make_async_copy(tok_ref.at[0], pack_ref.at[pl.ds(0, ROWS), :], sem.at[0]),
        pltpu.make_async_copy(cot_ref.at[0], pack_ref.at[pl.ds(ROWS, ROWS), :], sem.at[1]),
    ]
    for n, (half, dst) in enumerate(((c, rest_ref), (1 - c, rest_mate))):
        rows = pl.ds(pl.multiple_of(half * HALF, 32), HALF)
        down_rows = pl.ds(pl.multiple_of(k * QUARTER + half * HALF, 32), HALF)
        out_part, down_part = dst.at[pl.ds(0, HALF), :], dst.at[pl.ds(2 * HALF, HALF), :]
        copies += [
            pltpu.make_async_copy(w_ref.at[rows, :], w_rows.at[n], sem.at[2 + 4 * n]),
            pltpu.make_async_copy(wu_ref.at[rows, :], up_rows.at[n], sem.at[3 + 4 * n]),
            pltpu.make_async_copy(wo_ref.at[rows, :], out_part, sem.at[4 + 4 * n]),
            pltpu.make_async_copy(wd_ref.at[down_rows, :], down_part, sem.at[5 + 4 * n]),
        ]
    for copy in copies:
        copy.start()
    up = up_ref[...].astype(f32).reshape(1, WIDTH)
    part = jnp.zeros((1, QUARTER), f32)
    for q in range(4):
        part = jnp.where(k == q, up[:, QUARTER * q : QUARTER * (q + 1)], part)
    vecs = [ref[...].astype(f32).reshape(1, QUARTER) for ref in small] + [part]
    lines = [jnp.concatenate(vecs[3 * n : 3 * n + 3], 1) for n in range(3)]
    lines = jnp.concatenate(lines + [jnp.zeros((13, 3 * QUARTER), f32)], 0)
    piece_ref[HALF:, :] = lines.astype(bf16)
    ids = jnp.concatenate([ids_ref[...].astype(f32), jnp.zeros((1, WIDTH - ROWS), f32)], 1)
    pack_ref[2 * ROWS :, :] = jnp.concatenate([ids, jnp.zeros((7, WIDTH), f32)], 0).astype(bf16)
    for copy in copies:
        copy.wait()
    for q in range(4):

        @pl.when(k == q)
        def _():
            for p in range(4):
                at = WIDTH * p + QUARTER * q
                cols = slice(QUARTER * p, QUARTER * (p + 1))
                if p < 3:
                    piece_ref[:HALF, cols] = w_rows[0, :, at : at + QUARTER]
                    mate_ref[:HALF, cols] = w_rows[1, :, at : at + QUARTER]
                rest_ref[HALF : 2 * HALF, cols] = up_rows[0, :, at : at + QUARTER]
                rest_mate[HALF : 2 * HALF, cols] = up_rows[1, :, at : at + QUARTER]


def qkv_body(pos, *refs):
    tok, own, oth = refs[0:4], refs[4:8], refs[8:12]
    q_ref, k0, k1, v0, v1, normed_ref, vec_ref, w_ref, sm = refs[12:]
    s, k, c = pos[0], pos[1], pos[2]
    for m in range(4):
        z = s ^ m
        at = pl.ds(pl.multiple_of(z * QUARTER + c * HALF, 32), HALF)
        w_ref[at, :] = own[m][:HALF, :]
        at = pl.ds(pl.multiple_of(z * QUARTER + (1 - c) * HALF, 32), HALF)
        w_ref[at, :] = oth[m][:HALF, :]
        sm[z] = own[m][HALF:, :].astype(f32)

    def seg(z, n):
        return sm[z, n // 3 : n // 3 + 1, QUARTER * (n % 3) : QUARTER * (n % 3 + 1)]

    def vec(n):
        return jnp.concatenate([seg(z, n) for z in range(4)], 1)

    def chip_seg(n):
        return seg(k, n)

    gain, shift = vec(0), vec(1)
    bias = jnp.concatenate([chip_seg(2), jnp.zeros((1, QUARTER), f32), chip_seg(3)], 1)
    vec_ref[...] = jnp.concatenate(
        [gain, shift, vec(4), vec(5), vec(6), vec(7), vec(8), jnp.zeros((1, WIDTH), f32)], 0
    )
    for r in range(4):
        hat, _ = normal(tok[r][:ROWS, :].astype(f32))
        normed_ref[ROWS * r : ROWS * (r + 1), :] = (hat * gain + shift).astype(bf16)
    projected = dot(normed_ref[...], w_ref[...]) + bias
    q_ref[...] = (projected[:, :QUARTER].astype(bf16).astype(f32) * 0.125).astype(bf16)
    k0[: OWN // 2, :] = projected[: OWN // 2, QUARTER : 2 * QUARTER].astype(bf16)
    k1[...] = projected[OWN // 2 :, QUARTER : 2 * QUARTER].astype(bf16)
    v0[...] = projected[: OWN // 2, 2 * QUARTER :].astype(bf16)
    v1[...] = projected[OWN // 2 :, 2 * QUARTER :].astype(bf16)
    ids = [tok[r][2 * ROWS :, :ROWS].astype(f32)[:1] for r in range(4)]
    ids = jnp.concatenate(ids + [jnp.zeros((4, ROWS), f32)], 0).astype(bf16)
    k0[OWN // 2 :, :] = jnp.concatenate([ids, jnp.zeros((8, QUARTER - ROWS), bf16)], 1)


def split_ids(kva, kvb):
    ids_a = kva[OWN // 2 :, :ROWS].astype(f32)
    ids_b = kvb[OWN // 2 :, :ROWS].astype(f32)
    keys = jnp.concatenate(
        [ids_a[r : r + 1] for r in range(4)] + [ids_b[r : r + 1] for r in range(4)], 1
    )
    return ids_a.T, keys


def all_keys(pair, key_ref, value_ref):
    half = OWN // 2
    for n in range(2):
        key_ref[OWN * n : OWN * n + half, :] = pair[4 * n][:half, :]
        key_ref[OWN * n + half : OWN * (n + 1), :] = pair[4 * n + 1][...]
        value_ref[OWN * n : OWN * n + half, :] = pair[4 * n + 2][...]
        value_ref[OWN * n + half : OWN * (n + 1), :] = pair[4 * n + 3][...]


def attend_body(pos, q_ref, *refs):
    pair, (mixed_ref, state_ref, key_ref, value_ref) = refs[:8], refs[8:]
    cols, keys = split_ids(pair[0], pair[4])
    all_keys(pair, key_ref, value_ref)
    lane = lax.broadcasted_iota(jnp.int32, (ROWS, 64), 1)
    for r in range(4):
        rows = slice(ROWS * r, ROWS * (r + 1))
        hidden = keys > cols[:, r : r + 1]
        heads, lse = [], jnp.zeros((ROWS, 64), f32)
        for h in range(3):
            at = slice(64 * h, 64 * h + 64)
            query = q_ref[rows, at]
            scores = dot_t(query, key_ref[:, at])
            scores = jnp.where(hidden, NEGATIVE, scores)
            top = jnp.max(scores, -1, keepdims=True)
            weights = jnp.exp(scores - top)
            total = jnp.sum(weights, -1, keepdims=True)
            low = weights.astype(bf16)
            out = dot(low, value_ref[:, at])
            heads.append(out * (1.0 / total))
            lse = jnp.where(lane == h, top + jnp.log(total), lse)
        mixed = jnp.concatenate(heads, 1)
        mixed_ref[rows, :] = mixed.astype(bf16)
        state_ref[rows, :] = jnp.concatenate([mixed, lse], 1)


def feed_body(pos, *refs):
    tok, mixed, own, oth = refs[0:4], refs[4:8], refs[8:12], refs[12:16]
    vec_ref = refs[16]
    mid_ref, n2_ref, act_ref, pre_ref, d0, d1, d2, d3, g0, g1, g2, g3, sums_ref, wok_ref = refs[17:31]
    wo, wu, wd, hat_ref = refs[31:]
    s, k, c = pos[0], pos[1], pos[2]
    for m in range(4):
        z = s ^ m
        for half, src in ((c, own[m]), (1 - c, oth[m])):
            at = pl.ds(pl.multiple_of(z * QUARTER + half * HALF, 32), HALF)
            wo[at, :] = src[:HALF, :]
            wu[at, :] = src[HALF : 2 * HALF, :]
            wd[at, :] = src[2 * HALF :, :]
    wok_ref[...] = wo[pl.ds(pl.multiple_of(k * QUARTER, 64), QUARTER), :]
    bias_out, gain, shift = vec_ref[2:3, :], vec_ref[3:4, :], vec_ref[4:5, :]
    bias_up = vec_ref[6:7, :]
    attended = bias_out
    for m in range(4):
        block = jnp.concatenate(
            [mixed[m][ROWS * (r ^ m) : ROWS * (r ^ m) + ROWS, :] for r in range(4)], 0
        )
        at = pl.ds(pl.multiple_of((k ^ m) * QUARTER, 64), QUARTER)
        attended = attended + dot(block, wo[at, :])
    for r in range(4):
        rows = slice(ROWS * r, ROWS * (r + 1))
        middle = tok[r][:ROWS, :].astype(f32) + attended[rows]
        if r == 0:
            mid_ref[...] = middle
        hat, _ = normal(middle)
        hat_ref[rows, :] = hat
        n2_ref[rows, :] = (hat * gain + shift).astype(bf16)
    pre_act = dot(n2_ref[...], wu[...]) + bias_up
    cdf = 0.5 * (1.0 + lax.erf(pre_act * (1.0 / math.sqrt(2.0))))
    act_ref[...] = (pre_act * cdf).astype(bf16)
    slope = cdf + pre_act * jnp.exp(-0.5 * pre_act * pre_act) * (1.0 / math.sqrt(2.0 * math.pi))
    grads = jnp.concatenate([ref[ROWS : 2 * ROWS, :] for ref in tok], 0)
    pre = (dot_t(grads, wd[...]) * slope).astype(bf16)
    pre_ref[...] = pre
    back = dot_t(pre, wu[...])
    sums = [
        jnp.sum(back * hat_ref[...], 0, keepdims=True),
        jnp.sum(back, 0, keepdims=True),
        jnp.sum(pre.astype(f32), 0, keepdims=True),
    ]
    sums_ref[...] = jnp.concatenate(sums + [jnp.zeros((5, WIDTH), f32)], 0)
    g0[...] = back[:ROWS]
    for r, ref in ((1, g1), (2, g2), (3, g3)):
        ref[...] = back[ROWS * r : ROWS * (r + 1)].astype(bf16)
    down = dot(act_ref[...], wd[...])
    d0[...] = down[:ROWS]
    for r, ref in ((1, d1), (2, d2), (3, d3)):
        ref[...] = down[ROWS * r : ROWS * (r + 1)].astype(bf16)


def feed_grad_body(pos, act_ref, n2_ref, pre_ref, c0, c1, c2, c3, *refs):
    sends, (own_ref, wg) = refs[:8], refs[8:]
    s, c = pos[0], pos[2]
    grads = jnp.concatenate([ref[ROWS : 2 * ROWS, :] for ref in (c0, c1, c2, c3)], 0)
    for part in range(2):
        if part == 0:
            wg[...] = t_dot(act_ref[...], grads)
        else:
            wg[...] = t_dot(n2_ref[...], pre_ref[...])
        rows = slice(HALF * part, HALF * part + HALF)
        for m in range(4):
            z = s ^ m
            at = pl.ds(pl.multiple_of(z * QUARTER + c * HALF, 32), HALF)
            own_ref[m, rows, :] = wg[at, :]
            at = pl.ds(pl.multiple_of(z * QUARTER + (1 - c) * HALF, 32), HALF)
            sends[4 * part + m][...] = wg[at, :].astype(bf16)


def feed_halves_body(pos, own_ref, *refs):
    got, outs = refs[:8], refs[8:]
    for m, out in enumerate(outs):
        for part in range(2):
            rows = slice(HALF * part, HALF * part + HALF)
            total = own_ref[m, rows, :] + got[4 * part + m][...].astype(f32)
            out[rows, :] = total.astype(out.dtype)


def halves_body(pos, own_ref, y0, y1, y2, y3, o0, o1, o2, o3):
    rows = y0.shape[0]
    for m, (got, out) in enumerate(((y0, o0), (y1, o1), (y2, o2), (y3, o3))):
        out[:rows, :] = (own_ref[m, :rows, :] + got[...].astype(f32)).astype(out.dtype)
        if own_ref.shape[1] > rows:
            out[rows:, :] = own_ref[m, rows:, :].astype(out.dtype)


def add_body(pos, o0, r1, r2, r3, out):
    total = o0[...] + r1[...].astype(f32) + r2[...].astype(f32) + r3[...].astype(f32)
    out[...] = total.astype(out.dtype)


def middle_body(pos, g0, r1, r2, r3, mid_ref, tok_ref, vec_ref, gm_ref, ga_ref):
    err = g0[...] + r1[...].astype(f32) + r2[...].astype(f32) + r3[...].astype(f32)
    hat, rstd = normal(mid_ref[...])
    grad = tok_ref[ROWS : 2 * ROWS, :].astype(f32) + norm_back(err, vec_ref[3:4, :], hat, rstd)
    gm_ref[...] = grad
    ga_ref[...] = grad.astype(bf16)


def attend_grad_body(pos, a0, a1, a2, a3, wok, q_ref, *refs):
    pair, state_ref, outs = refs[:8], refs[8], refs[9:]
    dq_ref, own_ref, x0, x1, x2, x3, p_ref, ds_ref, key_ref, value_ref = outs
    cols, keys = split_ids(pair[0], pair[4])
    all_keys(pair, key_ref, value_ref)
    grads = jnp.concatenate([ref[...] for ref in (a0, a1, a2, a3)], 0)
    grad_mixed = dot_t(grads, wok[...]).astype(bf16)
    dq = []
    for h in range(3):
        at = slice(64 * h, 64 * h + 64)
        at_v = slice(QUARTER + 64 * h, QUARTER + 64 * h + 64)
        query, grad = q_ref[:, at], grad_mixed[:, at]
        grad_q = []
        for r in range(4):
            rows = slice(ROWS * r, ROWS * (r + 1))
            hidden = keys > cols[:, r : r + 1]
            g = grad[rows]
            inner = jnp.sum(g.astype(f32) * state_ref[rows, at], -1, keepdims=True)
            lse = state_ref[rows, QUARTER + h : QUARTER + h + 1]
            scores = dot_t(query[rows], key_ref[:, at])
            probs = jnp.exp(jnp.where(hidden, NEGATIVE, scores) - lse)
            slopes = dot_t(g, value_ref[:, at])
            ds = (probs * (slopes - inner)).astype(bf16)
            p_ref[rows, :] = probs.astype(bf16)
            ds_ref[rows, :] = ds
            grad_q.append(dot(ds, key_ref[:, at]))
        dq.append(jnp.concatenate(grad_q, 0))
        dk = t_dot(ds_ref[...], query)
        dv = t_dot(p_ref[...], grad)
        own_ref[:, at] = dk[:OWN]
        own_ref[:, at_v] = dv[:OWN]
        half = OWN // 2
        x0[:, at] = dk[OWN : OWN + half].astype(bf16)
        x1[:, at] = dk[OWN + half :].astype(bf16)
        x2[:, at] = dv[OWN : OWN + half].astype(bf16)
        x3[:, at] = dv[OWN + half :].astype(bf16)
    dq_ref[...] = (jnp.concatenate(dq, 1) * 0.125).astype(bf16)


def project_grad_body(pos, *refs):
    tok, mixed, ga = refs[0:4], refs[4:8], refs[8:12]
    normed, dq, kv_own, y0, y1, y2, y3, w_ref, vec_ref, sums_ref = refs[12:22]
    x0, x1, x2, x3, own_ref, g0, g1, g2, g3, wg, sm, gk, gp = refs[22:]
    s, k, c = pos[0], pos[1], pos[2]
    gp[:, :QUARTER] = dq[...]
    got_k = jnp.concatenate([y0[...], y1[...]], 0)
    got_v = jnp.concatenate([y2[...], y3[...]], 0)
    got = jnp.concatenate([got_k, got_v], 1).astype(f32)
    gp[:, QUARTER:] = (kv_own[...] + got).astype(bf16)
    wg[:, : 3 * QUARTER] = t_dot(normed[...], gp[...])
    for q in range(4):

        @pl.when(k == q)
        def _():
            for r in range(4):
                gk[ROWS * r : ROWS * (r + 1), :] = ga[r][:, QUARTER * q : QUARTER * (q + 1)]

    for m in range(4):
        block = jnp.concatenate(
            [mixed[m][ROWS * (r ^ m) : ROWS * (r ^ m) + ROWS, :] for r in range(4)], 0
        )
        at = pl.ds(pl.multiple_of((k ^ m) * QUARTER, 64), QUARTER)
        wg[at, 3 * QUARTER :] = t_dot(block, gk[...])
    back = dot_t(gp[...], w_ref[...])
    hat = jnp.concatenate([normal(tok[r][:ROWS, :].astype(f32))[0] for r in range(4)], 0)
    ln1_gain = jnp.sum(back * hat, 0, keepdims=True)
    ln1_bias = jnp.sum(back, 0, keepdims=True)
    g0[...] = back[:ROWS]
    for r, ref in ((1, g1), (2, g2), (3, g3)):
        ref[...] = back[ROWS * r : ROWS * (r + 1)].astype(bf16)
    gp_sums = jnp.sum(gp[...].astype(f32), 0, keepdims=True)
    out_bias = jnp.sum(ga[0][...].astype(f32), 0, keepdims=True)
    down_bias = jnp.sum(tok[0][ROWS : 2 * ROWS, :].astype(f32), 0, keepdims=True)
    for z in range(4):
        at = slice(QUARTER * z, QUARTER * (z + 1))
        here = jnp.where(k == z, 1.0, 0.0).astype(f32)
        row0 = [ln1_gain[:, at], ln1_bias[:, at], gp_sums[:, :QUARTER] * here]
        row0 = jnp.concatenate(row0 + [gp_sums[:, 2 * QUARTER :] * here], 1)
        row1 = [out_bias[:, at], sums_ref[0:1, at], sums_ref[1:2, at], down_bias[:, at]]
        row1 = jnp.concatenate(row1, 1)
        row2 = jnp.concatenate([sums_ref[2:3, at], jnp.zeros((1, 3 * QUARTER), f32)], 1)
        sm[z] = jnp.concatenate([row0, row1, row2, jnp.zeros((5, WIDTH), f32)], 0)
    for m in range(4):
        z = s ^ m
        at = pl.ds(pl.multiple_of(z * QUARTER + c * HALF, 32), HALF)
        own_ref[m, :HALF, :] = wg[at, :]
        own_ref[m, HALF:, :] = sm[z]
        at = pl.ds(pl.multiple_of(z * QUARTER + (1 - c) * HALF, 32), HALF)
        (x0, x1, x2, x3)[m][...] = wg[at, :].astype(bf16)


def rows_body(pos, g0, r1, r2, r3, d0, s1, s2, s3, tok_ref, gm_ref, mid_ref, vec_ref, *outs):
    grad_ref, out_ref = outs
    err = g0[...] + r1[...].astype(f32) + r2[...].astype(f32) + r3[...].astype(f32)
    hat, rstd = normal(tok_ref[:ROWS, :].astype(f32))
    grad_ref[0] = gm_ref[...] + norm_back(err, vec_ref[0:1, :], hat, rstd)
    total = d0[...] + s1[...].astype(f32) + s2[...].astype(f32) + s3[...].astype(f32)
    out_ref[0] = (mid_ref[...] + total + vec_ref[5:6, :]).astype(bf16)


def feed_join_body(pos, *refs):
    own, oth = refs[0:4], refs[4:8]
    down_ref, up_ref, sc = refs[8:]
    k, c = pos[1], pos[2]
    for m in range(4):
        sc[c, k ^ m] = own[m][...]
        sc[1 - c, k ^ m] = oth[m][...]
    for q in range(4):
        for half in range(2):
            at = QUARTER * q + HALF * half
            down_ref[at : at + HALF, :] = sc[half, q, :HALF, :].astype(f32)
            rows = slice(HALF * half, HALF * half + HALF)
            for p in range(4):
                cols = slice(WIDTH * p + QUARTER * q, WIDTH * p + QUARTER * (q + 1))
                piece = sc[half, q, HALF:, QUARTER * p : QUARTER * (p + 1)]
                up_ref[rows, cols] = piece.astype(f32)


def last_join_body(pos, *refs):
    own, oth = refs[0:4], refs[4:8]
    qkv_ref, out_ref, up_ref, sc = refs[8], refs[9], refs[18], refs[19]
    vec_refs = refs[10:18]
    k, c = pos[1], pos[2]
    for m in range(4):
        sc[c, k ^ m] = own[m][...]
        sc[1 - c, k ^ m] = oth[m][...]
    total = jnp.zeros((8, WIDTH), f32)
    ups = []
    for q in range(4):
        small = sc[0, q, HALF:, :].astype(f32) + sc[1, q, HALF:, :].astype(f32)
        total = total + small
        ups.append(small[2:3, :QUARTER])
        for half in range(2):
            rows = slice(HALF * half, HALF * half + HALF)
            for p in range(3):
                cols = slice(WIDTH * p + QUARTER * q, WIDTH * p + QUARTER * (q + 1))
                piece = sc[half, q, :HALF, QUARTER * p : QUARTER * (p + 1)]
                qkv_ref[rows, cols] = piece.astype(f32)
            out_ref[rows, QUARTER * q : QUARTER * (q + 1)] = sc[
                half, q, :HALF, 3 * QUARTER :
            ].astype(f32)
    for n, ref in enumerate(vec_refs):
        row = total[n // 4 : n // 4 + 1, QUARTER * (n % 4) : QUARTER * (n % 4 + 1)]
        ref[...] = row.reshape(QUARTER)
    up_ref[...] = jnp.concatenate(ups, 1).reshape(WIDTH)


def shards(
    tokens,
    block_ids,
    ln1_gain,
    ln1_bias,
    w_qkv,
    q_bias,
    v_bias,
    w_out,
    out_bias,
    ln2_gain,
    ln2_bias,
    w_up,
    up_bias,
    w_down,
    down_bias,
    cotangent,
):
    seq = lax.axis_index("seq")
    ctx = lax.axis_index("ctx")
    k, core = ctx // 2, ctx % 2
    pos = jnp.stack([seq, k, core]).astype(jnp.int32)

    small = [ln1_gain, ln1_bias, q_bias, v_bias, out_bias, ln2_gain, ln2_bias, down_bias, up_bias]
    piece_qkv, mate_qkv, pack, rest, mate_rest = run(
        pack_body,
        pos,
        [w_qkv, tokens, cotangent, w_out, w_up, w_down, block_ids, *small],
        [((HALF + 16, 3 * QUARTER), bf16)] * 2
        + [((2 * ROWS + 8, WIDTH), bf16)]
        + [((3 * HALF, WIDTH), bf16)] * 2,
        [((2, HALF, 3 * WIDTH), bf16), ((2, HALF, 4 * WIDTH), bf16)],
        hbm=range(6),
        sems=10,
        limit=60,
    )
    got_qkv = seq_gather(piece_qkv)
    tok = chip_gather(pack)
    got_rest = seq_gather(rest)
    oth_qkv = [mate_qkv] + [core_swap(block) for block in got_qkv[1:]]
    half = (OWN // 2, QUARTER)
    query, *pair, normed, vec, weight_qkv = run(
        qkv_body,
        pos,
        [*tok, *got_qkv, *oth_qkv],
        [((OWN, QUARTER), bf16), ((OWN // 2 + 8, QUARTER), bf16), (half, bf16), (half, bf16)]
        + [(half, bf16), ((OWN, WIDTH), bf16), ((8, WIDTH), f32), ((WIDTH, 3 * QUARTER), bf16)],
        [((4, 16, 3 * QUARTER), f32)],
    )
    pair = [*pair, *[core_swap(x) for x in pair]]
    mixed_own, state = run(
        attend_body,
        pos,
        [query, *pair],
        [((OWN, QUARTER), bf16), ((OWN, 256), f32)],
        [((2 * OWN, QUARTER), bf16)] * 2,
    )
    mixed = chip_gather(mixed_own)
    got_rest = lax.optimization_barrier((*got_rest, *mixed[1:]))[:4]
    oth_rest = [mate_rest] + [core_swap(block) for block in got_rest[1:]]
    big, block = (OWN, WIDTH), (ROWS, WIDTH)
    mid, normed_two, act, pre, d0, d1, d2, d3, g0, g1, g2, g3, sums, w_out_k = run(
        feed_body,
        pos,
        [*tok, *mixed, *got_rest, *oth_rest, vec],
        [(block, f32), (big, bf16), (big, bf16), (big, bf16)]
        + [(block, f32), (block, bf16), (block, bf16), (block, bf16)] * 2
        + [((8, WIDTH), f32), ((QUARTER, WIDTH), bf16)],
        [((WIDTH, WIDTH), bf16)] * 3 + [(big, f32)],
        limit=32,
    )
    got_g = [chip_swap(g, m) for m, g in ((1, g1), (2, g2), (3, g3))]
    piece = (QUARTER, WIDTH)
    *feed_send, feed_own = run(
        feed_grad_body,
        pos,
        [act, normed_two, pre, *tok],
        [((HALF, WIDTH), bf16)] * 8 + [((4, *piece), f32)],
        [((WIDTH, WIDTH), f32)],
    )
    feed_got = [core_swap(x) for x in feed_send]
    h0, h1, h2, h3 = run(
        feed_halves_body, pos, [feed_own, *feed_got], [(piece, f32)] + [(piece, bf16)] * 3
    )
    grad_mid, grad_att = run(
        middle_body, pos, [after(g0, h0), *got_g, mid, tok[0], vec], [(block, f32), (block, bf16)]
    )
    ga = chip_gather(grad_att)
    feed_terms = [seq_swap(h, m) for m, h in ((1, h1), (2, h2), (3, h3))]
    dq, kv_own, *pair_send = run(
        attend_grad_body,
        pos,
        [*ga, w_out_k, query, *pair, state],
        [((OWN, QUARTER), bf16), ((OWN, 2 * QUARTER), f32)] + [(half, bf16)] * 4,
        [((OWN, 2 * OWN), bf16)] * 2 + [((2 * OWN, QUARTER), bf16)] * 2,
    )
    pair_got = [core_swap(x) for x in pair_send]
    got_d = [chip_swap(after(d, dq), m) for m, d in ((1, d1), (2, d2), (3, d3))]
    lpiece = (HALF + 8, WIDTH)
    *last_send, last_own, e0, e1, e2, e3 = run(
        project_grad_body,
        pos,
        [*tok, *mixed, *ga, normed, dq, kv_own, *pair_got, weight_qkv, vec, sums],
        [((HALF, WIDTH), bf16)] * 4
        + [((4, *lpiece), f32), (block, f32)]
        + [(block, bf16)] * 3,
        [
            ((WIDTH, WIDTH), f32),
            ((4, 8, WIDTH), f32),
            ((OWN, QUARTER), bf16),
            ((OWN, 3 * QUARTER), bf16),
        ],
    )
    last_send[2], *got_d = lax.optimization_barrier((last_send[2], *got_d))
    last_send[3], *feed_terms = lax.optimization_barrier((last_send[3], *feed_terms))
    last_got = [core_swap(x) for x in last_send]
    l0, l1, l2, l3 = run(
        halves_body, pos, [last_own, *last_got], [(lpiece, f32)] + [(lpiece, bf16)] * 3
    )
    last_terms = [seq_swap(h, m) for m, h in ((1, l1), (2, l2), (3, l3))]
    got_e = [chip_swap(e, m) for m, e in ((1, e1), (2, e2), (3, e3))]
    (feed_sum,) = run(add_body, pos, [h0, *feed_terms], [(piece, bf16)])
    feed_blocks = chip_gather(feed_sum)
    input_grad, result = run(
        rows_body,
        pos,
        [e0, *got_e, d0, *got_d, tok[0], grad_mid, mid, vec],
        [((1, *block), f32), ((1, *block), bf16)],
    )
    l0, *got_e = lax.optimization_barrier((l0, *got_e))
    (last_sum,) = run(add_body, pos, [l0, *last_terms], [(lpiece, bf16)], cost=3)
    last_blocks = chip_gather(last_sum)
    feed_oth = [core_swap(b) for b in feed_blocks]
    grad_w_down, grad_w_up = run(
        feed_join_body,
        pos,
        [after(feed_blocks[0], last_sum), *feed_blocks[1:], *feed_oth],
        [((WIDTH, WIDTH), f32), ((QUARTER, 4 * WIDTH), f32)],
        [((2, 4, QUARTER, WIDTH), bf16)],
    )
    last_oth = [core_swap(b) for b in last_blocks]
    grad_w_qkv, grad_w_out, *g, g_up = run(
        last_join_body,
        pos,
        [*last_blocks, *last_oth],
        [((QUARTER, 3 * WIDTH), f32), ((QUARTER, WIDTH), f32)]
        + [((QUARTER,), f32)] * 8
        + [((WIDTH,), f32)],
        [((2, 4, HALF + 8, WIDTH), bf16)],
    )
    return (
        result,
        input_grad,
        g[0],
        g[1],
        grad_w_qkv,
        g[2],
        g[3],
        grad_w_out,
        g[4],
        g[5],
        g[6],
        grad_w_up,
        g_up,
        grad_w_down,
        g[7],
    )


def solution(mesh):
    placed = (
        P("seq", "ctx", None),
        P("seq", "ctx"),
        P("seq"),
        P("seq"),
        P("seq", None),
        P("seq"),
        P("seq"),
        P("seq", None),
        P("seq"),
        P("seq"),
        P("seq"),
        P("seq", None),
        P("seq"),
        P("seq", None),
        P("seq"),
        P("seq", "ctx", None),
    )
    return jax.shard_map(
        shards if mesh.shape["ctx"] == 8 and mesh.shape["seq"] == 4 else shards_general,
        mesh=mesh,
        in_specs=placed,
        out_specs=(
            P("seq", "ctx", None),
            P("seq", "ctx", None),
            P("seq"),
            P("seq"),
            P("seq", None),
            P("seq"),
            P("seq"),
            P("seq", None),
            P("seq"),
            P("seq"),
            P("seq"),
            P("seq", None),
            P("seq"),
            P("seq", None),
            P("seq"),
        ),
        check_vma=False,
    )
```

```python
import math

import jax
import jax.numpy as jnp
from jax import lax
from jax.experimental import pallas as pl
from jax.experimental.pallas import tpu as pltpu
from jax.sharding import PartitionSpec as P

HEADS = 12


EPSILON = 1e-06
NEGATIVE = -1e30


def layer_norm(values, gain, shift):
    center = values - jnp.mean(values, -1, keepdims=True)
    spread = jnp.mean(center * center, -1, keepdims=True)
    return center * lax.rsqrt(spread + EPSILON) * gain + shift


def block_rows(count):
    return math.gcd(count, 512)


def masked_scores(query_heads, key_heads, query_ids, key_ids, scale):
    raw = (
        jnp.einsum("qhd,khd->hqk", query_heads, key_heads, preferred_element_type=jnp.float32)
        * scale
    )
    allowed = key_ids[None, None, :] <= query_ids[None, :, None]
    return (raw, allowed)


def attend_forward(query_heads, query_ids, keys_all, values_all, ids_all, scale):
    tok_rows, heads, head_dim = query_heads.shape
    total_keys = keys_all.shape[0]
    step = block_rows(total_keys)
    blocks = total_keys // step

    def attend_visit(carry, inputs):
        running, total, accum = carry
        key_block, value_block, id_block = inputs
        raw, allowed = masked_scores(query_heads, key_block, query_ids, id_block, scale)
        masked = jnp.where(allowed, raw, NEGATIVE)
        new_top = jnp.maximum(running, jnp.max(masked, -1))
        weights = jnp.where(allowed, jnp.exp(masked - new_top[..., None]), 0.0)
        factor = jnp.exp(running - new_top)
        total = total * factor + jnp.sum(weights, -1)
        accum = accum * factor[..., None] + jnp.einsum(
            "hqk,khd->hqd",
            weights.astype(jnp.bfloat16),
            value_block,
            preferred_element_type=jnp.float32,
        )
        return ((new_top, total, accum), None)

    start_state = (
        jnp.full((heads, tok_rows), NEGATIVE, jnp.float32),
        jnp.zeros((heads, tok_rows), jnp.float32),
        jnp.zeros((heads, tok_rows, head_dim), jnp.float32),
    )
    (running, total, accum), _ = lax.scan(
        attend_visit,
        start_state,
        (
            keys_all.reshape(blocks, step, heads, head_dim),
            values_all.reshape(blocks, step, heads, head_dim),
            ids_all.reshape(blocks, step),
        ),
    )
    output_heads = jnp.transpose(accum / total[..., None], (1, 0, 2))
    return (output_heads, running + jnp.log(total))


def query_gradient(
    query_heads, grad_heads, query_ids, keys_all, values_all, ids_all, logsum, inner, scale
):
    tok_rows, heads, head_dim = query_heads.shape
    total_keys = keys_all.shape[0]
    step = block_rows(total_keys)
    blocks = total_keys // step

    def query_visit(accum, inputs):
        key_block, value_block, id_block = inputs
        raw, allowed = masked_scores(query_heads, key_block, query_ids, id_block, scale)
        probs = jnp.where(allowed, jnp.exp(raw - logsum[..., None]), 0.0)
        grad_probs = jnp.einsum(
            "qhd,khd->hqk", grad_heads, value_block, preferred_element_type=jnp.float32
        )
        grad_scores = (probs * (grad_probs - inner[..., None])).astype(jnp.bfloat16)
        accum = accum + jnp.einsum(
            "hqk,khd->qhd", grad_scores, key_block, preferred_element_type=jnp.float32
        )
        return (accum, None)

    accum, _ = lax.scan(
        query_visit,
        jnp.zeros((tok_rows, heads, head_dim), jnp.float32),
        (
            keys_all.reshape(blocks, step, heads, head_dim),
            values_all.reshape(blocks, step, heads, head_dim),
            ids_all.reshape(blocks, step),
        ),
    )
    return accum * scale


def pair_grads(
    query_heads, grad_heads, query_ids, logsum, inner, key_heads, value_heads, key_ids, scale
):
    raw, allowed = masked_scores(query_heads, key_heads, query_ids, key_ids, scale)
    probs = jnp.where(allowed, jnp.exp(raw - logsum[..., None]), 0.0)
    grad_probs = jnp.einsum(
        "qhd,khd->hqk", grad_heads, value_heads, preferred_element_type=jnp.float32
    )
    grad_scores = (probs * (grad_probs - inner[..., None])).astype(jnp.bfloat16)
    grad_keys = (
        jnp.einsum("hqk,qhd->khd", grad_scores, query_heads, preferred_element_type=jnp.float32)
        * scale
    )
    grad_values = jnp.einsum(
        "hqk,qhd->khd", probs.astype(jnp.bfloat16), grad_heads, preferred_element_type=jnp.float32
    )
    return (grad_keys, grad_values)


def shards_general(
    tokens,
    block_ids,
    ln1_gain,
    ln1_bias,
    w_qkv,
    q_bias,
    v_bias,
    w_out,
    out_bias,
    ln2_gain,
    ln2_bias,
    w_up,
    up_bias,
    w_down,
    down_bias,
    cotangent,
):
    gathered = (
        lax.all_gather(ln1_gain, "seq", axis=0, tiled=True),
        lax.all_gather(ln1_bias, "seq", axis=0, tiled=True),
        lax.all_gather(w_qkv, "seq", axis=0, tiled=True),
        lax.all_gather(q_bias, "seq", axis=0, tiled=True),
        lax.all_gather(v_bias, "seq", axis=0, tiled=True),
        lax.all_gather(w_out, "seq", axis=0, tiled=True),
        lax.all_gather(out_bias, "seq", axis=0, tiled=True),
        lax.all_gather(ln2_gain, "seq", axis=0, tiled=True),
        lax.all_gather(ln2_bias, "seq", axis=0, tiled=True),
        lax.all_gather(w_up, "seq", axis=0, tiled=True),
        lax.all_gather(up_bias, "seq", axis=0, tiled=True),
        lax.all_gather(w_down, "seq", axis=0, tiled=True),
        lax.all_gather(down_bias, "seq", axis=0, tiled=True),
    )
    attention_part = gathered[:7]
    feed_part = gathered[7:]
    gain_one, shift_one, weight_qkv, bias_query, bias_value, weight_out, bias_out = attention_part
    width = weight_out.shape[0]
    heads = HEADS
    head_dim = width // heads
    scale = 1.0 / math.sqrt(head_dim)
    inputs = tokens[0].astype(jnp.float32)
    tok_rows = inputs.shape[0]
    own_ids = block_ids[0]
    gain_one_f = gain_one.astype(jnp.float32)
    shift_one_f = shift_one.astype(jnp.float32)
    normed_one, norm_one_pull = jax.vjp(layer_norm, inputs, gain_one_f, shift_one_f)
    normed_low = normed_one.astype(jnp.bfloat16)
    qkv_bias = jnp.concatenate(
        [
            bias_query.astype(jnp.float32),
            jnp.zeros((width,), jnp.float32),
            bias_value.astype(jnp.float32),
        ]
    )
    projected = (
        jnp.dot(normed_low, weight_qkv, preferred_element_type=jnp.float32) + qkv_bias
    ).astype(jnp.bfloat16)
    query_low = projected[:, :width]
    key_low = projected[:, width : 2 * width]
    value_low = projected[:, 2 * width :]
    ids_all = lax.all_gather(block_ids, "ctx", axis=1, tiled=True)[0]
    keys_all, values_all = (
        lax.all_gather(key_low, "ctx", axis=0, tiled=True),
        lax.all_gather(value_low, "ctx", axis=0, tiled=True),
    )
    query_heads = query_low.reshape(tok_rows, heads, head_dim)
    output_heads, logsum = attend_forward(
        query_heads, own_ids, keys_all, values_all, ids_all, scale
    )
    mixed_low = output_heads.reshape(tok_rows, width).astype(jnp.bfloat16)
    attended = jnp.dot(mixed_low, weight_out, preferred_element_type=jnp.float32) + bias_out.astype(
        jnp.float32
    )
    middle = inputs + attended
    gain_two, shift_two, weight_up, bias_up, weight_down, bias_down = feed_part
    gain_two_f = gain_two.astype(jnp.float32)
    shift_two_f = shift_two.astype(jnp.float32)
    normed_two, norm_two_pull = jax.vjp(layer_norm, middle, gain_two_f, shift_two_f)
    normed_two_low = normed_two.astype(jnp.bfloat16)
    pre_act = jnp.dot(
        normed_two_low, weight_up, preferred_element_type=jnp.float32
    ) + bias_up.astype(jnp.float32)
    activated, gelu_pull = jax.vjp(lambda values: jax.nn.gelu(values, approximate=False), pre_act)
    activated_low = activated.astype(jnp.bfloat16)
    result = (
        middle
        + jnp.dot(activated_low, weight_down, preferred_element_type=jnp.float32)
        + bias_down.astype(jnp.float32)
    )
    grad_out = cotangent[0]
    grad_out_f = grad_out.astype(jnp.float32)
    grad_weight_down = jnp.einsum(
        "tf,td->fd", activated_low, grad_out, preferred_element_type=jnp.float32
    )
    grad_bias_down = jnp.sum(grad_out_f, 0)
    grad_hidden = jnp.einsum("td,fd->tf", grad_out, weight_down, preferred_element_type=jnp.float32)
    grad_pre_low = gelu_pull(grad_hidden)[0].astype(jnp.bfloat16)
    grad_weight_up = jnp.einsum(
        "td,tf->df", normed_two_low, grad_pre_low, preferred_element_type=jnp.float32
    )
    grad_bias_up = jnp.sum(grad_pre_low.astype(jnp.float32), 0)
    grad_normed_two = jnp.einsum(
        "tf,df->td", grad_pre_low, weight_up, preferred_element_type=jnp.float32
    )
    grad_middle_part, grad_gain_two, grad_shift_two = norm_two_pull(grad_normed_two)
    grad_middle = grad_out_f + grad_middle_part
    grad_attended = grad_middle.astype(jnp.bfloat16)
    grad_weight_out = jnp.einsum(
        "td,te->de", mixed_low, grad_attended, preferred_element_type=jnp.float32
    )
    grad_bias_out = jnp.sum(grad_attended.astype(jnp.float32), 0)
    grad_mixed = jnp.einsum(
        "te,de->td", grad_attended, weight_out, preferred_element_type=jnp.float32
    ).astype(jnp.bfloat16)
    grad_heads = grad_mixed.reshape(tok_rows, heads, head_dim)
    inner = jnp.einsum("thd,thd->ht", grad_heads.astype(jnp.float32), output_heads)
    grad_query = query_gradient(
        query_heads, grad_heads, own_ids, keys_all, values_all, ids_all, logsum, inner, scale
    )
    step = block_rows(lax.axis_size("ctx") * tok_rows)
    blocks = lax.axis_size("ctx") * tok_rows // step
    key_part = keys_all.reshape(blocks, step, heads, head_dim)
    value_part = values_all.reshape(blocks, step, heads, head_dim)
    id_part = ids_all.reshape(blocks, step)

    def key_visit(carry, inputs):
        grad_keys, grad_values = pair_grads(
            query_heads, grad_heads, own_ids, logsum, inner, inputs[0], inputs[1], inputs[2], scale
        )
        joined = jnp.concatenate(
            [grad_keys.reshape(step, width), grad_values.reshape(step, width)], 1
        )
        return (carry, joined)

    _, terms = lax.scan(key_visit, jnp.zeros((), jnp.float32), (key_part, value_part, id_part))
    key_value_grads = lax.psum_scatter(
        terms.reshape(lax.axis_size("ctx") * tok_rows, 2 * width),
        "ctx",
        scatter_dimension=0,
        tiled=True,
    )
    grad_keys_all = key_value_grads[:, :width]
    grad_values_all = key_value_grads[:, width:]
    grad_query_low = grad_query.reshape(tok_rows, width).astype(jnp.bfloat16)
    grad_value_low = grad_values_all.astype(jnp.bfloat16)
    grad_projected = jnp.concatenate(
        [grad_query_low, grad_keys_all.astype(jnp.bfloat16), grad_value_low], 1
    )
    grad_weight_qkv = jnp.einsum(
        "td,te->de", normed_low, grad_projected, preferred_element_type=jnp.float32
    )
    grad_bias_query = jnp.sum(grad_query_low.astype(jnp.float32), 0)
    grad_bias_value = jnp.sum(grad_value_low.astype(jnp.float32), 0)
    grad_normed_one = jnp.einsum(
        "te,de->td", grad_projected, weight_qkv, preferred_element_type=jnp.float32
    )
    grad_input_part, grad_gain_one, grad_shift_one = norm_one_pull(grad_normed_one)
    input_grad = grad_middle + grad_input_part
    local_grads = (
        grad_gain_one,
        grad_shift_one,
        grad_weight_qkv,
        grad_bias_query,
        grad_bias_value,
        grad_weight_out,
        grad_bias_out,
        grad_gain_two,
        grad_shift_two,
        grad_weight_up,
        grad_bias_up,
        grad_weight_down,
        grad_bias_down,
    )
    shares = (
        lax.psum_scatter(
            local_grads[0].astype(jnp.bfloat16), "seq", scatter_dimension=0, tiled=True
        ).astype(jnp.float32),
        lax.psum_scatter(
            local_grads[1].astype(jnp.bfloat16), "seq", scatter_dimension=0, tiled=True
        ).astype(jnp.float32),
        lax.psum_scatter(
            local_grads[2].astype(jnp.bfloat16), "seq", scatter_dimension=0, tiled=True
        ).astype(jnp.float32),
        lax.psum_scatter(
            local_grads[3].astype(jnp.bfloat16), "seq", scatter_dimension=0, tiled=True
        ).astype(jnp.float32),
        lax.psum_scatter(
            local_grads[4].astype(jnp.bfloat16), "seq", scatter_dimension=0, tiled=True
        ).astype(jnp.float32),
        lax.psum_scatter(
            local_grads[5].astype(jnp.bfloat16), "seq", scatter_dimension=0, tiled=True
        ).astype(jnp.float32),
        lax.psum_scatter(
            local_grads[6].astype(jnp.bfloat16), "seq", scatter_dimension=0, tiled=True
        ).astype(jnp.float32),
        lax.psum_scatter(
            local_grads[7].astype(jnp.bfloat16), "seq", scatter_dimension=0, tiled=True
        ).astype(jnp.float32),
        lax.psum_scatter(
            local_grads[8].astype(jnp.bfloat16), "seq", scatter_dimension=0, tiled=True
        ).astype(jnp.float32),
        lax.psum_scatter(
            local_grads[9].astype(jnp.bfloat16), "seq", scatter_dimension=0, tiled=True
        ).astype(jnp.float32),
        lax.psum_scatter(
            local_grads[10].astype(jnp.bfloat16), "seq", scatter_dimension=0, tiled=True
        ).astype(jnp.float32),
        lax.psum_scatter(
            local_grads[11].astype(jnp.bfloat16), "seq", scatter_dimension=0, tiled=True
        ).astype(jnp.float32),
        lax.psum_scatter(
            local_grads[12].astype(jnp.bfloat16), "seq", scatter_dimension=0, tiled=True
        ).astype(jnp.float32),
    )
    totals = lax.psum(
        (
            shares[0],
            shares[1],
            shares[2],
            shares[3],
            shares[4],
            shares[5],
            shares[6],
            shares[7],
            shares[8],
            shares[9],
            shares[10],
            shares[11],
            shares[12],
        ),
        "ctx",
    )
    return (result.astype(jnp.bfloat16)[None], input_grad[None]) + tuple(totals)


QUARTER = 192
HALF = 96
ROWS = 128
WIDTH = 768
OWN = 512
f32, bf16 = jnp.float32, jnp.bfloat16


def core_swap(values):
    return lax.ppermute(values, "ctx", [(i, i ^ 1) for i in range(8)])


def chip_swap(values, mask):
    return lax.ppermute(values, "ctx", [(i, i ^ (2 * mask)) for i in range(8)])


def seq_swap(values, mask):
    return lax.ppermute(values, "seq", [(i, i ^ mask) for i in range(4)])


def chip_gather(values):
    return [values] + [chip_swap(values, m) for m in (1, 2, 3)]


def seq_gather(values):
    return [values] + [seq_swap(values, m) for m in (1, 2, 3)]


def after(values, *earlier):
    return lax.optimization_barrier((values, *earlier))[0]


def run(body, pos, args, outs, scratch=(), hbm=(), sems=0, limit=24, cost=0.001):
    vmem = pl.BlockSpec(memory_space=pltpu.VMEM)
    whole = pl.BlockSpec(memory_space=pl.ANY)
    scratch_shapes = [pltpu.VMEM(shape, kind) for shape, kind in scratch]
    if sems:
        scratch_shapes.append(pltpu.SemaphoreType.DMA((sems,)))
    return pl.pallas_call(
        body,
        out_shape=[jax.ShapeDtypeStruct(shape, kind) for shape, kind in outs],
        in_specs=[pl.BlockSpec(memory_space=pltpu.SMEM)]
        + [whole if n in hbm else vmem for n in range(len(args))],
        out_specs=[vmem] * len(outs),
        scratch_shapes=scratch_shapes,
        compiler_params=pltpu.CompilerParams(vmem_limit_bytes=limit << 20),
        cost_estimate=pl.CostEstimate(
            flops=int(cost * 524288000), bytes_accessed=1000, transcendentals=1
        ),
    )(pos, *args)


def dot(left, right):
    return lax.dot_general(left, right, (((1,), (0,)), ((), ())), preferred_element_type=f32)


def dot_t(left, right):
    return lax.dot_general(left, right, (((1,), (1,)), ((), ())), preferred_element_type=f32)


def t_dot(left, right):
    return lax.dot_general(left, right, (((0,), (0,)), ((), ())), preferred_element_type=f32)


def normal(values):
    center = values - jnp.mean(values, -1, keepdims=True)
    rstd = lax.rsqrt(jnp.mean(center * center, -1, keepdims=True) + EPSILON)
    return center * rstd, rstd


def norm_back(err, gain, hat, rstd):
    scaled = err * gain
    return rstd * (
        scaled
        - jnp.mean(scaled, -1, keepdims=True)
        - hat * jnp.mean(scaled * hat, -1, keepdims=True)
    )


def pack_body(pos, w_ref, tok_ref, cot_ref, wo_ref, wu_ref, wd_ref, ids_ref, *refs):
    small, up_ref = refs[:8], refs[8]
    piece_ref, mate_ref, pack_ref, rest_ref, rest_mate, w_rows, up_rows, sem = refs[9:]
    k, c = pos[1], pos[2]
    copies = [
        pltpu.make_async_copy(tok_ref.at[0], pack_ref.at[pl.ds(0, ROWS), :], sem.at[0]),
        pltpu.make_async_copy(cot_ref.at[0], pack_ref.at[pl.ds(ROWS, ROWS), :], sem.at[1]),
    ]
    for n, (half, dst) in enumerate(((c, rest_ref), (1 - c, rest_mate))):
        rows = pl.ds(pl.multiple_of(half * HALF, 32), HALF)
        down_rows = pl.ds(pl.multiple_of(k * QUARTER + half * HALF, 32), HALF)
        out_part, down_part = dst.at[pl.ds(0, HALF), :], dst.at[pl.ds(2 * HALF, HALF), :]
        copies += [
            pltpu.make_async_copy(w_ref.at[rows, :], w_rows.at[n], sem.at[2 + 4 * n]),
            pltpu.make_async_copy(wu_ref.at[rows, :], up_rows.at[n], sem.at[3 + 4 * n]),
            pltpu.make_async_copy(wo_ref.at[rows, :], out_part, sem.at[4 + 4 * n]),
            pltpu.make_async_copy(wd_ref.at[down_rows, :], down_part, sem.at[5 + 4 * n]),
        ]
    for copy in copies:
        copy.start()
    up = up_ref[...].astype(f32).reshape(1, WIDTH)
    part = jnp.zeros((1, QUARTER), f32)
    for q in range(4):
        part = jnp.where(k == q, up[:, QUARTER * q : QUARTER * (q + 1)], part)
    vecs = [ref[...].astype(f32).reshape(1, QUARTER) for ref in small] + [part]
    lines = [jnp.concatenate(vecs[3 * n : 3 * n + 3], 1) for n in range(3)]
    lines = jnp.concatenate(lines + [jnp.zeros((13, 3 * QUARTER), f32)], 0)
    piece_ref[HALF:, :] = lines.astype(bf16)
    ids = jnp.concatenate([ids_ref[...].astype(f32), jnp.zeros((1, WIDTH - ROWS), f32)], 1)
    pack_ref[2 * ROWS :, :] = jnp.concatenate([ids, jnp.zeros((7, WIDTH), f32)], 0).astype(bf16)
    for copy in copies:
        copy.wait()
    for q in range(4):

        @pl.when(k == q)
        def _():
            for p in range(4):
                at = WIDTH * p + QUARTER * q
                cols = slice(QUARTER * p, QUARTER * (p + 1))
                if p < 3:
                    piece_ref[:HALF, cols] = w_rows[0, :, at : at + QUARTER]
                    mate_ref[:HALF, cols] = w_rows[1, :, at : at + QUARTER]
                rest_ref[HALF : 2 * HALF, cols] = up_rows[0, :, at : at + QUARTER]
                rest_mate[HALF : 2 * HALF, cols] = up_rows[1, :, at : at + QUARTER]


def qkv_body(pos, *refs):
    tok, own, oth = refs[0:4], refs[4:8], refs[8:12]
    q_ref, k_ref, v_ref, normed_ref, vec_ref, w_ref, sm = refs[12:]
    s, k, c = pos[0], pos[1], pos[2]
    for m in range(4):
        z = s ^ m
        at = pl.ds(pl.multiple_of(z * QUARTER + c * HALF, 32), HALF)
        w_ref[at, :] = own[m][:HALF, :]
        at = pl.ds(pl.multiple_of(z * QUARTER + (1 - c) * HALF, 32), HALF)
        w_ref[at, :] = oth[m][:HALF, :]
        sm[z] = own[m][HALF:, :].astype(f32)

    def seg(z, n):
        return sm[z, n // 3 : n // 3 + 1, QUARTER * (n % 3) : QUARTER * (n % 3 + 1)]

    def vec(n):
        return jnp.concatenate([seg(z, n) for z in range(4)], 1)

    def chip_seg(n):
        return seg(k, n)

    gain, shift = vec(0), vec(1)
    bias = jnp.concatenate([chip_seg(2), jnp.zeros((1, QUARTER), f32), chip_seg(3)], 1)
    vec_ref[...] = jnp.concatenate(
        [gain, shift, vec(4), vec(5), vec(6), vec(7), vec(8), jnp.zeros((1, WIDTH), f32)], 0
    )
    for r in range(4):
        hat, _ = normal(tok[r][:ROWS, :].astype(f32))
        normed_ref[ROWS * r : ROWS * (r + 1), :] = (hat * gain + shift).astype(bf16)
    projected = dot(normed_ref[...], w_ref[...]) + bias
    q_ref[...] = (projected[:, :QUARTER].astype(bf16).astype(f32) * 0.125).astype(bf16)
    k_ref[:OWN, :] = projected[:, QUARTER : 2 * QUARTER].astype(bf16)
    v_ref[...] = projected[:, 2 * QUARTER :].astype(bf16)
    ids = [tok[r][2 * ROWS :, :ROWS].astype(f32)[:1] for r in range(4)]
    ids = jnp.concatenate(ids + [jnp.zeros((4, ROWS), f32)], 0).astype(bf16)
    k_ref[OWN:, :] = jnp.concatenate([ids, jnp.zeros((8, QUARTER - ROWS), bf16)], 1)


def split_ids(kva, kvb):
    ids_a = kva[OWN:, :ROWS].astype(f32)
    ids_b = kvb[OWN:, :ROWS].astype(f32)
    keys = jnp.concatenate(
        [ids_a[r : r + 1] for r in range(4)] + [ids_b[r : r + 1] for r in range(4)], 1
    )
    return ids_a.T, keys


def all_keys(pair, key_ref, value_ref):
    for n in range(2):
        key_ref[OWN * n : OWN * (n + 1), :] = pair[2 * n][:OWN, :]
        value_ref[OWN * n : OWN * (n + 1), :] = pair[2 * n + 1][...]


def attend_body(pos, q_ref, *refs):
    pair, (mixed_ref, state_ref, key_ref, value_ref) = refs[:4], refs[4:]
    cols, keys = split_ids(pair[0], pair[2])
    all_keys(pair, key_ref, value_ref)
    lane = lax.broadcasted_iota(jnp.int32, (ROWS, 64), 1)
    for r in range(4):
        rows = slice(ROWS * r, ROWS * (r + 1))
        hidden = keys > cols[:, r : r + 1]
        heads, lse = [], jnp.zeros((ROWS, 64), f32)
        for h in range(3):
            at = slice(64 * h, 64 * h + 64)
            query = q_ref[rows, at]
            scores = dot_t(query, key_ref[:, at])
            scores = jnp.where(hidden, NEGATIVE, scores)
            top = jnp.max(scores, -1, keepdims=True)
            weights = jnp.exp(scores - top)
            total = jnp.sum(weights, -1, keepdims=True)
            low = weights.astype(bf16)
            out = dot(low, value_ref[:, at])
            heads.append(out * (1.0 / total))
            lse = jnp.where(lane == h, top + jnp.log(total), lse)
        mixed = jnp.concatenate(heads, 1)
        mixed_ref[rows, :] = mixed.astype(bf16)
        state_ref[rows, :] = jnp.concatenate([mixed, lse], 1)


def feed_body(pos, *refs):
    tok, mixed, own, oth = refs[0:4], refs[4:8], refs[8:12], refs[12:16]
    vec_ref = refs[16]
    mid_ref, d0, d1, d2, d3, g0, g1, g2, g3, sums_ref, wok_ref, send_ref, own_ref = refs[17:30]
    wo, wu, wd, hat_ref, n2_ref, act_ref, wg = refs[30:]
    s, k, c = pos[0], pos[1], pos[2]
    for m in range(4):
        z = s ^ m
        for half, src in ((c, own[m]), (1 - c, oth[m])):
            at = pl.ds(pl.multiple_of(z * QUARTER + half * HALF, 32), HALF)
            wo[at, :] = src[:HALF, :]
            wu[at, :] = src[HALF : 2 * HALF, :]
            wd[at, :] = src[2 * HALF :, :]
    wok_ref[...] = wo[pl.ds(pl.multiple_of(k * QUARTER, 64), QUARTER), :]
    bias_out, gain, shift = vec_ref[2:3, :], vec_ref[3:4, :], vec_ref[4:5, :]
    bias_up = vec_ref[6:7, :]
    attended = bias_out
    for m in range(4):
        block = jnp.concatenate(
            [mixed[m][ROWS * (r ^ m) : ROWS * (r ^ m) + ROWS, :] for r in range(4)], 0
        )
        at = pl.ds(pl.multiple_of((k ^ m) * QUARTER, 64), QUARTER)
        attended = attended + dot(block, wo[at, :])
    for r in range(4):
        rows = slice(ROWS * r, ROWS * (r + 1))
        middle = tok[r][:ROWS, :].astype(f32) + attended[rows]
        if r == 0:
            mid_ref[...] = middle
        hat, _ = normal(middle)
        hat_ref[rows, :] = hat
        n2_ref[rows, :] = (hat * gain + shift).astype(bf16)
    pre_act = dot(n2_ref[...], wu[...]) + bias_up
    cdf = 0.5 * (1.0 + lax.erf(pre_act * (1.0 / math.sqrt(2.0))))
    act_ref[...] = (pre_act * cdf).astype(bf16)
    slope = cdf + pre_act * jnp.exp(-0.5 * pre_act * pre_act) * (1.0 / math.sqrt(2.0 * math.pi))
    grads = jnp.concatenate([ref[ROWS : 2 * ROWS, :] for ref in tok], 0)
    pre = (dot_t(grads, wd[...]) * slope).astype(bf16)
    back = dot_t(pre, wu[...])
    sums = [
        jnp.sum(back * hat_ref[...], 0, keepdims=True),
        jnp.sum(back, 0, keepdims=True),
        jnp.sum(pre.astype(f32), 0, keepdims=True),
    ]
    sums_ref[...] = jnp.concatenate(sums + [jnp.zeros((5, WIDTH), f32)], 0)
    g0[...] = back[:ROWS]
    for r, ref in ((1, g1), (2, g2), (3, g3)):
        ref[...] = back[ROWS * r : ROWS * (r + 1)].astype(bf16)
    down = dot(act_ref[...], wd[...])
    d0[...] = down[:ROWS]
    for r, ref in ((1, d1), (2, d2), (3, d3)):
        ref[...] = down[ROWS * r : ROWS * (r + 1)].astype(bf16)
    for part in range(2):
        wg[...] = t_dot(act_ref[...], grads) if part == 0 else t_dot(n2_ref[...], pre)
        rows = slice(HALF * part, HALF * part + HALF)
        for m in range(4):
            z = s ^ m
            at = pl.ds(pl.multiple_of(z * QUARTER + c * HALF, 32), HALF)
            own_ref[m, rows, :] = wg[at, :]
            at = pl.ds(pl.multiple_of(z * QUARTER + (1 - c) * HALF, 32), HALF)
            send_ref[m, rows, :] = wg[at, :].astype(bf16)


def feed_halves_body(pos, own_ref, got_ref, o0, o1, o2, o3):
    for m, out in enumerate((o0, o1, o2, o3)):
        out[...] = (own_ref[m] + got_ref[m].astype(f32)).astype(out.dtype)


def add_body(pos, o0, r1, r2, r3, out):
    total = o0[...] + r1[...].astype(f32) + r2[...].astype(f32) + r3[...].astype(f32)
    out[...] = total.astype(out.dtype)


def middle_body(pos, g0, r1, r2, r3, mid_ref, tok_ref, vec_ref, gm_ref, ga_ref):
    err = g0[...] + r1[...].astype(f32) + r2[...].astype(f32) + r3[...].astype(f32)
    hat, rstd = normal(mid_ref[...])
    grad = tok_ref[ROWS : 2 * ROWS, :].astype(f32) + norm_back(err, vec_ref[3:4, :], hat, rstd)
    gm_ref[...] = grad
    ga_ref[...] = grad.astype(bf16)


def attend_grad_body(pos, a0, a1, a2, a3, wok, q_ref, *refs):
    pair, state_ref, outs = refs[:4], refs[4], refs[5:]
    dq_ref, own_ref, send_k, send_v, p_ref, ds_ref, key_ref, value_ref = outs
    cols, keys = split_ids(pair[0], pair[2])
    all_keys(pair, key_ref, value_ref)
    grads = jnp.concatenate([ref[...] for ref in (a0, a1, a2, a3)], 0)
    grad_mixed = dot_t(grads, wok[...]).astype(bf16)
    dq = []
    for h in range(3):
        at = slice(64 * h, 64 * h + 64)
        at_v = slice(QUARTER + 64 * h, QUARTER + 64 * h + 64)
        query, grad = q_ref[:, at], grad_mixed[:, at]
        grad_q = []
        for r in range(4):
            rows = slice(ROWS * r, ROWS * (r + 1))
            hidden = keys > cols[:, r : r + 1]
            g = grad[rows]
            inner = jnp.sum(g.astype(f32) * state_ref[rows, at], -1, keepdims=True)
            lse = state_ref[rows, QUARTER + h : QUARTER + h + 1]
            scores = dot_t(query[rows], key_ref[:, at])
            probs = jnp.exp(jnp.where(hidden, NEGATIVE, scores) - lse)
            slopes = dot_t(g, value_ref[:, at])
            ds = (probs * (slopes - inner)).astype(bf16)
            p_ref[rows, :] = probs.astype(bf16)
            ds_ref[rows, :] = ds
            grad_q.append(dot(ds, key_ref[:, at]))
        dq.append(jnp.concatenate(grad_q, 0))
        dk = t_dot(ds_ref[...], query)
        dv = t_dot(p_ref[...], grad)
        own_ref[:, at] = dk[:OWN]
        own_ref[:, at_v] = dv[:OWN]
        send_k[:, at] = dk[OWN:].astype(bf16)
        send_v[:, at] = dv[OWN:].astype(bf16)
    dq_ref[...] = (jnp.concatenate(dq, 1) * 0.125).astype(bf16)


def project_grad_body(pos, *refs):
    mixed, ga = refs[0:4], refs[4:8]
    normed, dq, kv_own, got_k, got_v = refs[8:13]
    send_ref, own_ref, gp, wg, gk = refs[13:]
    s, k, c = pos[0], pos[1], pos[2]
    gp[:, :QUARTER] = dq[...]
    got = jnp.concatenate([got_k[...], got_v[...]], 1).astype(f32)
    gp[:, QUARTER:] = (kv_own[...] + got).astype(bf16)
    wg[:, : 3 * QUARTER] = t_dot(normed[...], gp[...])
    for q in range(4):

        @pl.when(k == q)
        def _():
            for r in range(4):
                gk[ROWS * r : ROWS * (r + 1), :] = ga[r][:, QUARTER * q : QUARTER * (q + 1)]

    for m in range(4):
        block = jnp.concatenate(
            [mixed[m][ROWS * (r ^ m) : ROWS * (r ^ m) + ROWS, :] for r in range(4)], 0
        )
        at = pl.ds(pl.multiple_of((k ^ m) * QUARTER, 64), QUARTER)
        wg[at, 3 * QUARTER :] = t_dot(block, gk[...])
    for m in range(4):
        z = s ^ m
        at = pl.ds(pl.multiple_of(z * QUARTER + c * HALF, 32), HALF)
        own_ref[m] = wg[at, :]
        at = pl.ds(pl.multiple_of(z * QUARTER + (1 - c) * HALF, 32), HALF)
        send_ref[m] = wg[at, :].astype(bf16)


def normed_grad_body(pos, *refs):
    tok, (gp, w_ref, ga_ref, sums_ref) = refs[0:4], refs[4:8]
    small_ref, g0, g1, g2, g3 = refs[8:]
    k = pos[1]
    back = dot_t(gp[...], w_ref[...])
    hat = jnp.concatenate([normal(tok[r][:ROWS, :].astype(f32))[0] for r in range(4)], 0)
    ln1_gain = jnp.sum(back * hat, 0, keepdims=True)
    ln1_bias = jnp.sum(back, 0, keepdims=True)
    g0[...] = back[:ROWS]
    for r, ref in ((1, g1), (2, g2), (3, g3)):
        ref[...] = back[ROWS * r : ROWS * (r + 1)].astype(bf16)
    gp_sums = jnp.sum(gp[...].astype(f32), 0, keepdims=True)
    out_bias = jnp.sum(ga_ref[...].astype(f32), 0, keepdims=True)
    down_bias = jnp.sum(tok[0][ROWS : 2 * ROWS, :].astype(f32), 0, keepdims=True)
    for z in range(4):
        at = slice(QUARTER * z, QUARTER * (z + 1))
        here = jnp.where(k == z, 1.0, 0.0).astype(f32)
        row0 = [ln1_gain[:, at], ln1_bias[:, at], gp_sums[:, :QUARTER] * here]
        row0 = jnp.concatenate(row0 + [gp_sums[:, 2 * QUARTER :] * here], 1)
        row1 = [out_bias[:, at], sums_ref[0:1, at], sums_ref[1:2, at], down_bias[:, at]]
        row1 = jnp.concatenate(row1, 1)
        row2 = jnp.concatenate([sums_ref[2:3, at], jnp.zeros((1, 3 * QUARTER), f32)], 1)
        small_ref[z] = jnp.concatenate([row0, row1, row2, jnp.zeros((5, WIDTH), f32)], 0)


def last_halves_body(pos, own_ref, small_ref, got, o0, o1, o2, o3):
    s = pos[0]
    for m, out in enumerate((o0, o1, o2, o3)):
        out[:HALF, :] = (own_ref[m] + got[m].astype(f32)).astype(out.dtype)
        out[HALF:, :] = small_ref[s ^ m].astype(out.dtype)


def rows_body(pos, g0, r1, r2, r3, d0, s1, s2, s3, tok_ref, gm_ref, mid_ref, vec_ref, *outs):
    grad_ref, out_ref = outs
    err = g0[...] + r1[...].astype(f32) + r2[...].astype(f32) + r3[...].astype(f32)
    hat, rstd = normal(tok_ref[:ROWS, :].astype(f32))
    grad_ref[0] = gm_ref[...] + norm_back(err, vec_ref[0:1, :], hat, rstd)
    total = d0[...] + s1[...].astype(f32) + s2[...].astype(f32) + s3[...].astype(f32)
    out_ref[0] = (mid_ref[...] + total + vec_ref[5:6, :]).astype(bf16)


def feed_join_body(pos, *refs):
    own, oth = refs[0:4], refs[4:8]
    down_ref, up_ref, sc = refs[8:]
    k, c = pos[1], pos[2]
    for m in range(4):
        sc[c, k ^ m] = own[m][...]
        sc[1 - c, k ^ m] = oth[m][...]
    for q in range(4):
        for half in range(2):
            at = QUARTER * q + HALF * half
            down_ref[at : at + HALF, :] = sc[half, q, :HALF, :].astype(f32)
            rows = slice(HALF * half, HALF * half + HALF)
            for p in range(4):
                cols = slice(WIDTH * p + QUARTER * q, WIDTH * p + QUARTER * (q + 1))
                piece = sc[half, q, HALF:, QUARTER * p : QUARTER * (p + 1)]
                up_ref[rows, cols] = piece.astype(f32)


def last_join_body(pos, *refs):
    own, oth = refs[0:4], refs[4:8]
    qkv_ref, out_ref, up_ref, sc = refs[8], refs[9], refs[18], refs[19]
    vec_refs = refs[10:18]
    k, c = pos[1], pos[2]
    for m in range(4):
        sc[c, k ^ m] = own[m][...]
        sc[1 - c, k ^ m] = oth[m][...]
    total = jnp.zeros((8, WIDTH), f32)
    ups = []
    for q in range(4):
        small = sc[0, q, HALF:, :].astype(f32) + sc[1, q, HALF:, :].astype(f32)
        total = total + small
        ups.append(small[2:3, :QUARTER])
        for half in range(2):
            rows = slice(HALF * half, HALF * half + HALF)
            for p in range(3):
                cols = slice(WIDTH * p + QUARTER * q, WIDTH * p + QUARTER * (q + 1))
                piece = sc[half, q, :HALF, QUARTER * p : QUARTER * (p + 1)]
                qkv_ref[rows, cols] = piece.astype(f32)
            out_ref[rows, QUARTER * q : QUARTER * (q + 1)] = sc[
                half, q, :HALF, 3 * QUARTER :
            ].astype(f32)
    for n, ref in enumerate(vec_refs):
        row = total[n // 4 : n // 4 + 1, QUARTER * (n % 4) : QUARTER * (n % 4 + 1)]
        ref[...] = row.reshape(QUARTER)
    up_ref[...] = jnp.concatenate(ups, 1).reshape(WIDTH)


def shards(
    tokens,
    block_ids,
    ln1_gain,
    ln1_bias,
    w_qkv,
    q_bias,
    v_bias,
    w_out,
    out_bias,
    ln2_gain,
    ln2_bias,
    w_up,
    up_bias,
    w_down,
    down_bias,
    cotangent,
):
    seq = lax.axis_index("seq")
    ctx = lax.axis_index("ctx")
    k, core = ctx // 2, ctx % 2
    pos = jnp.stack([seq, k, core]).astype(jnp.int32)

    small = [ln1_gain, ln1_bias, q_bias, v_bias, out_bias, ln2_gain, ln2_bias, down_bias, up_bias]
    piece_qkv, mate_qkv, pack, rest, mate_rest = run(
        pack_body,
        pos,
        [w_qkv, tokens, cotangent, w_out, w_up, w_down, block_ids, *small],
        [((HALF + 16, 3 * QUARTER), bf16)] * 2
        + [((2 * ROWS + 8, WIDTH), bf16)]
        + [((3 * HALF, WIDTH), bf16)] * 2,
        [((2, HALF, 3 * WIDTH), bf16), ((2, HALF, 4 * WIDTH), bf16)],
        hbm=range(6),
        sems=10,
        limit=60,
    )
    got_qkv = seq_gather(piece_qkv)
    tok = chip_gather(pack)
    got_rest = seq_gather(rest)
    oth_qkv = [mate_qkv] + [core_swap(block) for block in got_qkv[1:]]
    third = (OWN, QUARTER)
    query, *pair, normed, vec, weight_qkv = run(
        qkv_body,
        pos,
        [*tok, *got_qkv, *oth_qkv],
        [(third, bf16), ((OWN + 8, QUARTER), bf16), (third, bf16)]
        + [((OWN, WIDTH), bf16), ((8, WIDTH), f32), ((WIDTH, 3 * QUARTER), bf16)],
        [((4, 16, 3 * QUARTER), f32)],
    )
    pair = [*pair, *[core_swap(x) for x in pair]]
    mixed_own, state = run(
        attend_body,
        pos,
        [query, *pair],
        [((OWN, QUARTER), bf16), ((OWN, 256), f32)],
        [((2 * OWN, QUARTER), bf16)] * 2,
    )
    mixed = chip_gather(mixed_own)
    got_rest = lax.optimization_barrier((*got_rest, *mixed[1:]))[:4]
    oth_rest = [mate_rest] + [core_swap(block) for block in got_rest[1:]]
    big, block, piece = (OWN, WIDTH), (ROWS, WIDTH), (QUARTER, WIDTH)
    mid, d0, d1, d2, d3, g0, g1, g2, g3, sums, w_out_k, feed_send, feed_own = run(
        feed_body,
        pos,
        [*tok, *mixed, *got_rest, *oth_rest, vec],
        [(block, f32)]
        + [(block, f32), (block, bf16), (block, bf16), (block, bf16)] * 2
        + [((8, WIDTH), f32), (piece, bf16), ((4, *piece), bf16), ((4, *piece), f32)],
        [((WIDTH, WIDTH), bf16)] * 3 + [(big, f32), (big, bf16), (big, bf16), ((WIDTH, WIDTH), f32)],
        limit=40,
    )
    got_g = [chip_swap(g, m) for m, g in ((1, g1), (2, g2), (3, g3))]
    feed_got = core_swap(feed_send)
    h0, h1, h2, h3 = run(
        feed_halves_body, pos, [feed_own, feed_got], [(piece, f32)] + [(piece, bf16)] * 3
    )
    grad_mid, grad_att = run(
        middle_body, pos, [after(g0, h0), *got_g, mid, tok[0], vec], [(block, f32), (block, bf16)]
    )
    ga = chip_gather(grad_att)
    feed_terms = [seq_swap(h, m) for m, h in ((1, h1), (2, h2), (3, h3))]
    dq, kv_own, *pair_send = run(
        attend_grad_body,
        pos,
        [*ga, w_out_k, query, *pair, state],
        [(third, bf16), ((OWN, 2 * QUARTER), f32)] + [(third, bf16)] * 2,
        [((OWN, 2 * OWN), bf16)] * 2 + [((2 * OWN, QUARTER), bf16)] * 2,
    )
    pair_send[0], *feed_terms[1:] = lax.optimization_barrier((pair_send[0], *feed_terms[1:]))
    pair_got = [core_swap(x) for x in pair_send]
    lpiece = (HALF + 8, WIDTH)
    last_send, last_own, grad_proj = run(
        project_grad_body,
        pos,
        [*mixed, *ga, normed, dq, kv_own, *pair_got],
        [((4, HALF, WIDTH), bf16), ((4, HALF, WIDTH), f32), ((OWN, 3 * QUARTER), bf16)],
        [((WIDTH, WIDTH), f32), ((OWN, QUARTER), bf16)],
    )
    last_send, feed_terms[0] = lax.optimization_barrier((last_send, feed_terms[0]))
    last_got = core_swap(last_send)
    got_d = [chip_swap(after(d, grad_proj), m) for m, d in ((1, d1), (2, d2), (3, d3))]
    last_small, e0, e1, e2, e3 = run(
        normed_grad_body,
        pos,
        [*tok, grad_proj, weight_qkv, ga[0], sums],
        [((4, 8, WIDTH), f32), (block, f32)] + [(block, bf16)] * 3,
    )
    l0, l1, l2, l3 = run(
        last_halves_body,
        pos,
        [last_own, last_small, last_got],
        [(lpiece, f32)] + [(lpiece, bf16)] * 3,
    )
    last_terms = [seq_swap(h, m) for m, h in ((1, l1), (2, l2), (3, l3))]
    (feed_sum,) = run(add_body, pos, [after(h0, l1), *feed_terms], [(piece, bf16)])
    feed_blocks = chip_gather(feed_sum)
    l0, *got_d = lax.optimization_barrier((l0, *got_d))
    (last_sum,) = run(add_body, pos, [l0, *last_terms], [(lpiece, bf16)], cost=2)
    last_blocks = chip_gather(last_sum)
    got_e = [chip_swap(after(e, last_sum), m) for m, e in ((1, e1), (2, e2), (3, e3))]
    feed_oth = [core_swap(after(b, last_sum)) for b in feed_blocks]
    grad_w_down, grad_w_up = run(
        feed_join_body,
        pos,
        [after(feed_blocks[0], last_sum), *feed_blocks[1:], *feed_oth],
        [((WIDTH, WIDTH), f32), ((QUARTER, 4 * WIDTH), f32)],
        [((2, 4, QUARTER, WIDTH), bf16)],
    )
    input_grad, result = run(
        rows_body,
        pos,
        [after(e0, grad_w_up), *got_e, d0, *got_d, tok[0], grad_mid, mid, vec],
        [((1, *block), f32), ((1, *block), bf16)],
    )
    last_oth = [core_swap(b) for b in last_blocks]
    grad_w_qkv, grad_w_out, *g, g_up = run(
        last_join_body,
        pos,
        [*last_blocks, *last_oth],
        [((QUARTER, 3 * WIDTH), f32), ((QUARTER, WIDTH), f32)]
        + [((QUARTER,), f32)] * 8
        + [((WIDTH,), f32)],
        [((2, 4, HALF + 8, WIDTH), bf16)],
    )
    return (
        result,
        input_grad,
        g[0],
        g[1],
        grad_w_qkv,
        g[2],
        g[3],
        grad_w_out,
        g[4],
        g[5],
        g[6],
        grad_w_up,
        g_up,
        grad_w_down,
        g[7],
    )


def solution(mesh):
    placed = (
        P("seq", "ctx", None),
        P("seq", "ctx"),
        P("seq"),
        P("seq"),
        P("seq", None),
        P("seq"),
        P("seq"),
        P("seq", None),
        P("seq"),
        P("seq"),
        P("seq"),
        P("seq", None),
        P("seq"),
        P("seq", None),
        P("seq"),
        P("seq", "ctx", None),
    )
    return jax.shard_map(
        shards if mesh.shape["ctx"] == 8 and mesh.shape["seq"] == 4 else shards_general,
        mesh=mesh,
        in_specs=placed,
        out_specs=(
            P("seq", "ctx", None),
            P("seq", "ctx", None),
            P("seq"),
            P("seq"),
            P("seq", None),
            P("seq"),
            P("seq"),
            P("seq", None),
            P("seq"),
            P("seq"),
            P("seq"),
            P("seq", None),
            P("seq"),
            P("seq", None),
            P("seq"),
        ),
        check_vma=False,
    )
```

```python
import math

import jax
import jax.numpy as jnp
from jax import lax
from jax.experimental import pallas as pl
from jax.experimental.pallas import tpu as pltpu
from jax.sharding import PartitionSpec as P

HEADS = 12


EPSILON = 1e-06
NEGATIVE = -1e30


def layer_norm(values, gain, shift):
    center = values - jnp.mean(values, -1, keepdims=True)
    spread = jnp.mean(center * center, -1, keepdims=True)
    return center * lax.rsqrt(spread + EPSILON) * gain + shift


def block_rows(count):
    return math.gcd(count, 512)


def masked_scores(query_heads, key_heads, query_ids, key_ids, scale):
    raw = (
        jnp.einsum("qhd,khd->hqk", query_heads, key_heads, preferred_element_type=jnp.float32)
        * scale
    )
    allowed = key_ids[None, None, :] <= query_ids[None, :, None]
    return (raw, allowed)


def attend_forward(query_heads, query_ids, keys_all, values_all, ids_all, scale):
    tok_rows, heads, head_dim = query_heads.shape
    total_keys = keys_all.shape[0]
    step = block_rows(total_keys)
    blocks = total_keys // step

    def attend_visit(carry, inputs):
        running, total, accum = carry
        key_block, value_block, id_block = inputs
        raw, allowed = masked_scores(query_heads, key_block, query_ids, id_block, scale)
        masked = jnp.where(allowed, raw, NEGATIVE)
        new_top = jnp.maximum(running, jnp.max(masked, -1))
        weights = jnp.where(allowed, jnp.exp(masked - new_top[..., None]), 0.0)
        factor = jnp.exp(running - new_top)
        total = total * factor + jnp.sum(weights, -1)
        accum = accum * factor[..., None] + jnp.einsum(
            "hqk,khd->hqd",
            weights.astype(jnp.bfloat16),
            value_block,
            preferred_element_type=jnp.float32,
        )
        return ((new_top, total, accum), None)

    start_state = (
        jnp.full((heads, tok_rows), NEGATIVE, jnp.float32),
        jnp.zeros((heads, tok_rows), jnp.float32),
        jnp.zeros((heads, tok_rows, head_dim), jnp.float32),
    )
    (running, total, accum), _ = lax.scan(
        attend_visit,
        start_state,
        (
            keys_all.reshape(blocks, step, heads, head_dim),
            values_all.reshape(blocks, step, heads, head_dim),
            ids_all.reshape(blocks, step),
        ),
    )
    output_heads = jnp.transpose(accum / total[..., None], (1, 0, 2))
    return (output_heads, running + jnp.log(total))


def query_gradient(
    query_heads, grad_heads, query_ids, keys_all, values_all, ids_all, logsum, inner, scale
):
    tok_rows, heads, head_dim = query_heads.shape
    total_keys = keys_all.shape[0]
    step = block_rows(total_keys)
    blocks = total_keys // step

    def query_visit(accum, inputs):
        key_block, value_block, id_block = inputs
        raw, allowed = masked_scores(query_heads, key_block, query_ids, id_block, scale)
        probs = jnp.where(allowed, jnp.exp(raw - logsum[..., None]), 0.0)
        grad_probs = jnp.einsum(
            "qhd,khd->hqk", grad_heads, value_block, preferred_element_type=jnp.float32
        )
        grad_scores = (probs * (grad_probs - inner[..., None])).astype(jnp.bfloat16)
        accum = accum + jnp.einsum(
            "hqk,khd->qhd", grad_scores, key_block, preferred_element_type=jnp.float32
        )
        return (accum, None)

    accum, _ = lax.scan(
        query_visit,
        jnp.zeros((tok_rows, heads, head_dim), jnp.float32),
        (
            keys_all.reshape(blocks, step, heads, head_dim),
            values_all.reshape(blocks, step, heads, head_dim),
            ids_all.reshape(blocks, step),
        ),
    )
    return accum * scale


def pair_grads(
    query_heads, grad_heads, query_ids, logsum, inner, key_heads, value_heads, key_ids, scale
):
    raw, allowed = masked_scores(query_heads, key_heads, query_ids, key_ids, scale)
    probs = jnp.where(allowed, jnp.exp(raw - logsum[..., None]), 0.0)
    grad_probs = jnp.einsum(
        "qhd,khd->hqk", grad_heads, value_heads, preferred_element_type=jnp.float32
    )
    grad_scores = (probs * (grad_probs - inner[..., None])).astype(jnp.bfloat16)
    grad_keys = (
        jnp.einsum("hqk,qhd->khd", grad_scores, query_heads, preferred_element_type=jnp.float32)
        * scale
    )
    grad_values = jnp.einsum(
        "hqk,qhd->khd", probs.astype(jnp.bfloat16), grad_heads, preferred_element_type=jnp.float32
    )
    return (grad_keys, grad_values)


def shards_general(
    tokens,
    block_ids,
    ln1_gain,
    ln1_bias,
    w_qkv,
    q_bias,
    v_bias,
    w_out,
    out_bias,
    ln2_gain,
    ln2_bias,
    w_up,
    up_bias,
    w_down,
    down_bias,
    cotangent,
):
    gathered = (
        lax.all_gather(ln1_gain, "seq", axis=0, tiled=True),
        lax.all_gather(ln1_bias, "seq", axis=0, tiled=True),
        lax.all_gather(w_qkv, "seq", axis=0, tiled=True),
        lax.all_gather(q_bias, "seq", axis=0, tiled=True),
        lax.all_gather(v_bias, "seq", axis=0, tiled=True),
        lax.all_gather(w_out, "seq", axis=0, tiled=True),
        lax.all_gather(out_bias, "seq", axis=0, tiled=True),
        lax.all_gather(ln2_gain, "seq", axis=0, tiled=True),
        lax.all_gather(ln2_bias, "seq", axis=0, tiled=True),
        lax.all_gather(w_up, "seq", axis=0, tiled=True),
        lax.all_gather(up_bias, "seq", axis=0, tiled=True),
        lax.all_gather(w_down, "seq", axis=0, tiled=True),
        lax.all_gather(down_bias, "seq", axis=0, tiled=True),
    )
    attention_part = gathered[:7]
    feed_part = gathered[7:]
    gain_one, shift_one, weight_qkv, bias_query, bias_value, weight_out, bias_out = attention_part
    width = weight_out.shape[0]
    heads = HEADS
    head_dim = width // heads
    scale = 1.0 / math.sqrt(head_dim)
    inputs = tokens[0].astype(jnp.float32)
    tok_rows = inputs.shape[0]
    own_ids = block_ids[0]
    gain_one_f = gain_one.astype(jnp.float32)
    shift_one_f = shift_one.astype(jnp.float32)
    normed_one, norm_one_pull = jax.vjp(layer_norm, inputs, gain_one_f, shift_one_f)
    normed_low = normed_one.astype(jnp.bfloat16)
    qkv_bias = jnp.concatenate(
        [
            bias_query.astype(jnp.float32),
            jnp.zeros((width,), jnp.float32),
            bias_value.astype(jnp.float32),
        ]
    )
    projected = (
        jnp.dot(normed_low, weight_qkv, preferred_element_type=jnp.float32) + qkv_bias
    ).astype(jnp.bfloat16)
    query_low = projected[:, :width]
    key_low = projected[:, width : 2 * width]
    value_low = projected[:, 2 * width :]
    ids_all = lax.all_gather(block_ids, "ctx", axis=1, tiled=True)[0]
    keys_all, values_all = (
        lax.all_gather(key_low, "ctx", axis=0, tiled=True),
        lax.all_gather(value_low, "ctx", axis=0, tiled=True),
    )
    query_heads = query_low.reshape(tok_rows, heads, head_dim)
    output_heads, logsum = attend_forward(
        query_heads, own_ids, keys_all, values_all, ids_all, scale
    )
    mixed_low = output_heads.reshape(tok_rows, width).astype(jnp.bfloat16)
    attended = jnp.dot(mixed_low, weight_out, preferred_element_type=jnp.float32) + bias_out.astype(
        jnp.float32
    )
    middle = inputs + attended
    gain_two, shift_two, weight_up, bias_up, weight_down, bias_down = feed_part
    gain_two_f = gain_two.astype(jnp.float32)
    shift_two_f = shift_two.astype(jnp.float32)
    normed_two, norm_two_pull = jax.vjp(layer_norm, middle, gain_two_f, shift_two_f)
    normed_two_low = normed_two.astype(jnp.bfloat16)
    pre_act = jnp.dot(
        normed_two_low, weight_up, preferred_element_type=jnp.float32
    ) + bias_up.astype(jnp.float32)
    activated, gelu_pull = jax.vjp(lambda values: jax.nn.gelu(values, approximate=False), pre_act)
    activated_low = activated.astype(jnp.bfloat16)
    result = (
        middle
        + jnp.dot(activated_low, weight_down, preferred_element_type=jnp.float32)
        + bias_down.astype(jnp.float32)
    )
    grad_out = cotangent[0]
    grad_out_f = grad_out.astype(jnp.float32)
    grad_weight_down = jnp.einsum(
        "tf,td->fd", activated_low, grad_out, preferred_element_type=jnp.float32
    )
    grad_bias_down = jnp.sum(grad_out_f, 0)
    grad_hidden = jnp.einsum("td,fd->tf", grad_out, weight_down, preferred_element_type=jnp.float32)
    grad_pre_low = gelu_pull(grad_hidden)[0].astype(jnp.bfloat16)
    grad_weight_up = jnp.einsum(
        "td,tf->df", normed_two_low, grad_pre_low, preferred_element_type=jnp.float32
    )
    grad_bias_up = jnp.sum(grad_pre_low.astype(jnp.float32), 0)
    grad_normed_two = jnp.einsum(
        "tf,df->td", grad_pre_low, weight_up, preferred_element_type=jnp.float32
    )
    grad_middle_part, grad_gain_two, grad_shift_two = norm_two_pull(grad_normed_two)
    grad_middle = grad_out_f + grad_middle_part
    grad_attended = grad_middle.astype(jnp.bfloat16)
    grad_weight_out = jnp.einsum(
        "td,te->de", mixed_low, grad_attended, preferred_element_type=jnp.float32
    )
    grad_bias_out = jnp.sum(grad_attended.astype(jnp.float32), 0)
    grad_mixed = jnp.einsum(
        "te,de->td", grad_attended, weight_out, preferred_element_type=jnp.float32
    ).astype(jnp.bfloat16)
    grad_heads = grad_mixed.reshape(tok_rows, heads, head_dim)
    inner = jnp.einsum("thd,thd->ht", grad_heads.astype(jnp.float32), output_heads)
    grad_query = query_gradient(
        query_heads, grad_heads, own_ids, keys_all, values_all, ids_all, logsum, inner, scale
    )
    step = block_rows(lax.axis_size("ctx") * tok_rows)
    blocks = lax.axis_size("ctx") * tok_rows // step
    key_part = keys_all.reshape(blocks, step, heads, head_dim)
    value_part = values_all.reshape(blocks, step, heads, head_dim)
    id_part = ids_all.reshape(blocks, step)

    def key_visit(carry, inputs):
        grad_keys, grad_values = pair_grads(
            query_heads, grad_heads, own_ids, logsum, inner, inputs[0], inputs[1], inputs[2], scale
        )
        joined = jnp.concatenate(
            [grad_keys.reshape(step, width), grad_values.reshape(step, width)], 1
        )
        return (carry, joined)

    _, terms = lax.scan(key_visit, jnp.zeros((), jnp.float32), (key_part, value_part, id_part))
    key_value_grads = lax.psum_scatter(
        terms.reshape(lax.axis_size("ctx") * tok_rows, 2 * width),
        "ctx",
        scatter_dimension=0,
        tiled=True,
    )
    grad_keys_all = key_value_grads[:, :width]
    grad_values_all = key_value_grads[:, width:]
    grad_query_low = grad_query.reshape(tok_rows, width).astype(jnp.bfloat16)
    grad_value_low = grad_values_all.astype(jnp.bfloat16)
    grad_projected = jnp.concatenate(
        [grad_query_low, grad_keys_all.astype(jnp.bfloat16), grad_value_low], 1
    )
    grad_weight_qkv = jnp.einsum(
        "td,te->de", normed_low, grad_projected, preferred_element_type=jnp.float32
    )
    grad_bias_query = jnp.sum(grad_query_low.astype(jnp.float32), 0)
    grad_bias_value = jnp.sum(grad_value_low.astype(jnp.float32), 0)
    grad_normed_one = jnp.einsum(
        "te,de->td", grad_projected, weight_qkv, preferred_element_type=jnp.float32
    )
    grad_input_part, grad_gain_one, grad_shift_one = norm_one_pull(grad_normed_one)
    input_grad = grad_middle + grad_input_part
    local_grads = (
        grad_gain_one,
        grad_shift_one,
        grad_weight_qkv,
        grad_bias_query,
        grad_bias_value,
        grad_weight_out,
        grad_bias_out,
        grad_gain_two,
        grad_shift_two,
        grad_weight_up,
        grad_bias_up,
        grad_weight_down,
        grad_bias_down,
    )
    shares = (
        lax.psum_scatter(
            local_grads[0].astype(jnp.bfloat16), "seq", scatter_dimension=0, tiled=True
        ).astype(jnp.float32),
        lax.psum_scatter(
            local_grads[1].astype(jnp.bfloat16), "seq", scatter_dimension=0, tiled=True
        ).astype(jnp.float32),
        lax.psum_scatter(
            local_grads[2].astype(jnp.bfloat16), "seq", scatter_dimension=0, tiled=True
        ).astype(jnp.float32),
        lax.psum_scatter(
            local_grads[3].astype(jnp.bfloat16), "seq", scatter_dimension=0, tiled=True
        ).astype(jnp.float32),
        lax.psum_scatter(
            local_grads[4].astype(jnp.bfloat16), "seq", scatter_dimension=0, tiled=True
        ).astype(jnp.float32),
        lax.psum_scatter(
            local_grads[5].astype(jnp.bfloat16), "seq", scatter_dimension=0, tiled=True
        ).astype(jnp.float32),
        lax.psum_scatter(
            local_grads[6].astype(jnp.bfloat16), "seq", scatter_dimension=0, tiled=True
        ).astype(jnp.float32),
        lax.psum_scatter(
            local_grads[7].astype(jnp.bfloat16), "seq", scatter_dimension=0, tiled=True
        ).astype(jnp.float32),
        lax.psum_scatter(
            local_grads[8].astype(jnp.bfloat16), "seq", scatter_dimension=0, tiled=True
        ).astype(jnp.float32),
        lax.psum_scatter(
            local_grads[9].astype(jnp.bfloat16), "seq", scatter_dimension=0, tiled=True
        ).astype(jnp.float32),
        lax.psum_scatter(
            local_grads[10].astype(jnp.bfloat16), "seq", scatter_dimension=0, tiled=True
        ).astype(jnp.float32),
        lax.psum_scatter(
            local_grads[11].astype(jnp.bfloat16), "seq", scatter_dimension=0, tiled=True
        ).astype(jnp.float32),
        lax.psum_scatter(
            local_grads[12].astype(jnp.bfloat16), "seq", scatter_dimension=0, tiled=True
        ).astype(jnp.float32),
    )
    totals = lax.psum(
        (
            shares[0],
            shares[1],
            shares[2],
            shares[3],
            shares[4],
            shares[5],
            shares[6],
            shares[7],
            shares[8],
            shares[9],
            shares[10],
            shares[11],
            shares[12],
        ),
        "ctx",
    )
    return (result.astype(jnp.bfloat16)[None], input_grad[None]) + tuple(totals)


QUARTER = 192
HALF = 96
ROWS = 128
WIDTH = 768
OWN = 512
f32, bf16 = jnp.float32, jnp.bfloat16


def core_swap(values):
    return lax.ppermute(values, "ctx", [(i, i ^ 1) for i in range(8)])


def chip_swap(values, mask):
    return lax.ppermute(values, "ctx", [(i, i ^ (2 * mask)) for i in range(8)])


def seq_swap(values, mask):
    return lax.ppermute(values, "seq", [(i, i ^ mask) for i in range(4)])


def chip_gather(values):
    return [values] + [chip_swap(values, m) for m in (1, 2, 3)]


def seq_gather(values):
    return [values] + [seq_swap(values, m) for m in (1, 2, 3)]


def after(values, *earlier):
    return lax.optimization_barrier((values, *earlier))[0]


def run(body, pos, args, outs, scratch=(), hbm=(), sems=0, limit=24, cost=0.001):
    vmem = pl.BlockSpec(memory_space=pltpu.VMEM)
    whole = pl.BlockSpec(memory_space=pl.ANY)
    scratch_shapes = [pltpu.VMEM(shape, kind) for shape, kind in scratch]
    if sems:
        scratch_shapes.append(pltpu.SemaphoreType.DMA((sems,)))
    return pl.pallas_call(
        body,
        out_shape=[jax.ShapeDtypeStruct(shape, kind) for shape, kind in outs],
        in_specs=[pl.BlockSpec(memory_space=pltpu.SMEM)]
        + [whole if n in hbm else vmem for n in range(len(args))],
        out_specs=[vmem] * len(outs),
        scratch_shapes=scratch_shapes,
        compiler_params=pltpu.CompilerParams(vmem_limit_bytes=limit << 20),
        cost_estimate=pl.CostEstimate(
            flops=int(cost * 524288000), bytes_accessed=1000, transcendentals=1
        ),
    )(pos, *args)


def dot(left, right):
    return lax.dot_general(left, right, (((1,), (0,)), ((), ())), preferred_element_type=f32)


def dot_t(left, right):
    return lax.dot_general(left, right, (((1,), (1,)), ((), ())), preferred_element_type=f32)


def t_dot(left, right):
    return lax.dot_general(left, right, (((0,), (0,)), ((), ())), preferred_element_type=f32)


def normal(values):
    center = values - jnp.mean(values, -1, keepdims=True)
    rstd = lax.rsqrt(jnp.mean(center * center, -1, keepdims=True) + EPSILON)
    return center * rstd, rstd


def norm_back(err, gain, hat, rstd):
    scaled = err * gain
    return rstd * (
        scaled
        - jnp.mean(scaled, -1, keepdims=True)
        - hat * jnp.mean(scaled * hat, -1, keepdims=True)
    )


def pack_body(pos, w_ref, tok_ref, cot_ref, wo_ref, wu_ref, wd_ref, ids_ref, *refs):
    small, up_ref = refs[:8], refs[8]
    piece_ref, mate_ref, pack_ref, rest_ref, rest_mate, w_rows, up_rows, sem = refs[9:]
    k, c = pos[1], pos[2]
    copies = [
        pltpu.make_async_copy(tok_ref.at[0], pack_ref.at[pl.ds(0, ROWS), :], sem.at[0]),
        pltpu.make_async_copy(cot_ref.at[0], pack_ref.at[pl.ds(ROWS, ROWS), :], sem.at[1]),
    ]
    for n, (half, dst) in enumerate(((c, rest_ref), (1 - c, rest_mate))):
        rows = pl.ds(pl.multiple_of(half * HALF, 32), HALF)
        down_rows = pl.ds(pl.multiple_of(k * QUARTER + half * HALF, 32), HALF)
        out_part, down_part = dst.at[pl.ds(0, HALF), :], dst.at[pl.ds(2 * HALF, HALF), :]
        copies += [
            pltpu.make_async_copy(w_ref.at[rows, :], w_rows.at[n], sem.at[2 + 4 * n]),
            pltpu.make_async_copy(wu_ref.at[rows, :], up_rows.at[n], sem.at[3 + 4 * n]),
            pltpu.make_async_copy(wo_ref.at[rows, :], out_part, sem.at[4 + 4 * n]),
            pltpu.make_async_copy(wd_ref.at[down_rows, :], down_part, sem.at[5 + 4 * n]),
        ]
    for copy in copies:
        copy.start()
    up = up_ref[...].astype(f32).reshape(1, WIDTH)
    part = jnp.zeros((1, QUARTER), f32)
    for q in range(4):
        part = jnp.where(k == q, up[:, QUARTER * q : QUARTER * (q + 1)], part)
    vecs = [ref[...].astype(f32).reshape(1, QUARTER) for ref in small] + [part]
    lines = [jnp.concatenate(vecs[3 * n : 3 * n + 3], 1) for n in range(3)]
    lines = jnp.concatenate(lines + [jnp.zeros((13, 3 * QUARTER), f32)], 0)
    piece_ref[HALF:, :] = lines.astype(bf16)
    ids = jnp.concatenate([ids_ref[...].astype(f32), jnp.zeros((1, WIDTH - ROWS), f32)], 1)
    pack_ref[2 * ROWS :, :] = jnp.concatenate([ids, jnp.zeros((7, WIDTH), f32)], 0).astype(bf16)
    for copy in copies:
        copy.wait()
    for q in range(4):

        @pl.when(k == q)
        def _():
            for p in range(4):
                at = WIDTH * p + QUARTER * q
                cols = slice(QUARTER * p, QUARTER * (p + 1))
                if p < 3:
                    piece_ref[:HALF, cols] = w_rows[0, :, at : at + QUARTER]
                    mate_ref[:HALF, cols] = w_rows[1, :, at : at + QUARTER]
                rest_ref[HALF : 2 * HALF, cols] = up_rows[0, :, at : at + QUARTER]
                rest_mate[HALF : 2 * HALF, cols] = up_rows[1, :, at : at + QUARTER]


def qkv_body(pos, *refs):
    tok, own, oth = refs[0:4], refs[4:8], refs[8:12]
    q_ref, k_ref, v_ref, normed_ref, vec_ref, w_ref, sm = refs[12:]
    s, k, c = pos[0], pos[1], pos[2]
    for m in range(4):
        z = s ^ m
        at = pl.ds(pl.multiple_of(z * QUARTER + c * HALF, 32), HALF)
        w_ref[at, :] = own[m][:HALF, :]
        at = pl.ds(pl.multiple_of(z * QUARTER + (1 - c) * HALF, 32), HALF)
        w_ref[at, :] = oth[m][:HALF, :]
        sm[z] = own[m][HALF:, :].astype(f32)

    def seg(z, n):
        return sm[z, n // 3 : n // 3 + 1, QUARTER * (n % 3) : QUARTER * (n % 3 + 1)]

    def vec(n):
        return jnp.concatenate([seg(z, n) for z in range(4)], 1)

    def chip_seg(n):
        return seg(k, n)

    gain, shift = vec(0), vec(1)
    bias = jnp.concatenate([chip_seg(2), jnp.zeros((1, QUARTER), f32), chip_seg(3)], 1)
    vec_ref[...] = jnp.concatenate(
        [gain, shift, vec(4), vec(5), vec(6), vec(7), vec(8), jnp.zeros((1, WIDTH), f32)], 0
    )
    for r in range(4):
        hat, _ = normal(tok[r][:ROWS, :].astype(f32))
        normed_ref[ROWS * r : ROWS * (r + 1), :] = (hat * gain + shift).astype(bf16)
    projected = dot(normed_ref[...], w_ref[...]) + bias
    q_ref[...] = (projected[:, :QUARTER].astype(bf16).astype(f32) * 0.125).astype(bf16)
    k_ref[:OWN, :] = projected[:, QUARTER : 2 * QUARTER].astype(bf16)
    v_ref[...] = projected[:, 2 * QUARTER :].astype(bf16)
    ids = [tok[r][2 * ROWS :, :ROWS].astype(f32)[:1] for r in range(4)]
    ids = jnp.concatenate(ids + [jnp.zeros((4, ROWS), f32)], 0).astype(bf16)
    k_ref[OWN:, :] = jnp.concatenate([ids, jnp.zeros((8, QUARTER - ROWS), bf16)], 1)


def split_ids(kva, kvb):
    ids_a = kva[OWN:, :ROWS].astype(f32)
    ids_b = kvb[OWN:, :ROWS].astype(f32)
    keys = jnp.concatenate(
        [ids_a[r : r + 1] for r in range(4)] + [ids_b[r : r + 1] for r in range(4)], 1
    )
    return ids_a.T, keys


def all_keys(pair, key_ref, value_ref):
    for n in range(2):
        for h in range(3):
            at = slice(64 * h, 64 * h + 64)
            key_ref[h, OWN * n : OWN * (n + 1), :] = pair[2 * n][:OWN, at]
            value_ref[h, OWN * n : OWN * (n + 1), :] = pair[2 * n + 1][:, at]


def attend_body(pos, q_ref, *refs):
    pair, (mixed_ref, state_ref, key_ref, value_ref) = refs[:4], refs[4:]
    cols, keys = split_ids(pair[0], pair[2])
    all_keys(pair, key_ref, value_ref)
    lane = lax.broadcasted_iota(jnp.int32, (ROWS, 64), 1)
    for r in range(4):
        rows = slice(ROWS * r, ROWS * (r + 1))
        hidden = keys > cols[:, r : r + 1]
        heads, lse = [], jnp.zeros((ROWS, 64), f32)
        for h in range(3):
            at = slice(64 * h, 64 * h + 64)
            query = q_ref[rows, at]
            scores = dot_t(query, key_ref[h])
            scores = jnp.where(hidden, NEGATIVE, scores)
            top = jnp.max(scores, -1, keepdims=True)
            weights = jnp.exp(scores - top)
            total = jnp.sum(weights, -1, keepdims=True)
            low = weights.astype(bf16)
            out = dot(low, value_ref[h])
            heads.append(out * (1.0 / total))
            lse = jnp.where(lane == h, top + jnp.log(total), lse)
        mixed = jnp.concatenate(heads, 1)
        mixed_ref[rows, :] = mixed.astype(bf16)
        state_ref[rows, :] = jnp.concatenate([mixed, lse], 1)


def feed_body(pos, *refs):
    tok, mixed, own, oth = refs[0:4], refs[4:8], refs[8:12], refs[12:16]
    vec_ref = refs[16]
    mid_ref, d0, d1, d2, d3, g0, g1, g2, g3, sums_ref, wok_ref, send_ref, own_ref = refs[17:30]
    wo, wu, wd, hat_ref, n2_ref, act_ref, wg = refs[30:]
    s, k, c = pos[0], pos[1], pos[2]
    for m in range(4):
        z = s ^ m
        for half, src in ((c, own[m]), (1 - c, oth[m])):
            at = pl.ds(pl.multiple_of(z * QUARTER + half * HALF, 32), HALF)
            wo[at, :] = src[:HALF, :]
            wu[at, :] = src[HALF : 2 * HALF, :]
            wd[at, :] = src[2 * HALF :, :]
    wok_ref[...] = wo[pl.ds(pl.multiple_of(k * QUARTER, 64), QUARTER), :]
    bias_out, gain, shift = vec_ref[2:3, :], vec_ref[3:4, :], vec_ref[4:5, :]
    bias_up = vec_ref[6:7, :]
    attended = bias_out
    for m in range(4):
        block = jnp.concatenate(
            [mixed[m][ROWS * (r ^ m) : ROWS * (r ^ m) + ROWS, :] for r in range(4)], 0
        )
        at = pl.ds(pl.multiple_of((k ^ m) * QUARTER, 64), QUARTER)
        attended = attended + dot(block, wo[at, :])
    for r in range(4):
        rows = slice(ROWS * r, ROWS * (r + 1))
        middle = tok[r][:ROWS, :].astype(f32) + attended[rows]
        if r == 0:
            mid_ref[...] = middle
        hat, _ = normal(middle)
        hat_ref[rows, :] = hat
        n2_ref[rows, :] = (hat * gain + shift).astype(bf16)
    pre_act = dot(n2_ref[...], wu[...]) + bias_up
    cdf = 0.5 * (1.0 + lax.erf(pre_act * (1.0 / math.sqrt(2.0))))
    act_ref[...] = (pre_act * cdf).astype(bf16)
    slope = cdf + pre_act * jnp.exp(-0.5 * pre_act * pre_act) * (1.0 / math.sqrt(2.0 * math.pi))
    grads = jnp.concatenate([ref[ROWS : 2 * ROWS, :] for ref in tok], 0)
    pre = (dot_t(grads, wd[...]) * slope).astype(bf16)
    back = dot_t(pre, wu[...])
    sums = [
        jnp.sum(back * hat_ref[...], 0, keepdims=True),
        jnp.sum(back, 0, keepdims=True),
        jnp.sum(pre.astype(f32), 0, keepdims=True),
    ]
    sums_ref[...] = jnp.concatenate(sums + [jnp.zeros((5, WIDTH), f32)], 0)
    g0[...] = back[:ROWS]
    for r, ref in ((1, g1), (2, g2), (3, g3)):
        ref[...] = back[ROWS * r : ROWS * (r + 1)].astype(bf16)
    down = dot(act_ref[...], wd[...])
    d0[...] = down[:ROWS]
    for r, ref in ((1, d1), (2, d2), (3, d3)):
        ref[...] = down[ROWS * r : ROWS * (r + 1)].astype(bf16)
    for part in range(2):
        wg[...] = t_dot(act_ref[...], grads) if part == 0 else t_dot(n2_ref[...], pre)
        rows = slice(HALF * part, HALF * part + HALF)
        for m in range(4):
            z = s ^ m
            at = pl.ds(pl.multiple_of(z * QUARTER + c * HALF, 32), HALF)
            own_ref[m, rows, :] = wg[at, :]
            at = pl.ds(pl.multiple_of(z * QUARTER + (1 - c) * HALF, 32), HALF)
            send_ref[m, rows, :] = wg[at, :].astype(bf16)


def feed_halves_body(pos, own_ref, got_ref, o0, o1, o2, o3):
    for m, out in enumerate((o0, o1, o2, o3)):
        out[...] = (own_ref[m] + got_ref[m].astype(f32)).astype(out.dtype)


def add_body(pos, o0, r1, r2, r3, out):
    total = o0[...] + r1[...].astype(f32) + r2[...].astype(f32) + r3[...].astype(f32)
    out[...] = total.astype(out.dtype)


def middle_body(pos, g0, r1, r2, r3, mid_ref, tok_ref, vec_ref, gm_ref, ga_ref):
    err = g0[...] + r1[...].astype(f32) + r2[...].astype(f32) + r3[...].astype(f32)
    hat, rstd = normal(mid_ref[...])
    grad = tok_ref[ROWS : 2 * ROWS, :].astype(f32) + norm_back(err, vec_ref[3:4, :], hat, rstd)
    gm_ref[...] = grad
    ga_ref[...] = grad.astype(bf16)


def attend_grad_body(pos, a0, a1, a2, a3, wok, q_ref, *refs):
    pair, state_ref, outs = refs[:4], refs[4], refs[5:]
    dq_ref, own_ref, send_k, send_v, p_ref, ds_ref, key_ref, value_ref = outs
    cols, keys = split_ids(pair[0], pair[2])
    all_keys(pair, key_ref, value_ref)
    grads = jnp.concatenate([ref[...] for ref in (a0, a1, a2, a3)], 0)
    grad_mixed = dot_t(grads, wok[...]).astype(bf16)
    dq, dks, dvs = [], [], []
    for h in range(3):
        at = slice(64 * h, 64 * h + 64)
        query, grad = q_ref[:, at], grad_mixed[:, at]
        grad_q = []
        for r in range(4):
            rows = slice(ROWS * r, ROWS * (r + 1))
            hidden = keys > cols[:, r : r + 1]
            g = grad[rows]
            inner = jnp.sum(g.astype(f32) * state_ref[rows, at], -1, keepdims=True)
            lse = state_ref[rows, QUARTER + h : QUARTER + h + 1]
            scores = dot_t(query[rows], key_ref[h])
            probs = jnp.exp(jnp.where(hidden, NEGATIVE, scores) - lse)
            slopes = dot_t(g, value_ref[h])
            ds = (probs * (slopes - inner)).astype(bf16)
            p_ref[rows, :] = probs.astype(bf16)
            ds_ref[rows, :] = ds
            grad_q.append(dot(ds, key_ref[h]))
        dq.append(jnp.concatenate(grad_q, 0))
        dks.append(t_dot(query, ds_ref[...]))
        dvs.append(t_dot(grad, p_ref[...]))
    dk = jnp.concatenate(dks, 0).T
    dv = jnp.concatenate(dvs, 0).T
    own_ref[:, :QUARTER] = dk[:OWN]
    own_ref[:, QUARTER:] = dv[:OWN]
    send_k[...] = dk[OWN:].astype(bf16)
    send_v[...] = dv[OWN:].astype(bf16)
    dq_ref[...] = (jnp.concatenate(dq, 1) * 0.125).astype(bf16)


def project_grad_body(pos, *refs):
    mixed, ga = refs[0:4], refs[4:8]
    normed, dq, kv_own, got_k, got_v = refs[8:13]
    send_ref, own_ref, gp, wg, gk = refs[13:]
    s, k, c = pos[0], pos[1], pos[2]
    gp[:, :QUARTER] = dq[...]
    got = jnp.concatenate([got_k[...], got_v[...]], 1).astype(f32)
    gp[:, QUARTER:] = (kv_own[...] + got).astype(bf16)
    wg[:, : 3 * QUARTER] = t_dot(normed[...], gp[...])
    for q in range(4):

        @pl.when(k == q)
        def _():
            for r in range(4):
                gk[ROWS * r : ROWS * (r + 1), :] = ga[r][:, QUARTER * q : QUARTER * (q + 1)]

    for m in range(4):
        block = jnp.concatenate(
            [mixed[m][ROWS * (r ^ m) : ROWS * (r ^ m) + ROWS, :] for r in range(4)], 0
        )
        at = pl.ds(pl.multiple_of((k ^ m) * QUARTER, 64), QUARTER)
        wg[at, 3 * QUARTER :] = t_dot(block, gk[...])
    for m in range(4):
        z = s ^ m
        at = pl.ds(pl.multiple_of(z * QUARTER + c * HALF, 32), HALF)
        own_ref[m] = wg[at, :]
        at = pl.ds(pl.multiple_of(z * QUARTER + (1 - c) * HALF, 32), HALF)
        send_ref[m] = wg[at, :].astype(bf16)


def normed_grad_body(pos, *refs):
    tok, (gp, w_ref, ga_ref, sums_ref) = refs[0:4], refs[4:8]
    small_ref, g0, g1, g2, g3 = refs[8:]
    k = pos[1]
    back = dot_t(gp[...], w_ref[...])
    hat = jnp.concatenate([normal(tok[r][:ROWS, :].astype(f32))[0] for r in range(4)], 0)
    ln1_gain = jnp.sum(back * hat, 0, keepdims=True)
    ln1_bias = jnp.sum(back, 0, keepdims=True)
    g0[...] = back[:ROWS]
    for r, ref in ((1, g1), (2, g2), (3, g3)):
        ref[...] = back[ROWS * r : ROWS * (r + 1)].astype(bf16)
    gp_sums = jnp.sum(gp[...].astype(f32), 0, keepdims=True)
    out_bias = jnp.sum(ga_ref[...].astype(f32), 0, keepdims=True)
    down_bias = jnp.sum(tok[0][ROWS : 2 * ROWS, :].astype(f32), 0, keepdims=True)
    for z in range(4):
        at = slice(QUARTER * z, QUARTER * (z + 1))
        here = jnp.where(k == z, 1.0, 0.0).astype(f32)
        row0 = [ln1_gain[:, at], ln1_bias[:, at], gp_sums[:, :QUARTER] * here]
        row0 = jnp.concatenate(row0 + [gp_sums[:, 2 * QUARTER :] * here], 1)
        row1 = [out_bias[:, at], sums_ref[0:1, at], sums_ref[1:2, at], down_bias[:, at]]
        row1 = jnp.concatenate(row1, 1)
        row2 = jnp.concatenate([sums_ref[2:3, at], jnp.zeros((1, 3 * QUARTER), f32)], 1)
        small_ref[z] = jnp.concatenate([row0, row1, row2, jnp.zeros((5, WIDTH), f32)], 0)


def last_halves_body(pos, own_ref, small_ref, got, o0, o1, o2, o3):
    s = pos[0]
    for m, out in enumerate((o0, o1, o2, o3)):
        out[:HALF, :] = (own_ref[m] + got[m].astype(f32)).astype(out.dtype)
        out[HALF:, :] = small_ref[s ^ m].astype(out.dtype)


def rows_body(pos, g0, r1, r2, r3, d0, s1, s2, s3, tok_ref, gm_ref, mid_ref, vec_ref, *outs):
    grad_ref, out_ref = outs
    err = g0[...] + r1[...].astype(f32) + r2[...].astype(f32) + r3[...].astype(f32)
    hat, rstd = normal(tok_ref[:ROWS, :].astype(f32))
    grad_ref[0] = gm_ref[...] + norm_back(err, vec_ref[0:1, :], hat, rstd)
    total = d0[...] + s1[...].astype(f32) + s2[...].astype(f32) + s3[...].astype(f32)
    out_ref[0] = (mid_ref[...] + total + vec_ref[5:6, :]).astype(bf16)


def feed_join_body(pos, *refs):
    own, oth = refs[0:4], refs[4:8]
    down_ref, up_ref, sc = refs[8:]
    k, c = pos[1], pos[2]
    for m in range(4):
        sc[c, k ^ m] = own[m][...]
        sc[1 - c, k ^ m] = oth[m][...]
    for q in range(4):
        for half in range(2):
            at = QUARTER * q + HALF * half
            down_ref[at : at + HALF, :] = sc[half, q, :HALF, :].astype(f32)
            rows = slice(HALF * half, HALF * half + HALF)
            for p in range(4):
                cols = slice(WIDTH * p + QUARTER * q, WIDTH * p + QUARTER * (q + 1))
                piece = sc[half, q, HALF:, QUARTER * p : QUARTER * (p + 1)]
                up_ref[rows, cols] = piece.astype(f32)


def last_join_body(pos, *refs):
    own, oth = refs[0:4], refs[4:8]
    qkv_ref, out_ref, up_ref, sc = refs[8], refs[9], refs[18], refs[19]
    vec_refs = refs[10:18]
    k, c = pos[1], pos[2]
    for m in range(4):
        sc[c, k ^ m] = own[m][...]
        sc[1 - c, k ^ m] = oth[m][...]
    total = jnp.zeros((8, WIDTH), f32)
    ups = []
    for q in range(4):
        small = sc[0, q, HALF:, :].astype(f32) + sc[1, q, HALF:, :].astype(f32)
        total = total + small
        ups.append(small[2:3, :QUARTER])
        for half in range(2):
            rows = slice(HALF * half, HALF * half + HALF)
            for p in range(3):
                cols = slice(WIDTH * p + QUARTER * q, WIDTH * p + QUARTER * (q + 1))
                piece = sc[half, q, :HALF, QUARTER * p : QUARTER * (p + 1)]
                qkv_ref[rows, cols] = piece.astype(f32)
            out_ref[rows, QUARTER * q : QUARTER * (q + 1)] = sc[
                half, q, :HALF, 3 * QUARTER :
            ].astype(f32)
    for n, ref in enumerate(vec_refs):
        row = total[n // 4 : n // 4 + 1, QUARTER * (n % 4) : QUARTER * (n % 4 + 1)]
        ref[...] = row.reshape(QUARTER)
    up_ref[...] = jnp.concatenate(ups, 1).reshape(WIDTH)


def shards(
    tokens,
    block_ids,
    ln1_gain,
    ln1_bias,
    w_qkv,
    q_bias,
    v_bias,
    w_out,
    out_bias,
    ln2_gain,
    ln2_bias,
    w_up,
    up_bias,
    w_down,
    down_bias,
    cotangent,
):
    seq = lax.axis_index("seq")
    ctx = lax.axis_index("ctx")
    k, core = ctx // 2, ctx % 2
    pos = jnp.stack([seq, k, core]).astype(jnp.int32)

    small = [ln1_gain, ln1_bias, q_bias, v_bias, out_bias, ln2_gain, ln2_bias, down_bias, up_bias]
    piece_qkv, mate_qkv, pack, rest, mate_rest = run(
        pack_body,
        pos,
        [w_qkv, tokens, cotangent, w_out, w_up, w_down, block_ids, *small],
        [((HALF + 16, 3 * QUARTER), bf16)] * 2
        + [((2 * ROWS + 8, WIDTH), bf16)]
        + [((3 * HALF, WIDTH), bf16)] * 2,
        [((2, HALF, 3 * WIDTH), bf16), ((2, HALF, 4 * WIDTH), bf16)],
        hbm=range(6),
        sems=10,
        limit=60,
    )
    got_qkv = seq_gather(piece_qkv)
    tok = chip_gather(pack)
    got_rest = seq_gather(rest)
    oth_qkv = [mate_qkv] + [core_swap(block) for block in got_qkv[1:]]
    third = (OWN, QUARTER)
    query, *pair, normed, vec, weight_qkv = run(
        qkv_body,
        pos,
        [*tok, *got_qkv, *oth_qkv],
        [(third, bf16), ((OWN + 8, QUARTER), bf16), (third, bf16)]
        + [((OWN, WIDTH), bf16), ((8, WIDTH), f32), ((WIDTH, 3 * QUARTER), bf16)],
        [((4, 16, 3 * QUARTER), f32)],
    )
    pair = [*pair, *[core_swap(x) for x in pair]]
    mixed_own, state = run(
        attend_body,
        pos,
        [query, *pair],
        [((OWN, QUARTER), bf16), ((OWN, 256), f32)],
        [((3, 2 * OWN, 64), bf16)] * 2,
    )
    mixed = chip_gather(mixed_own)
    got_rest = lax.optimization_barrier((*got_rest, *mixed[1:]))[:4]
    oth_rest = [mate_rest] + [core_swap(block) for block in got_rest[1:]]
    big, block, piece = (OWN, WIDTH), (ROWS, WIDTH), (QUARTER, WIDTH)
    mid, d0, d1, d2, d3, g0, g1, g2, g3, sums, w_out_k, feed_send, feed_own = run(
        feed_body,
        pos,
        [*tok, *mixed, *got_rest, *oth_rest, vec],
        [(block, f32)]
        + [(block, f32), (block, bf16), (block, bf16), (block, bf16)] * 2
        + [((8, WIDTH), f32), (piece, bf16), ((4, *piece), bf16), ((4, *piece), f32)],
        [((WIDTH, WIDTH), bf16)] * 3 + [(big, f32), (big, bf16), (big, bf16), ((WIDTH, WIDTH), f32)],
        limit=40,
    )
    got_g = [chip_swap(g, m) for m, g in ((1, g1), (2, g2), (3, g3))]
    feed_got = core_swap(feed_send)
    h0, h1, h2, h3 = run(
        feed_halves_body, pos, [feed_own, feed_got], [(piece, f32)] + [(piece, bf16)] * 3
    )
    grad_mid, grad_att = run(
        middle_body, pos, [after(g0, h0), *got_g, mid, tok[0], vec], [(block, f32), (block, bf16)]
    )
    ga = chip_gather(grad_att)
    feed_terms = [seq_swap(h, m) for m, h in ((1, h1), (2, h2), (3, h3))]
    dq, kv_own, *pair_send = run(
        attend_grad_body,
        pos,
        [*ga, w_out_k, query, *pair, state],
        [(third, bf16), ((OWN, 2 * QUARTER), f32)] + [(third, bf16)] * 2,
        [((OWN, 2 * OWN), bf16)] * 2 + [((3, 2 * OWN, 64), bf16)] * 2,
    )
    pair_send[0], *feed_terms[1:] = lax.optimization_barrier((pair_send[0], *feed_terms[1:]))
    pair_got = [core_swap(x) for x in pair_send]
    lpiece = (HALF + 8, WIDTH)
    last_send, last_own, grad_proj = run(
        project_grad_body,
        pos,
        [*mixed, *ga, normed, dq, kv_own, *pair_got],
        [((4, HALF, WIDTH), bf16), ((4, HALF, WIDTH), f32), ((OWN, 3 * QUARTER), bf16)],
        [((WIDTH, WIDTH), f32), ((OWN, QUARTER), bf16)],
    )
    last_send, feed_terms[0] = lax.optimization_barrier((last_send, feed_terms[0]))
    last_got = core_swap(last_send)
    got_d = [chip_swap(after(d, grad_proj), m) for m, d in ((1, d1), (2, d2), (3, d3))]
    last_small, e0, e1, e2, e3 = run(
        normed_grad_body,
        pos,
        [*tok, grad_proj, weight_qkv, ga[0], sums],
        [((4, 8, WIDTH), f32), (block, f32)] + [(block, bf16)] * 3,
    )
    l0, l1, l2, l3 = run(
        last_halves_body,
        pos,
        [last_own, last_small, last_got],
        [(lpiece, f32)] + [(lpiece, bf16)] * 3,
    )
    last_terms = [seq_swap(h, m) for m, h in ((1, l1), (2, l2), (3, l3))]
    (feed_sum,) = run(add_body, pos, [after(h0, l1), *feed_terms], [(piece, bf16)])
    feed_blocks = chip_gather(feed_sum)
    l0, *got_d = lax.optimization_barrier((l0, *got_d))
    (last_sum,) = run(add_body, pos, [l0, *last_terms], [(lpiece, bf16)], cost=2)
    last_blocks = chip_gather(last_sum)
    got_e = [chip_swap(after(e, last_sum), m) for m, e in ((1, e1), (2, e2), (3, e3))]
    feed_oth = [core_swap(after(b, last_sum)) for b in feed_blocks]
    grad_w_down, grad_w_up = run(
        feed_join_body,
        pos,
        [after(feed_blocks[0], last_sum), *feed_blocks[1:], *feed_oth],
        [((WIDTH, WIDTH), f32), ((QUARTER, 4 * WIDTH), f32)],
        [((2, 4, QUARTER, WIDTH), bf16)],
    )
    input_grad, result = run(
        rows_body,
        pos,
        [after(e0, grad_w_up), *got_e, d0, *got_d, tok[0], grad_mid, mid, vec],
        [((1, *block), f32), ((1, *block), bf16)],
    )
    last_oth = [core_swap(b) for b in last_blocks]
    grad_w_qkv, grad_w_out, *g, g_up = run(
        last_join_body,
        pos,
        [*last_blocks, *last_oth],
        [((QUARTER, 3 * WIDTH), f32), ((QUARTER, WIDTH), f32)]
        + [((QUARTER,), f32)] * 8
        + [((WIDTH,), f32)],
        [((2, 4, HALF + 8, WIDTH), bf16)],
    )
    return (
        result,
        input_grad,
        g[0],
        g[1],
        grad_w_qkv,
        g[2],
        g[3],
        grad_w_out,
        g[4],
        g[5],
        g[6],
        grad_w_up,
        g_up,
        grad_w_down,
        g[7],
    )


def solution(mesh):
    placed = (
        P("seq", "ctx", None),
        P("seq", "ctx"),
        P("seq"),
        P("seq"),
        P("seq", None),
        P("seq"),
        P("seq"),
        P("seq", None),
        P("seq"),
        P("seq"),
        P("seq"),
        P("seq", None),
        P("seq"),
        P("seq", None),
        P("seq"),
        P("seq", "ctx", None),
    )
    return jax.shard_map(
        shards if mesh.shape["ctx"] == 8 and mesh.shape["seq"] == 4 else shards_general,
        mesh=mesh,
        in_specs=placed,
        out_specs=(
            P("seq", "ctx", None),
            P("seq", "ctx", None),
            P("seq"),
            P("seq"),
            P("seq", None),
            P("seq"),
            P("seq"),
            P("seq", None),
            P("seq"),
            P("seq"),
            P("seq"),
            P("seq", None),
            P("seq"),
            P("seq", None),
            P("seq"),
        ),
        check_vma=False,
    )
```

```python
import math

import jax
import jax.numpy as jnp
from jax import lax
from jax.experimental import pallas as pl
from jax.experimental.pallas import tpu as pltpu
from jax.sharding import PartitionSpec as P

HEADS = 12


EPSILON = 1e-06
NEGATIVE = -1e30


def layer_norm(values, gain, shift):
    center = values - jnp.mean(values, -1, keepdims=True)
    spread = jnp.mean(center * center, -1, keepdims=True)
    return center * lax.rsqrt(spread + EPSILON) * gain + shift


def block_rows(count):
    return math.gcd(count, 512)


def masked_scores(query_heads, key_heads, query_ids, key_ids, scale):
    raw = (
        jnp.einsum("qhd,khd->hqk", query_heads, key_heads, preferred_element_type=jnp.float32)
        * scale
    )
    allowed = key_ids[None, None, :] <= query_ids[None, :, None]
    return (raw, allowed)


def attend_forward(query_heads, query_ids, keys_all, values_all, ids_all, scale):
    tok_rows, heads, head_dim = query_heads.shape
    total_keys = keys_all.shape[0]
    step = block_rows(total_keys)
    blocks = total_keys // step

    def attend_visit(carry, inputs):
        running, total, accum = carry
        key_block, value_block, id_block = inputs
        raw, allowed = masked_scores(query_heads, key_block, query_ids, id_block, scale)
        masked = jnp.where(allowed, raw, NEGATIVE)
        new_top = jnp.maximum(running, jnp.max(masked, -1))
        weights = jnp.where(allowed, jnp.exp(masked - new_top[..., None]), 0.0)
        factor = jnp.exp(running - new_top)
        total = total * factor + jnp.sum(weights, -1)
        accum = accum * factor[..., None] + jnp.einsum(
            "hqk,khd->hqd",
            weights.astype(jnp.bfloat16),
            value_block,
            preferred_element_type=jnp.float32,
        )
        return ((new_top, total, accum), None)

    start_state = (
        jnp.full((heads, tok_rows), NEGATIVE, jnp.float32),
        jnp.zeros((heads, tok_rows), jnp.float32),
        jnp.zeros((heads, tok_rows, head_dim), jnp.float32),
    )
    (running, total, accum), _ = lax.scan(
        attend_visit,
        start_state,
        (
            keys_all.reshape(blocks, step, heads, head_dim),
            values_all.reshape(blocks, step, heads, head_dim),
            ids_all.reshape(blocks, step),
        ),
    )
    output_heads = jnp.transpose(accum / total[..., None], (1, 0, 2))
    return (output_heads, running + jnp.log(total))


def query_gradient(
    query_heads, grad_heads, query_ids, keys_all, values_all, ids_all, logsum, inner, scale
):
    tok_rows, heads, head_dim = query_heads.shape
    total_keys = keys_all.shape[0]
    step = block_rows(total_keys)
    blocks = total_keys // step

    def query_visit(accum, inputs):
        key_block, value_block, id_block = inputs
        raw, allowed = masked_scores(query_heads, key_block, query_ids, id_block, scale)
        probs = jnp.where(allowed, jnp.exp(raw - logsum[..., None]), 0.0)
        grad_probs = jnp.einsum(
            "qhd,khd->hqk", grad_heads, value_block, preferred_element_type=jnp.float32
        )
        grad_scores = (probs * (grad_probs - inner[..., None])).astype(jnp.bfloat16)
        accum = accum + jnp.einsum(
            "hqk,khd->qhd", grad_scores, key_block, preferred_element_type=jnp.float32
        )
        return (accum, None)

    accum, _ = lax.scan(
        query_visit,
        jnp.zeros((tok_rows, heads, head_dim), jnp.float32),
        (
            keys_all.reshape(blocks, step, heads, head_dim),
            values_all.reshape(blocks, step, heads, head_dim),
            ids_all.reshape(blocks, step),
        ),
    )
    return accum * scale


def pair_grads(
    query_heads, grad_heads, query_ids, logsum, inner, key_heads, value_heads, key_ids, scale
):
    raw, allowed = masked_scores(query_heads, key_heads, query_ids, key_ids, scale)
    probs = jnp.where(allowed, jnp.exp(raw - logsum[..., None]), 0.0)
    grad_probs = jnp.einsum(
        "qhd,khd->hqk", grad_heads, value_heads, preferred_element_type=jnp.float32
    )
    grad_scores = (probs * (grad_probs - inner[..., None])).astype(jnp.bfloat16)
    grad_keys = (
        jnp.einsum("hqk,qhd->khd", grad_scores, query_heads, preferred_element_type=jnp.float32)
        * scale
    )
    grad_values = jnp.einsum(
        "hqk,qhd->khd", probs.astype(jnp.bfloat16), grad_heads, preferred_element_type=jnp.float32
    )
    return (grad_keys, grad_values)


def shards_general(
    tokens,
    block_ids,
    ln1_gain,
    ln1_bias,
    w_qkv,
    q_bias,
    v_bias,
    w_out,
    out_bias,
    ln2_gain,
    ln2_bias,
    w_up,
    up_bias,
    w_down,
    down_bias,
    cotangent,
):
    gathered = (
        lax.all_gather(ln1_gain, "seq", axis=0, tiled=True),
        lax.all_gather(ln1_bias, "seq", axis=0, tiled=True),
        lax.all_gather(w_qkv, "seq", axis=0, tiled=True),
        lax.all_gather(q_bias, "seq", axis=0, tiled=True),
        lax.all_gather(v_bias, "seq", axis=0, tiled=True),
        lax.all_gather(w_out, "seq", axis=0, tiled=True),
        lax.all_gather(out_bias, "seq", axis=0, tiled=True),
        lax.all_gather(ln2_gain, "seq", axis=0, tiled=True),
        lax.all_gather(ln2_bias, "seq", axis=0, tiled=True),
        lax.all_gather(w_up, "seq", axis=0, tiled=True),
        lax.all_gather(up_bias, "seq", axis=0, tiled=True),
        lax.all_gather(w_down, "seq", axis=0, tiled=True),
        lax.all_gather(down_bias, "seq", axis=0, tiled=True),
    )
    attention_part = gathered[:7]
    feed_part = gathered[7:]
    gain_one, shift_one, weight_qkv, bias_query, bias_value, weight_out, bias_out = attention_part
    width = weight_out.shape[0]
    heads = HEADS
    head_dim = width // heads
    scale = 1.0 / math.sqrt(head_dim)
    inputs = tokens[0].astype(jnp.float32)
    tok_rows = inputs.shape[0]
    own_ids = block_ids[0]
    gain_one_f = gain_one.astype(jnp.float32)
    shift_one_f = shift_one.astype(jnp.float32)
    normed_one, norm_one_pull = jax.vjp(layer_norm, inputs, gain_one_f, shift_one_f)
    normed_low = normed_one.astype(jnp.bfloat16)
    qkv_bias = jnp.concatenate(
        [
            bias_query.astype(jnp.float32),
            jnp.zeros((width,), jnp.float32),
            bias_value.astype(jnp.float32),
        ]
    )
    projected = (
        jnp.dot(normed_low, weight_qkv, preferred_element_type=jnp.float32) + qkv_bias
    ).astype(jnp.bfloat16)
    query_low = projected[:, :width]
    key_low = projected[:, width : 2 * width]
    value_low = projected[:, 2 * width :]
    ids_all = lax.all_gather(block_ids, "ctx", axis=1, tiled=True)[0]
    keys_all, values_all = (
        lax.all_gather(key_low, "ctx", axis=0, tiled=True),
        lax.all_gather(value_low, "ctx", axis=0, tiled=True),
    )
    query_heads = query_low.reshape(tok_rows, heads, head_dim)
    output_heads, logsum = attend_forward(
        query_heads, own_ids, keys_all, values_all, ids_all, scale
    )
    mixed_low = output_heads.reshape(tok_rows, width).astype(jnp.bfloat16)
    attended = jnp.dot(mixed_low, weight_out, preferred_element_type=jnp.float32) + bias_out.astype(
        jnp.float32
    )
    middle = inputs + attended
    gain_two, shift_two, weight_up, bias_up, weight_down, bias_down = feed_part
    gain_two_f = gain_two.astype(jnp.float32)
    shift_two_f = shift_two.astype(jnp.float32)
    normed_two, norm_two_pull = jax.vjp(layer_norm, middle, gain_two_f, shift_two_f)
    normed_two_low = normed_two.astype(jnp.bfloat16)
    pre_act = jnp.dot(
        normed_two_low, weight_up, preferred_element_type=jnp.float32
    ) + bias_up.astype(jnp.float32)
    activated, gelu_pull = jax.vjp(lambda values: jax.nn.gelu(values, approximate=False), pre_act)
    activated_low = activated.astype(jnp.bfloat16)
    result = (
        middle
        + jnp.dot(activated_low, weight_down, preferred_element_type=jnp.float32)
        + bias_down.astype(jnp.float32)
    )
    grad_out = cotangent[0]
    grad_out_f = grad_out.astype(jnp.float32)
    grad_weight_down = jnp.einsum(
        "tf,td->fd", activated_low, grad_out, preferred_element_type=jnp.float32
    )
    grad_bias_down = jnp.sum(grad_out_f, 0)
    grad_hidden = jnp.einsum("td,fd->tf", grad_out, weight_down, preferred_element_type=jnp.float32)
    grad_pre_low = gelu_pull(grad_hidden)[0].astype(jnp.bfloat16)
    grad_weight_up = jnp.einsum(
        "td,tf->df", normed_two_low, grad_pre_low, preferred_element_type=jnp.float32
    )
    grad_bias_up = jnp.sum(grad_pre_low.astype(jnp.float32), 0)
    grad_normed_two = jnp.einsum(
        "tf,df->td", grad_pre_low, weight_up, preferred_element_type=jnp.float32
    )
    grad_middle_part, grad_gain_two, grad_shift_two = norm_two_pull(grad_normed_two)
    grad_middle = grad_out_f + grad_middle_part
    grad_attended = grad_middle.astype(jnp.bfloat16)
    grad_weight_out = jnp.einsum(
        "td,te->de", mixed_low, grad_attended, preferred_element_type=jnp.float32
    )
    grad_bias_out = jnp.sum(grad_attended.astype(jnp.float32), 0)
    grad_mixed = jnp.einsum(
        "te,de->td", grad_attended, weight_out, preferred_element_type=jnp.float32
    ).astype(jnp.bfloat16)
    grad_heads = grad_mixed.reshape(tok_rows, heads, head_dim)
    inner = jnp.einsum("thd,thd->ht", grad_heads.astype(jnp.float32), output_heads)
    grad_query = query_gradient(
        query_heads, grad_heads, own_ids, keys_all, values_all, ids_all, logsum, inner, scale
    )
    step = block_rows(lax.axis_size("ctx") * tok_rows)
    blocks = lax.axis_size("ctx") * tok_rows // step
    key_part = keys_all.reshape(blocks, step, heads, head_dim)
    value_part = values_all.reshape(blocks, step, heads, head_dim)
    id_part = ids_all.reshape(blocks, step)

    def key_visit(carry, inputs):
        grad_keys, grad_values = pair_grads(
            query_heads, grad_heads, own_ids, logsum, inner, inputs[0], inputs[1], inputs[2], scale
        )
        joined = jnp.concatenate(
            [grad_keys.reshape(step, width), grad_values.reshape(step, width)], 1
        )
        return (carry, joined)

    _, terms = lax.scan(key_visit, jnp.zeros((), jnp.float32), (key_part, value_part, id_part))
    key_value_grads = lax.psum_scatter(
        terms.reshape(lax.axis_size("ctx") * tok_rows, 2 * width),
        "ctx",
        scatter_dimension=0,
        tiled=True,
    )
    grad_keys_all = key_value_grads[:, :width]
    grad_values_all = key_value_grads[:, width:]
    grad_query_low = grad_query.reshape(tok_rows, width).astype(jnp.bfloat16)
    grad_value_low = grad_values_all.astype(jnp.bfloat16)
    grad_projected = jnp.concatenate(
        [grad_query_low, grad_keys_all.astype(jnp.bfloat16), grad_value_low], 1
    )
    grad_weight_qkv = jnp.einsum(
        "td,te->de", normed_low, grad_projected, preferred_element_type=jnp.float32
    )
    grad_bias_query = jnp.sum(grad_query_low.astype(jnp.float32), 0)
    grad_bias_value = jnp.sum(grad_value_low.astype(jnp.float32), 0)
    grad_normed_one = jnp.einsum(
        "te,de->td", grad_projected, weight_qkv, preferred_element_type=jnp.float32
    )
    grad_input_part, grad_gain_one, grad_shift_one = norm_one_pull(grad_normed_one)
    input_grad = grad_middle + grad_input_part
    local_grads = (
        grad_gain_one,
        grad_shift_one,
        grad_weight_qkv,
        grad_bias_query,
        grad_bias_value,
        grad_weight_out,
        grad_bias_out,
        grad_gain_two,
        grad_shift_two,
        grad_weight_up,
        grad_bias_up,
        grad_weight_down,
        grad_bias_down,
    )
    shares = (
        lax.psum_scatter(
            local_grads[0].astype(jnp.bfloat16), "seq", scatter_dimension=0, tiled=True
        ).astype(jnp.float32),
        lax.psum_scatter(
            local_grads[1].astype(jnp.bfloat16), "seq", scatter_dimension=0, tiled=True
        ).astype(jnp.float32),
        lax.psum_scatter(
            local_grads[2].astype(jnp.bfloat16), "seq", scatter_dimension=0, tiled=True
        ).astype(jnp.float32),
        lax.psum_scatter(
            local_grads[3].astype(jnp.bfloat16), "seq", scatter_dimension=0, tiled=True
        ).astype(jnp.float32),
        lax.psum_scatter(
            local_grads[4].astype(jnp.bfloat16), "seq", scatter_dimension=0, tiled=True
        ).astype(jnp.float32),
        lax.psum_scatter(
            local_grads[5].astype(jnp.bfloat16), "seq", scatter_dimension=0, tiled=True
        ).astype(jnp.float32),
        lax.psum_scatter(
            local_grads[6].astype(jnp.bfloat16), "seq", scatter_dimension=0, tiled=True
        ).astype(jnp.float32),
        lax.psum_scatter(
            local_grads[7].astype(jnp.bfloat16), "seq", scatter_dimension=0, tiled=True
        ).astype(jnp.float32),
        lax.psum_scatter(
            local_grads[8].astype(jnp.bfloat16), "seq", scatter_dimension=0, tiled=True
        ).astype(jnp.float32),
        lax.psum_scatter(
            local_grads[9].astype(jnp.bfloat16), "seq", scatter_dimension=0, tiled=True
        ).astype(jnp.float32),
        lax.psum_scatter(
            local_grads[10].astype(jnp.bfloat16), "seq", scatter_dimension=0, tiled=True
        ).astype(jnp.float32),
        lax.psum_scatter(
            local_grads[11].astype(jnp.bfloat16), "seq", scatter_dimension=0, tiled=True
        ).astype(jnp.float32),
        lax.psum_scatter(
            local_grads[12].astype(jnp.bfloat16), "seq", scatter_dimension=0, tiled=True
        ).astype(jnp.float32),
    )
    totals = lax.psum(
        (
            shares[0],
            shares[1],
            shares[2],
            shares[3],
            shares[4],
            shares[5],
            shares[6],
            shares[7],
            shares[8],
            shares[9],
            shares[10],
            shares[11],
            shares[12],
        ),
        "ctx",
    )
    return (result.astype(jnp.bfloat16)[None], input_grad[None]) + tuple(totals)


QUARTER = 192
HALF = 96
ROWS = 128
WIDTH = 768
OWN = 512
f32, bf16 = jnp.float32, jnp.bfloat16


def core_swap(values):
    return lax.ppermute(values, "ctx", [(i, i ^ 1) for i in range(8)])


def chip_swap(values, mask):
    return lax.ppermute(values, "ctx", [(i, i ^ (2 * mask)) for i in range(8)])


def seq_swap(values, mask):
    return lax.ppermute(values, "seq", [(i, i ^ mask) for i in range(4)])


def chip_gather(values):
    return [values] + [chip_swap(values, m) for m in (1, 2, 3)]


def seq_gather(values):
    return [values] + [seq_swap(values, m) for m in (1, 2, 3)]


def after(values, *earlier):
    return lax.optimization_barrier((values, *earlier))[0]


def run(body, pos, args, outs, scratch=(), hbm=(), sems=0, limit=24, cost=0.001):
    vmem = pl.BlockSpec(memory_space=pltpu.VMEM)
    whole = pl.BlockSpec(memory_space=pl.ANY)
    scratch_shapes = [pltpu.VMEM(shape, kind) for shape, kind in scratch]
    if sems:
        scratch_shapes.append(pltpu.SemaphoreType.DMA((sems,)))
    return pl.pallas_call(
        body,
        out_shape=[jax.ShapeDtypeStruct(shape, kind) for shape, kind in outs],
        in_specs=[pl.BlockSpec(memory_space=pltpu.SMEM)]
        + [whole if n in hbm else vmem for n in range(len(args))],
        out_specs=[vmem] * len(outs),
        scratch_shapes=scratch_shapes,
        compiler_params=pltpu.CompilerParams(vmem_limit_bytes=limit << 20),
        cost_estimate=pl.CostEstimate(
            flops=int(cost * 524288000), bytes_accessed=1000, transcendentals=1
        ),
    )(pos, *args)


def dot(left, right):
    return lax.dot_general(left, right, (((1,), (0,)), ((), ())), preferred_element_type=f32)


def dot_t(left, right):
    return lax.dot_general(left, right, (((1,), (1,)), ((), ())), preferred_element_type=f32)


def t_dot(left, right):
    return lax.dot_general(left, right, (((0,), (0,)), ((), ())), preferred_element_type=f32)


def normal(values):
    center = values - jnp.mean(values, -1, keepdims=True)
    rstd = lax.rsqrt(jnp.mean(center * center, -1, keepdims=True) + EPSILON)
    return center * rstd, rstd


def norm_back(err, gain, hat, rstd):
    scaled = err * gain
    return rstd * (
        scaled
        - jnp.mean(scaled, -1, keepdims=True)
        - hat * jnp.mean(scaled * hat, -1, keepdims=True)
    )


def pack_body(pos, w_ref, tok_ref, cot_ref, wo_ref, wu_ref, wd_ref, ids_ref, *refs):
    small, up_ref = refs[:8], refs[8]
    piece_ref, mate_ref, pack_ref, rest_ref, rest_mate, w_rows, up_rows, sem = refs[9:]
    k, c = pos[1], pos[2]
    copies = [
        pltpu.make_async_copy(tok_ref.at[0], pack_ref.at[pl.ds(0, ROWS), :], sem.at[0]),
        pltpu.make_async_copy(cot_ref.at[0], pack_ref.at[pl.ds(ROWS, ROWS), :], sem.at[1]),
    ]
    for n, (half, dst) in enumerate(((c, rest_ref), (1 - c, rest_mate))):
        rows = pl.ds(pl.multiple_of(half * HALF, 32), HALF)
        down_rows = pl.ds(pl.multiple_of(k * QUARTER + half * HALF, 32), HALF)
        out_part, down_part = dst.at[pl.ds(0, HALF), :], dst.at[pl.ds(2 * HALF, HALF), :]
        copies += [
            pltpu.make_async_copy(w_ref.at[rows, :], w_rows.at[n], sem.at[2 + 4 * n]),
            pltpu.make_async_copy(wu_ref.at[rows, :], up_rows.at[n], sem.at[3 + 4 * n]),
            pltpu.make_async_copy(wo_ref.at[rows, :], out_part, sem.at[4 + 4 * n]),
            pltpu.make_async_copy(wd_ref.at[down_rows, :], down_part, sem.at[5 + 4 * n]),
        ]
    for copy in copies:
        copy.start()
    up = up_ref[...].astype(f32).reshape(1, WIDTH)
    part = jnp.zeros((1, QUARTER), f32)
    for q in range(4):
        part = jnp.where(k == q, up[:, QUARTER * q : QUARTER * (q + 1)], part)
    vecs = [ref[...].astype(f32).reshape(1, QUARTER) for ref in small] + [part]
    lines = [jnp.concatenate(vecs[3 * n : 3 * n + 3], 1) for n in range(3)]
    lines = jnp.concatenate(lines + [jnp.zeros((13, 3 * QUARTER), f32)], 0)
    piece_ref[HALF:, :] = lines.astype(bf16)
    ids = jnp.concatenate([ids_ref[...].astype(f32), jnp.zeros((1, WIDTH - ROWS), f32)], 1)
    pack_ref[2 * ROWS :, :] = jnp.concatenate([ids, jnp.zeros((7, WIDTH), f32)], 0).astype(bf16)
    for copy in copies:
        copy.wait()
    for q in range(4):

        @pl.when(k == q)
        def _():
            for p in range(4):
                at = WIDTH * p + QUARTER * q
                cols = slice(QUARTER * p, QUARTER * (p + 1))
                if p < 3:
                    piece_ref[:HALF, cols] = w_rows[0, :, at : at + QUARTER]
                    mate_ref[:HALF, cols] = w_rows[1, :, at : at + QUARTER]
                rest_ref[HALF : 2 * HALF, cols] = up_rows[0, :, at : at + QUARTER]
                rest_mate[HALF : 2 * HALF, cols] = up_rows[1, :, at : at + QUARTER]


def qkv_body(pos, *refs):
    tok, own, oth = refs[0:4], refs[4:8], refs[8:12]
    q_ref, k_ref, v_ref, normed_ref, vec_ref, w_ref, sm = refs[12:]
    s, k, c = pos[0], pos[1], pos[2]
    for m in range(4):
        z = s ^ m
        at = pl.ds(pl.multiple_of(z * QUARTER + c * HALF, 32), HALF)
        w_ref[at, :] = own[m][:HALF, :]
        at = pl.ds(pl.multiple_of(z * QUARTER + (1 - c) * HALF, 32), HALF)
        w_ref[at, :] = oth[m][:HALF, :]
        sm[z] = own[m][HALF:, :].astype(f32)

    def seg(z, n):
        return sm[z, n // 3 : n // 3 + 1, QUARTER * (n % 3) : QUARTER * (n % 3 + 1)]

    def vec(n):
        return jnp.concatenate([seg(z, n) for z in range(4)], 1)

    def chip_seg(n):
        return seg(k, n)

    gain, shift = vec(0), vec(1)
    bias = jnp.concatenate([chip_seg(2), jnp.zeros((1, QUARTER), f32), chip_seg(3)], 1)
    vec_ref[...] = jnp.concatenate(
        [gain, shift, vec(4), vec(5), vec(6), vec(7), vec(8), jnp.zeros((1, WIDTH), f32)], 0
    )
    for r in range(4):
        hat, _ = normal(tok[r][:ROWS, :].astype(f32))
        normed_ref[ROWS * r : ROWS * (r + 1), :] = (hat * gain + shift).astype(bf16)
    projected = dot(normed_ref[...], w_ref[...]) + bias
    q_ref[...] = (projected[:, :QUARTER].astype(bf16).astype(f32) * 0.125).astype(bf16)
    k_ref[:OWN, :] = projected[:, QUARTER : 2 * QUARTER].astype(bf16)
    v_ref[...] = projected[:, 2 * QUARTER :].astype(bf16)
    ids = [tok[r][2 * ROWS :, :ROWS].astype(f32)[:1] for r in range(4)]
    ids = jnp.concatenate(ids + [jnp.zeros((4, ROWS), f32)], 0).astype(bf16)
    k_ref[OWN:, :] = jnp.concatenate([ids, jnp.zeros((8, QUARTER - ROWS), bf16)], 1)


def split_ids(kva, kvb):
    ids_a = kva[OWN:, :ROWS].astype(f32)
    ids_b = kvb[OWN:, :ROWS].astype(f32)
    keys = jnp.concatenate(
        [ids_a[r : r + 1] for r in range(4)] + [ids_b[r : r + 1] for r in range(4)], 1
    )
    return ids_a.T, keys


def all_keys(pair, key_ref, value_ref):
    for n in range(2):
        for h in range(3):
            at = slice(64 * h, 64 * h + 64)
            key_ref[h, OWN * n : OWN * (n + 1), :] = pair[2 * n][:OWN, at]
            value_ref[h, OWN * n : OWN * (n + 1), :] = pair[2 * n + 1][:, at]


def attend_body(pos, q_ref, *refs):
    pair, (mixed_ref, state_ref, key_ref, value_ref) = refs[:4], refs[4:]
    cols, keys = split_ids(pair[0], pair[2])
    all_keys(pair, key_ref, value_ref)
    lane = lax.broadcasted_iota(jnp.int32, (2 * ROWS, 64), 1)
    for r in range(2):
        rows = slice(2 * ROWS * r, 2 * ROWS * (r + 1))
        ids = jnp.concatenate([cols[:, 2 * r : 2 * r + 1], cols[:, 2 * r + 1 : 2 * r + 2]], 0)
        hidden = keys > ids
        heads, lse = [], jnp.zeros((2 * ROWS, 64), f32)
        for h in range(3):
            at = slice(64 * h, 64 * h + 64)
            query = q_ref[rows, at]
            scores = dot_t(query, key_ref[h])
            scores = jnp.where(hidden, NEGATIVE, scores)
            top = jnp.max(scores, -1, keepdims=True)
            weights = jnp.exp(scores - top)
            total = jnp.sum(weights, -1, keepdims=True)
            low = weights.astype(bf16)
            out = dot(low, value_ref[h])
            heads.append(out * (1.0 / total))
            lse = jnp.where(lane == h, top + jnp.log(total), lse)
        mixed = jnp.concatenate(heads, 1)
        mixed_ref[rows, :] = mixed.astype(bf16)
        state_ref[rows, :] = jnp.concatenate([mixed, lse], 1)


def feed_body(pos, *refs):
    tok, mixed, own, oth = refs[0:4], refs[4:8], refs[8:12], refs[12:16]
    vec_ref = refs[16]
    mid_ref, d0, d1, d2, d3, g0, g1, g2, g3, sums_ref, wok_ref, send_ref, own_ref = refs[17:30]
    wo, wu, wd, hat_ref, n2_ref, act_ref, wg = refs[30:]
    s, k, c = pos[0], pos[1], pos[2]
    for m in range(4):
        z = s ^ m
        for half, src in ((c, own[m]), (1 - c, oth[m])):
            at = pl.ds(pl.multiple_of(z * QUARTER + half * HALF, 32), HALF)
            wo[at, :] = src[:HALF, :]
            wu[at, :] = src[HALF : 2 * HALF, :]
            wd[at, :] = src[2 * HALF :, :]
    wok_ref[...] = wo[pl.ds(pl.multiple_of(k * QUARTER, 64), QUARTER), :]
    bias_out, gain, shift = vec_ref[2:3, :], vec_ref[3:4, :], vec_ref[4:5, :]
    bias_up = vec_ref[6:7, :]
    attended = bias_out
    for m in range(4):
        block = jnp.concatenate(
            [mixed[m][ROWS * (r ^ m) : ROWS * (r ^ m) + ROWS, :] for r in range(4)], 0
        )
        at = pl.ds(pl.multiple_of((k ^ m) * QUARTER, 64), QUARTER)
        attended = attended + dot(block, wo[at, :])
    for r in range(4):
        rows = slice(ROWS * r, ROWS * (r + 1))
        middle = tok[r][:ROWS, :].astype(f32) + attended[rows]
        if r == 0:
            mid_ref[...] = middle
        hat, _ = normal(middle)
        hat_ref[rows, :] = hat
        n2_ref[rows, :] = (hat * gain + shift).astype(bf16)
    pre_act = dot(n2_ref[...], wu[...]) + bias_up
    cdf = 0.5 * (1.0 + lax.erf(pre_act * (1.0 / math.sqrt(2.0))))
    act_ref[...] = (pre_act * cdf).astype(bf16)
    slope = cdf + pre_act * jnp.exp(-0.5 * pre_act * pre_act) * (1.0 / math.sqrt(2.0 * math.pi))
    grads = jnp.concatenate([ref[ROWS : 2 * ROWS, :] for ref in tok], 0)
    pre = (dot_t(grads, wd[...]) * slope).astype(bf16)
    back = dot_t(pre, wu[...])
    sums = [
        jnp.sum(back * hat_ref[...], 0, keepdims=True),
        jnp.sum(back, 0, keepdims=True),
        jnp.sum(pre.astype(f32), 0, keepdims=True),
    ]
    sums_ref[...] = jnp.concatenate(sums + [jnp.zeros((5, WIDTH), f32)], 0)
    g0[...] = back[:ROWS]
    for r, ref in ((1, g1), (2, g2), (3, g3)):
        ref[...] = back[ROWS * r : ROWS * (r + 1)].astype(bf16)
    down = dot(act_ref[...], wd[...])
    d0[...] = down[:ROWS]
    for r, ref in ((1, d1), (2, d2), (3, d3)):
        ref[...] = down[ROWS * r : ROWS * (r + 1)].astype(bf16)
    for part in range(2):
        wg[...] = t_dot(act_ref[...], grads) if part == 0 else t_dot(n2_ref[...], pre)
        rows = slice(HALF * part, HALF * part + HALF)
        for m in range(4):
            z = s ^ m
            at = pl.ds(pl.multiple_of(z * QUARTER + c * HALF, 32), HALF)
            own_ref[m, rows, :] = wg[at, :]
            at = pl.ds(pl.multiple_of(z * QUARTER + (1 - c) * HALF, 32), HALF)
            send_ref[m, rows, :] = wg[at, :].astype(bf16)


def feed_halves_body(pos, own_ref, got_ref, o0, o1, o2, o3):
    for m, out in enumerate((o0, o1, o2, o3)):
        out[...] = (own_ref[m] + got_ref[m].astype(f32)).astype(out.dtype)


def add_body(pos, o0, r1, r2, r3, out):
    total = o0[...] + r1[...].astype(f32) + r2[...].astype(f32) + r3[...].astype(f32)
    out[...] = total.astype(out.dtype)


def middle_body(pos, g0, r1, r2, r3, mid_ref, tok_ref, vec_ref, gm_ref, ga_ref):
    err = g0[...] + r1[...].astype(f32) + r2[...].astype(f32) + r3[...].astype(f32)
    hat, rstd = normal(mid_ref[...])
    grad = tok_ref[ROWS : 2 * ROWS, :].astype(f32) + norm_back(err, vec_ref[3:4, :], hat, rstd)
    gm_ref[...] = grad
    ga_ref[...] = grad.astype(bf16)


def attend_grad_body(pos, a0, a1, a2, a3, wok, q_ref, *refs):
    pair, state_ref, outs = refs[:4], refs[4], refs[5:]
    dq_ref, own_ref, send_k, send_v, p_ref, ds_ref, key_ref, value_ref = outs
    cols, keys = split_ids(pair[0], pair[2])
    all_keys(pair, key_ref, value_ref)
    grads = jnp.concatenate([ref[...] for ref in (a0, a1, a2, a3)], 0)
    grad_mixed = dot_t(grads, wok[...]).astype(bf16)
    dq, dks, dvs = [], [], []
    for h in range(3):
        at = slice(64 * h, 64 * h + 64)
        query, grad = q_ref[:, at], grad_mixed[:, at]
        grad_q = []
        for r in range(2):
            rows = slice(2 * ROWS * r, 2 * ROWS * (r + 1))
            ids = jnp.concatenate([cols[:, 2 * r : 2 * r + 1], cols[:, 2 * r + 1 : 2 * r + 2]], 0)
            hidden = keys > ids
            g = grad[rows]
            inner = jnp.sum(g.astype(f32) * state_ref[rows, at], -1, keepdims=True)
            lse = state_ref[rows, QUARTER + h : QUARTER + h + 1]
            scores = dot_t(query[rows], key_ref[h])
            probs = jnp.exp(jnp.where(hidden, NEGATIVE, scores) - lse)
            slopes = dot_t(g, value_ref[h])
            ds = (probs * (slopes - inner)).astype(bf16)
            p_ref[rows, :] = probs.astype(bf16)
            ds_ref[rows, :] = ds
            grad_q.append(dot(ds, key_ref[h]))
        dq.append(jnp.concatenate(grad_q, 0))
        dks.append(t_dot(query, ds_ref[...]))
        dvs.append(t_dot(grad, p_ref[...]))
    dk = jnp.concatenate(dks, 0).T
    dv = jnp.concatenate(dvs, 0).T
    own_ref[:, :QUARTER] = dk[:OWN]
    own_ref[:, QUARTER:] = dv[:OWN]
    send_k[...] = dk[OWN:].astype(bf16)
    send_v[...] = dv[OWN:].astype(bf16)
    dq_ref[...] = (jnp.concatenate(dq, 1) * 0.125).astype(bf16)


def project_grad_body(pos, *refs):
    mixed, ga = refs[0:4], refs[4:8]
    normed, dq, kv_own, got_k, got_v = refs[8:13]
    send_ref, own_ref, gp, wg, gk = refs[13:]
    s, k, c = pos[0], pos[1], pos[2]
    gp[:, :QUARTER] = dq[...]
    got = jnp.concatenate([got_k[...], got_v[...]], 1).astype(f32)
    gp[:, QUARTER:] = (kv_own[...] + got).astype(bf16)
    wg[:, : 3 * QUARTER] = t_dot(normed[...], gp[...])
    for q in range(4):

        @pl.when(k == q)
        def _():
            for r in range(4):
                gk[ROWS * r : ROWS * (r + 1), :] = ga[r][:, QUARTER * q : QUARTER * (q + 1)]

    for m in range(4):
        block = jnp.concatenate(
            [mixed[m][ROWS * (r ^ m) : ROWS * (r ^ m) + ROWS, :] for r in range(4)], 0
        )
        at = pl.ds(pl.multiple_of((k ^ m) * QUARTER, 64), QUARTER)
        wg[at, 3 * QUARTER :] = t_dot(block, gk[...])
    for m in range(4):
        z = s ^ m
        at = pl.ds(pl.multiple_of(z * QUARTER + c * HALF, 32), HALF)
        own_ref[m] = wg[at, :]
        at = pl.ds(pl.multiple_of(z * QUARTER + (1 - c) * HALF, 32), HALF)
        send_ref[m] = wg[at, :].astype(bf16)


def normed_grad_body(pos, *refs):
    tok, (gp, w_ref, ga_ref, sums_ref) = refs[0:4], refs[4:8]
    small_ref, g0, g1, g2, g3 = refs[8:]
    k = pos[1]
    back = dot_t(gp[...], w_ref[...])
    hat = jnp.concatenate([normal(tok[r][:ROWS, :].astype(f32))[0] for r in range(4)], 0)
    ln1_gain = jnp.sum(back * hat, 0, keepdims=True)
    ln1_bias = jnp.sum(back, 0, keepdims=True)
    g0[...] = back[:ROWS]
    for r, ref in ((1, g1), (2, g2), (3, g3)):
        ref[...] = back[ROWS * r : ROWS * (r + 1)].astype(bf16)
    gp_sums = jnp.sum(gp[...].astype(f32), 0, keepdims=True)
    out_bias = jnp.sum(ga_ref[...].astype(f32), 0, keepdims=True)
    down_bias = jnp.sum(tok[0][ROWS : 2 * ROWS, :].astype(f32), 0, keepdims=True)
    for z in range(4):
        at = slice(QUARTER * z, QUARTER * (z + 1))
        here = jnp.where(k == z, 1.0, 0.0).astype(f32)
        row0 = [ln1_gain[:, at], ln1_bias[:, at], gp_sums[:, :QUARTER] * here]
        row0 = jnp.concatenate(row0 + [gp_sums[:, 2 * QUARTER :] * here], 1)
        row1 = [out_bias[:, at], sums_ref[0:1, at], sums_ref[1:2, at], down_bias[:, at]]
        row1 = jnp.concatenate(row1, 1)
        row2 = jnp.concatenate([sums_ref[2:3, at], jnp.zeros((1, 3 * QUARTER), f32)], 1)
        small_ref[z] = jnp.concatenate([row0, row1, row2, jnp.zeros((5, WIDTH), f32)], 0)


def last_halves_body(pos, own_ref, small_ref, got, o0, o1, o2, o3):
    s = pos[0]
    for m, out in enumerate((o0, o1, o2, o3)):
        out[:HALF, :] = (own_ref[m] + got[m].astype(f32)).astype(out.dtype)
        out[HALF:, :] = small_ref[s ^ m].astype(out.dtype)


def rows_body(pos, g0, r1, r2, r3, d0, s1, s2, s3, tok_ref, gm_ref, mid_ref, vec_ref, *outs):
    grad_ref, out_ref = outs
    err = g0[...] + r1[...].astype(f32) + r2[...].astype(f32) + r3[...].astype(f32)
    hat, rstd = normal(tok_ref[:ROWS, :].astype(f32))
    grad_ref[0] = gm_ref[...] + norm_back(err, vec_ref[0:1, :], hat, rstd)
    total = d0[...] + s1[...].astype(f32) + s2[...].astype(f32) + s3[...].astype(f32)
    out_ref[0] = (mid_ref[...] + total + vec_ref[5:6, :]).astype(bf16)


def feed_join_body(pos, *refs):
    own, oth = refs[0:4], refs[4:8]
    down_ref, up_ref, sc = refs[8:]
    k, c = pos[1], pos[2]
    for m in range(4):
        sc[c, k ^ m] = own[m][...]
        sc[1 - c, k ^ m] = oth[m][...]
    for q in range(4):
        for half in range(2):
            at = QUARTER * q + HALF * half
            down_ref[at : at + HALF, :] = sc[half, q, :HALF, :].astype(f32)
            rows = slice(HALF * half, HALF * half + HALF)
            for p in range(4):
                cols = slice(WIDTH * p + QUARTER * q, WIDTH * p + QUARTER * (q + 1))
                piece = sc[half, q, HALF:, QUARTER * p : QUARTER * (p + 1)]
                up_ref[rows, cols] = piece.astype(f32)


def last_join_body(pos, *refs):
    own, oth = refs[0:4], refs[4:8]
    qkv_ref, out_ref, up_ref, sc = refs[8], refs[9], refs[18], refs[19]
    vec_refs = refs[10:18]
    k, c = pos[1], pos[2]
    for m in range(4):
        sc[c, k ^ m] = own[m][...]
        sc[1 - c, k ^ m] = oth[m][...]
    total = jnp.zeros((8, WIDTH), f32)
    ups = []
    for q in range(4):
        small = sc[0, q, HALF:, :].astype(f32) + sc[1, q, HALF:, :].astype(f32)
        total = total + small
        ups.append(small[2:3, :QUARTER])
        for half in range(2):
            rows = slice(HALF * half, HALF * half + HALF)
            for p in range(3):
                cols = slice(WIDTH * p + QUARTER * q, WIDTH * p + QUARTER * (q + 1))
                piece = sc[half, q, :HALF, QUARTER * p : QUARTER * (p + 1)]
                qkv_ref[rows, cols] = piece.astype(f32)
            out_ref[rows, QUARTER * q : QUARTER * (q + 1)] = sc[
                half, q, :HALF, 3 * QUARTER :
            ].astype(f32)
    for n, ref in enumerate(vec_refs):
        row = total[n // 4 : n // 4 + 1, QUARTER * (n % 4) : QUARTER * (n % 4 + 1)]
        ref[...] = row.reshape(QUARTER)
    up_ref[...] = jnp.concatenate(ups, 1).reshape(WIDTH)


def shards(
    tokens,
    block_ids,
    ln1_gain,
    ln1_bias,
    w_qkv,
    q_bias,
    v_bias,
    w_out,
    out_bias,
    ln2_gain,
    ln2_bias,
    w_up,
    up_bias,
    w_down,
    down_bias,
    cotangent,
):
    seq = lax.axis_index("seq")
    ctx = lax.axis_index("ctx")
    k, core = ctx // 2, ctx % 2
    pos = jnp.stack([seq, k, core]).astype(jnp.int32)

    small = [ln1_gain, ln1_bias, q_bias, v_bias, out_bias, ln2_gain, ln2_bias, down_bias, up_bias]
    piece_qkv, mate_qkv, pack, rest, mate_rest = run(
        pack_body,
        pos,
        [w_qkv, tokens, cotangent, w_out, w_up, w_down, block_ids, *small],
        [((HALF + 16, 3 * QUARTER), bf16)] * 2
        + [((2 * ROWS + 8, WIDTH), bf16)]
        + [((3 * HALF, WIDTH), bf16)] * 2,
        [((2, HALF, 3 * WIDTH), bf16), ((2, HALF, 4 * WIDTH), bf16)],
        hbm=range(6),
        sems=10,
        limit=60,
    )
    got_qkv = seq_gather(piece_qkv)
    tok = chip_gather(pack)
    got_rest = seq_gather(rest)
    oth_qkv = [mate_qkv] + [core_swap(block) for block in got_qkv[1:]]
    third = (OWN, QUARTER)
    query, *pair, normed, vec, weight_qkv = run(
        qkv_body,
        pos,
        [*tok, *got_qkv, *oth_qkv],
        [(third, bf16), ((OWN + 8, QUARTER), bf16), (third, bf16)]
        + [((OWN, WIDTH), bf16), ((8, WIDTH), f32), ((WIDTH, 3 * QUARTER), bf16)],
        [((4, 16, 3 * QUARTER), f32)],
    )
    pair = [*pair, *[core_swap(x) for x in pair]]
    mixed_own, state = run(
        attend_body,
        pos,
        [query, *pair],
        [((OWN, QUARTER), bf16), ((OWN, 256), f32)],
        [((3, 2 * OWN, 64), bf16)] * 2,
    )
    mixed = chip_gather(mixed_own)
    got_rest = lax.optimization_barrier((*got_rest, *mixed[1:]))[:4]
    oth_rest = [mate_rest] + [core_swap(block) for block in got_rest[1:]]
    big, block, piece = (OWN, WIDTH), (ROWS, WIDTH), (QUARTER, WIDTH)
    mid, d0, d1, d2, d3, g0, g1, g2, g3, sums, w_out_k, feed_send, feed_own = run(
        feed_body,
        pos,
        [*tok, *mixed, *got_rest, *oth_rest, vec],
        [(block, f32)]
        + [(block, f32), (block, bf16), (block, bf16), (block, bf16)] * 2
        + [((8, WIDTH), f32), (piece, bf16), ((4, *piece), bf16), ((4, *piece), f32)],
        [((WIDTH, WIDTH), bf16)] * 3 + [(big, f32), (big, bf16), (big, bf16), ((WIDTH, WIDTH), f32)],
        limit=40,
    )
    got_g = [chip_swap(g, m) for m, g in ((1, g1), (2, g2), (3, g3))]
    feed_got = core_swap(feed_send)
    h0, h1, h2, h3 = run(
        feed_halves_body, pos, [feed_own, feed_got], [(piece, f32)] + [(piece, bf16)] * 3
    )
    grad_mid, grad_att = run(
        middle_body, pos, [after(g0, h0), *got_g, mid, tok[0], vec], [(block, f32), (block, bf16)]
    )
    ga = chip_gather(grad_att)
    feed_terms = [seq_swap(h, m) for m, h in ((1, h1), (2, h2), (3, h3))]
    dq, kv_own, *pair_send = run(
        attend_grad_body,
        pos,
        [*ga, w_out_k, query, *pair, state],
        [(third, bf16), ((OWN, 2 * QUARTER), f32)] + [(third, bf16)] * 2,
        [((OWN, 2 * OWN), bf16)] * 2 + [((3, 2 * OWN, 64), bf16)] * 2,
    )
    pair_send[0], *feed_terms[1:] = lax.optimization_barrier((pair_send[0], *feed_terms[1:]))
    pair_got = [core_swap(x) for x in pair_send]
    lpiece = (HALF + 8, WIDTH)
    last_send, last_own, grad_proj = run(
        project_grad_body,
        pos,
        [*mixed, *ga, normed, dq, kv_own, *pair_got],
        [((4, HALF, WIDTH), bf16), ((4, HALF, WIDTH), f32), ((OWN, 3 * QUARTER), bf16)],
        [((WIDTH, WIDTH), f32), ((OWN, QUARTER), bf16)],
    )
    last_send, feed_terms[0] = lax.optimization_barrier((last_send, feed_terms[0]))
    last_got = core_swap(last_send)
    got_d = [chip_swap(after(d, grad_proj), m) for m, d in ((1, d1), (2, d2), (3, d3))]
    last_small, e0, e1, e2, e3 = run(
        normed_grad_body,
        pos,
        [*tok, grad_proj, weight_qkv, ga[0], sums],
        [((4, 8, WIDTH), f32), (block, f32)] + [(block, bf16)] * 3,
    )
    l0, l1, l2, l3 = run(
        last_halves_body,
        pos,
        [last_own, last_small, last_got],
        [(lpiece, f32)] + [(lpiece, bf16)] * 3,
    )
    last_terms = [seq_swap(h, m) for m, h in ((1, l1), (2, l2), (3, l3))]
    (feed_sum,) = run(add_body, pos, [after(h0, l1), *feed_terms], [(piece, bf16)])
    feed_blocks = chip_gather(feed_sum)
    l0, *got_d = lax.optimization_barrier((l0, *got_d))
    (last_sum,) = run(add_body, pos, [l0, *last_terms], [(lpiece, bf16)], cost=2)
    last_blocks = chip_gather(last_sum)
    got_e = [chip_swap(after(e, last_sum), m) for m, e in ((1, e1), (2, e2), (3, e3))]
    feed_oth = [core_swap(after(b, last_sum)) for b in feed_blocks]
    grad_w_down, grad_w_up = run(
        feed_join_body,
        pos,
        [after(feed_blocks[0], last_sum), *feed_blocks[1:], *feed_oth],
        [((WIDTH, WIDTH), f32), ((QUARTER, 4 * WIDTH), f32)],
        [((2, 4, QUARTER, WIDTH), bf16)],
    )
    input_grad, result = run(
        rows_body,
        pos,
        [after(e0, grad_w_up), *got_e, d0, *got_d, tok[0], grad_mid, mid, vec],
        [((1, *block), f32), ((1, *block), bf16)],
    )
    last_oth = [core_swap(b) for b in last_blocks]
    grad_w_qkv, grad_w_out, *g, g_up = run(
        last_join_body,
        pos,
        [*last_blocks, *last_oth],
        [((QUARTER, 3 * WIDTH), f32), ((QUARTER, WIDTH), f32)]
        + [((QUARTER,), f32)] * 8
        + [((WIDTH,), f32)],
        [((2, 4, HALF + 8, WIDTH), bf16)],
    )
    return (
        result,
        input_grad,
        g[0],
        g[1],
        grad_w_qkv,
        g[2],
        g[3],
        grad_w_out,
        g[4],
        g[5],
        g[6],
        grad_w_up,
        g_up,
        grad_w_down,
        g[7],
    )


def solution(mesh):
    placed = (
        P("seq", "ctx", None),
        P("seq", "ctx"),
        P("seq"),
        P("seq"),
        P("seq", None),
        P("seq"),
        P("seq"),
        P("seq", None),
        P("seq"),
        P("seq"),
        P("seq"),
        P("seq", None),
        P("seq"),
        P("seq", None),
        P("seq"),
        P("seq", "ctx", None),
    )
    return jax.shard_map(
        shards if mesh.shape["ctx"] == 8 and mesh.shape["seq"] == 4 else shards_general,
        mesh=mesh,
        in_specs=placed,
        out_specs=(
            P("seq", "ctx", None),
            P("seq", "ctx", None),
            P("seq"),
            P("seq"),
            P("seq", None),
            P("seq"),
            P("seq"),
            P("seq", None),
            P("seq"),
            P("seq"),
            P("seq"),
            P("seq", None),
            P("seq"),
            P("seq", None),
            P("seq"),
        ),
        check_vma=False,
    )
```
